32 devices in a mesh: groups: 2 (over y), gz: 4 (over z), view: 2 (over x), gy: 2 (over core).
Axes of the slice: x: 2, y: 2, z: 4, core: 2. Of those that a mesh axis runs over, the one named last changes fastest.
Arguments:
- camera: float32 [2, 256, 3, 128, 128], P('view', ('groups', 'gz'), None, 'gy'), parts along dimension 1, may hold values from 0 to 4
- background: int32 [2, 2, 8], P('view', 'gy', ('groups', 'gz')), parts along dimension 2, may hold values from 0 to 2
- destination: int32 [2, 2, 256, 1], P('view', 'gy', ('groups', 'gz')), parts along dimension 2, may hold values from 0 to 3; in each aligned block of 32 rows (0 to 31, 32 to 63, ..., all dimensions but the last counted through in order) at most 16 rows name the same one
- offsets: int32 [2, 2, 256], P('view', 'gy', ('groups', 'gz')), parts along dimension 2, may hold values from 0 to 6
- shift_frac: float32 [2, 3], P('view'), may hold values from 0.15 to 0.85
- psf_taps: float32 [2, 3, 9], P('view'), may hold values from 0.05 to 1
Outputs:
- estimate: float32 [64, 128, 128], P(('groups', 'gz'), 'gy'), parts along dimension 0
- joined_views: float32 [2, 64, 128, 128], P('view', ('groups', 'gz'), 'gy'), parts along dimension 1
The draws below stay inside these ranges and needn't reach their ends.
There are 2 independent parts, one for each index of `groups`. The reference program is written for one: setup_inputs(seed, part) draws one part's arguments, and reference() takes and returns one part's arrays. A program takes and returns all parts, laid end to end along the dimension named above; an argument that names none is the same for every part. Nothing has to cross between parts.
Inputs may be any that keep to these rules, and one draw needn't show every extreme that they name: `destination`: within the 32 block rows of one tile, no slab is named more than 16 times; some tile names one slab exactly 16 times.
All inputs are finite; a program needn't handle non-finite values.
Results may differ from the reference program's by a relative error of at most 0.0001.
Values sent between devices are 32-bit elements; how exact they have to be, the bound alone decides.
A program may use at most 64 MiB of HBM per device.

```python
import math
import jax
import jax.numpy as jnp
import numpy as np
from jax import lax

CZ = 8
CY = 64
CX = 128
NB = 32
BZ = 3
TAPS = 9
ITERS = 2
VIEWS = 2
MOST = 16
NZ = 32
NY = 128
NBLK = 128
N_GZ = 4
N_GY = 2


def touch_ends(values, own_key, low, largest):
    index_at = [jax.random.randint(jax.random.fold_in(own_key, axis), (), 0, length) for axis, length in enumerate(values.shape)]
    widest = values.shape.index(max(values.shape))
    beside = index_at[:widest] + [(index_at[widest] + 1) % values.shape[widest]] + index_at[widest + 1:]
    return values.at[tuple(index_at)].set(low).at[tuple(beside)].set(largest)


def block_scale(stream_key, extent, cuts, least, largest):
    factor_of = 1.0
    for axis_at, shards_of in cuts:
        steps = jax.random.uniform(jax.random.fold_in(jax.random.fold_in(stream_key, 6), axis_at), (shards_of,), jnp.float32, least / len(cuts), largest / len(cuts))
        factor_of = factor_of * jnp.repeat(jnp.exp(steps), extent[axis_at] // shards_of).reshape((-1,) + (1,) * (len(extent) - 1 - axis_at))
    return factor_of


def shared_out(rng, own, number, rows, count, top, bound, slope):
    ranking = jax.random.permutation(rng, count)
    crowded, usual = load_shares(count, rows * top, bound, slope, True), load_shares(count, rows * top, bound, slope, False)
    places = jnp.arange(count)

    def named(tallies, turn):
        used = int((tallies > 0).sum())
        fixed = max(1, used // 4)
        shifted = fixed + (places - fixed + turn * (used - fixed)) % max(1, count - fixed)
        return jnp.zeros((count,), jnp.int32).at[ranking[jnp.where(places < fixed, places, shifted)]].set(jnp.asarray(tallies, jnp.int32))

    tallies = jnp.where(number % 4 == 0, named(crowded, number // 4), named(usual, number - number // 4 - 1))
    mixed = jax.random.permutation(jax.random.fold_in(own, 3), count)
    giver, receiver = mixed[0:count // 2 * 2:2], mixed[1:count // 2 * 2:2]
    room = jnp.minimum(tallies[giver] - 1, bound - tallies[receiver]) // 2
    room = jnp.where((giver == ranking[0]) | (receiver == ranking[0]) | (tallies[receiver] == 0), 0, jnp.maximum(room, 0))
    shifted = jax.random.randint(jax.random.fold_in(own, 4), (count // 2,), 0, 1 << 20) % (room + 1)
    tallies = tallies.at[giver].add(-shifted).at[receiver].add(shifted)
    members = jnp.searchsorted(jnp.cumsum(tallies), jnp.arange(rows * top), side="right").astype(jnp.int32)
    listing = members.reshape(top, rows).T
    listing = listing[jax.random.permutation(jax.random.fold_in(own, 1), rows)]
    turn = jax.random.randint(jax.random.fold_in(own, 2), (rows, 1), 0, top)
    return jnp.take_along_axis(listing, (jnp.arange(top)[None, :] + turn) % top, axis=1)


def load_shares(amount, total, reach, lean, full):
    loads = [(1 << 20) // math.isqrt(rank ** lean) + 1 for rank in range(1, amount + 1)]
    largest = reach if full else min(reach, max(-(-total // amount), total * loads[0] // sum(loads)))
    least = 1 if total - largest >= amount - 1 else 0
    holding, spare = [largest] + [least] * (amount - 1), total - largest - least * (amount - 1)
    while spare > 0:
        free = [i for i in range(1, amount) if holding[i] < largest] or [i for i in range(1, amount) if holding[i] < reach]
        whole, budget = sum([loads[i] for i in free]), spare
        for i in free:
            extra = min(reach - holding[i], max(1, budget * loads[i] // whole), spare)
            holding[i] = holding[i] + extra
            spare = spare - extra
    return np.array(holding)


def setup_inputs(seed: int = 0, part: int = 0) -> dict:
    seeds = jax.random.split(jax.random.key(seed), 7)
    own_keys = jax.random.split(jax.random.fold_in(seeds[6], part), 7)
    camera = jnp.clip(4.0 * jax.random.uniform(own_keys[0], (VIEWS, NBLK, BZ, NY, CX), jnp.float32) ** block_scale(own_keys[0], (VIEWS, NBLK, BZ, NY, CX), ((0, 2), (1, 4), (3, 2)), -0.2, 0.2), 0.0, 4.0)
    background = touch_ends(jax.random.randint(own_keys[1], (VIEWS, N_GY, N_GZ), 0, 3), jax.random.fold_in(own_keys[1], 1), 0, 2).astype(jnp.int32)
    destination_keys = jax.random.split(jax.random.fold_in(own_keys[2], 1), VIEWS * N_GY * NBLK // NB)
    destination_turns = jax.random.permutation(jax.random.fold_in(own_keys[2], 3), VIEWS * N_GY * NBLK // NB)
    destination = jax.vmap(lambda own, number: shared_out(jax.random.fold_in(own_keys[2], 2), own, number, NB, N_GZ, 1, MOST, 2))(destination_keys, destination_turns).reshape((VIEWS, N_GY, NBLK, 1))
    offsets = touch_ends(jax.random.randint(own_keys[3], (VIEWS, N_GY, NBLK), 0, CZ - 1), jax.random.fold_in(own_keys[3], 1), 0, (CZ - 1) - 1).astype(jnp.int32)
    shift_frac = jnp.clip(0.15 + 0.70000002 * jax.random.uniform(seeds[4], (VIEWS, 3), jnp.float32) ** block_scale(seeds[4], (VIEWS, 3), ((0, 2),), -0.2, 0.2), 0.15, 0.85)
    psf_taps = jnp.clip(jnp.exp(math.log(1.0) - 2.9957323 * jax.random.uniform(seeds[5], (VIEWS, 3, TAPS), jnp.float32) ** block_scale(seeds[5], (VIEWS, 3, TAPS), ((0, 2),), -0.2, 0.2)), 0.05, 1.0)
    return {"camera": camera, "background": background, "destination": destination, "offsets": offsets, "shift_frac": shift_frac, "psf_taps": psf_taps}


DATA_FLOOR = 0.25
PRECISE = lax.Precision.HIGHEST


def interp_matrix(length, fraction):
    places = jnp.arange(length, dtype=jnp.int32)
    follow = jnp.minimum(places + 1, length - 1)
    same_row = (places[:, None] == places[None, :]).astype(jnp.float32)
    next_row = (follow[:, None] == places[None, :]).astype(jnp.float32)
    return (1.0 - fraction) * same_row + fraction * next_row


def interp_blocks(blocks, fraction_z, y_matrix, x_matrix):
    lower = blocks[..., :-1, :, :]
    upper = blocks[..., 1:, :, :]
    planes = (1.0 - fraction_z) * lower + fraction_z * upper
    planes = jnp.einsum("ry,...yx->...rx", y_matrix, planes, precision=PRECISE)
    return jnp.einsum("...rx,cx->...rc", planes, x_matrix, precision=PRECISE)


def along_last(volume, weights):
    margin = weights.shape[0] // 2
    span_cells = volume.shape[-1]
    padded = jnp.pad(volume, [(0, 0)] * (volume.ndim - 1) + [(margin, margin)])
    result = weights[0] * padded[..., 0:span_cells]
    for offset in range(1, weights.shape[0]):
        result = result + weights[offset] * padded[..., offset:offset + span_cells]
    return result


def valid_pass(padded, weights, out_len, along_axis):
    result = weights[0] * lax.slice_in_dim(padded, 0, out_len, axis=along_axis)
    for offset in range(1, weights.shape[0]):
        result = result + weights[offset] * lax.slice_in_dim(padded, offset, offset + out_len, axis=along_axis)
    return result


def apply_passes(padded, kernel, planes_out, rows_out):
    x_done = along_last(padded, kernel[2])
    y_done = valid_pass(x_done, kernel[1], rows_out, 1)
    return valid_pass(y_done, kernel[0], planes_out, 0)


def blur_whole(volume, kernel):
    margin = kernel.shape[1] // 2
    padded = jnp.pad(volume, ((margin, margin), (margin, margin), (0, 0)))
    return apply_passes(padded, kernel, volume.shape[0], volume.shape[1])


def reference(camera, background, destination, offsets, shift_frac, psf_taps):
    joined_list = []
    for view_idx in range(VIEWS):
        fraction = shift_frac[view_idx]
        y_matrix = interp_matrix(CY, fraction[1])
        x_matrix = interp_matrix(CX, fraction[2])
        columns = []
        for row_idx in range(N_GY):
            tiles = camera[view_idx, :, :, row_idx * CY:(row_idx + 1) * CY, :]
            levels = jnp.repeat(background[view_idx, row_idx], NB).astype(jnp.float32)
            blocks = tiles - levels[:, None, None, None]
            planes = interp_blocks(blocks, fraction[0], y_matrix, x_matrix)
            start_plane = destination[view_idx, row_idx, :, 0] * CZ + offsets[view_idx, row_idx]
            target = (start_plane[:, None] + jnp.arange(BZ - 1, dtype=jnp.int32)[None, :]).reshape(-1).astype(jnp.int32)
            total = jax.ops.segment_sum(planes.reshape(-1, CY, CX), target, num_segments=NZ)
            covered = jax.ops.segment_sum(jnp.ones(target.shape, jnp.float32), target, num_segments=NZ)
            columns.append(jnp.maximum(total / (covered[:, None, None] + 1.0), DATA_FLOOR))
        joined_list.append(jnp.concatenate(columns, axis=1))
    joined_views = jnp.stack(joined_list)
    kernels = psf_taps / jnp.sum(psf_taps, axis=-1, keepdims=True)
    estimate = jnp.sum(joined_views, axis=0) / VIEWS
    for iteration in range(ITERS):
        log_total = jnp.zeros(estimate.shape, jnp.float32)
        for view_idx in range(VIEWS):
            blurred = blur_whole(estimate, kernels[view_idx])
            ratio = joined_views[view_idx] / blurred
            correction = blur_whole(ratio, kernels[view_idx][:, ::-1])
            log_total = log_total + jnp.log(correction)
        estimate = estimate * jnp.exp(log_total / VIEWS)
    return estimate, joined_views
```

```python
import functools

import jax
import jax.numpy as jnp
from jax import lax
from jax.experimental import pallas as pl
from jax.experimental.pallas import tpu as pltpu
from jax.sharding import PartitionSpec as P

CZ = 8
ITERS = 2
HALO = 8
CHUNK = 4
CP = 2
NCH = CZ // CP
OC = 4
NOUT = CZ // OC

DATA_FLOOR = 0.25
MESH = pl.DeviceIdType.MESH


def deposit_kernel(
    rows, dest_in, offs_in, level_in, frac_in, psf_in, cam_ref, acc_ref, tap_ref,
    dest, offs, level, frac, psf, cam, sems, small,
):
    taps = psf.shape[2]
    blocks, planes = cam_ref.shape[:2]
    pairs = ((dest_in, dest), (offs_in, offs), (level_in, level), (frac_in, frac), (psf_in, psf))
    copies = [pltpu.make_async_copy(a, b, small.at[n]) for n, (a, b) in enumerate(pairs)]
    for copy in copies:
        copy.start()

    def fetch(c):
        at = pl.ds(c * CHUNK, CHUNK)
        return pltpu.make_async_copy(cam_ref.at[at], cam.at[at], sems.at[c])

    for c in range(blocks // CHUNK):
        fetch(c).start()

    @pl.loop(0, acc_ref.shape[0])
    def _(s):
        acc_ref[s] = jnp.zeros(acc_ref.shape[1:], jnp.float32)

    for copy in copies:
        copy.wait()

    tap_ref[...] = jnp.zeros(tap_ref.shape, jnp.float32)
    for axis in range(3):
        scale = jnp.sum(psf[axis], axis=1, keepdims=True)
        share = psf[axis] / scale
        for t in range(taps):
            at = axis * taps + t
            tap_ref[at : at + 1, :] = jnp.broadcast_to(share[:, t : t + 1], (1, 128))
        at = 3 * taps + axis
        tap_ref[at : at + 1, :] = jnp.zeros((1, 128), jnp.float32) + frac[axis]

    fz = frac[0]
    base = level[0, 0, 0].astype(jnp.float32)

    @pl.loop(0, blocks // CHUNK)
    def _(c):
        fetch(c).wait()
        for i in range(CHUNK):
            b = c * CHUNK + i
            s = dest[b]
            o = offs[b]
            lower = cam[b, 0] - base
            for k in range(planes - 1):
                upper = cam[b, k + 1] - base
                at = pl.ds(pl.multiple_of(CZ + (o + k) * rows, 8), rows)
                acc_ref[s, at, :] = acc_ref[s, at, :] + ((1.0 - fz) * lower + fz * upper)
                cnt = pl.ds(o + k, 1)
                acc_ref[s, cnt, :] = acc_ref[s, cnt, :] + 1.0
                lower = upper


def world_kernel(
    dims, rows, taps,
    acc_ref, tap_in, est_ref, joined_ref,
    ru, rd, tap_all, jx, e0, e1, kx, za, zb, rt, yb, lg,
    us, ur, ds_, dr, tap_s, tap_r, loc_sem, ms, mr, los, lor, his, hir,
    zs, zr, es, er, out_s, out_r,
):
    slabs, views, bands = dims
    strip = rows // views
    wide = strip + 2 * HALO
    margin = taps // 2
    z = lax.axis_index("gz")
    v = lax.axis_index("view")
    g = lax.axis_index("gy")
    strips = views * bands
    me = v * bands + g
    band, idx = me // views, me % views

    def dev(zz, vv, gg):
        return {"gz": zz, "view": vv, "gy": gg}

    def strip_dev(zz, ss):
        return dev(zz, ss // bands, ss % bands)

    below, above = z > 0, z < slabs - 1
    left, right = me > 0, me < strips - 1

    barrier = pltpu.get_barrier_semaphore()

    def greet(target):
        pl.semaphore_signal(barrier, inc=1, device_id=target, device_id_type=MESH)

    amount = strips - 1
    for dz, zok in ((-1, below), (1, above)):
        for ds, sok in ((-1, left), (0, z >= 0), (1, right)):
            ok = zok & sok
            amount = amount + ok.astype(jnp.int32)

            @pl.when(ok)
            def _(dz=dz, ds=ds):
                greet(strip_dev(z + dz, me + ds))

    for d in range(1, strips):
        greet(strip_dev(z, (me + d) % strips))

    def clear(ref, planes, lo, hi):
        @pl.loop(planes[0], planes[1])
        def _(p):
            ref[p, lo:hi, :] = jnp.zeros((hi - lo, 128), jnp.float32)

    for edge, flow, halo in ((z == 0, ru, (0, CZ)), (z == slabs - 1, rd, (2 * CZ, 3 * CZ))):
        @pl.when(edge)
        def _(flow=flow, halo=halo):
            flow[z] = jnp.zeros(flow.shape[1:], jnp.float32)
            for ref in [e0, e1] + [jx.at[w] for w in range(views)]:
                clear(ref, halo, 0, wide)

    for edge, lo, hi in ((me == 0, 0, HALO), (me == strips - 1, HALO + strip, wide)):
        @pl.when(edge)
        def _(lo=lo, hi=hi):
            clear(e1, (0, 3 * CZ), lo, hi)
            for w in range(views):
                clear(jx.at[w], (CZ, 2 * CZ), lo, hi)

    pl.semaphore_wait(barrier, amount)

    def span(c):
        start = 0 if c == 0 else CZ + c * CP * rows
        return pl.ds(start, CZ + (c + 1) * CP * rows - start)

    def up_copy(src, t, c):
        return pltpu.make_async_remote_copy(
            src_ref=src.at[t, span(c)], dst_ref=ru.at[t, span(c)], send_sem=us.at[t, c],
            recv_sem=ur.at[t, c], device_id={"gz": z + 1}, device_id_type=MESH)

    def down_copy(src, t, c):
        return pltpu.make_async_remote_copy(
            src_ref=src.at[t, span(c)], dst_ref=rd.at[t, span(c)], send_sem=ds_.at[t, c],
            recv_sem=dr.at[t, c], device_id={"gz": z - 1}, device_id_type=MESH)

    @pl.when(z == 0)
    def _():
        @pl.loop(0, slabs - 1)
        def _(k):
            for c in range(NCH):
                up_copy(acc_ref, slabs - 1 - k, c).start()

    @pl.when(z == slabs - 1)
    def _():
        @pl.loop(0, slabs - 1)
        def _(k):
            for c in range(NCH):
                down_copy(acc_ref, k, c).start()

    own_tap = pltpu.make_async_copy(tap_in, tap_all.at[v], loc_sem)
    own_tap.start()

    def tap_copy(d):
        return pltpu.make_async_remote_copy(
            src_ref=tap_in, dst_ref=tap_all.at[v], send_sem=tap_s.at[d - 1],
            recv_sem=tap_r.at[d - 1], device_id={"view": (v + d) % views}, device_id_type=MESH)

    for d in range(1, views):
        tap_copy(d).start()

    @pl.loop(0, slabs - 1)
    def _(k):
        t_up, t_down = slabs - 1 - k, k
        for c in range(NCH):
            at = span(c)

            @pl.when(below & (t_up > z))
            def _():
                up_copy(ru, t_up, c).wait_recv()
                ru[t_up, at] = ru[t_up, at] + acc_ref[t_up, at]
                up_copy(ru, t_up, c).start()

            @pl.when(above & (t_down < z))
            def _():
                down_copy(rd, t_down, c).wait_recv()
                rd[t_down, at] = rd[t_down, at] + acc_ref[t_down, at]
                down_copy(rd, t_down, c).start()

    own_tap.wait()
    for d in range(1, views):
        tap_copy(d).wait()

    apart = lax.broadcasted_iota(jnp.int32, (128, 128), 0) - lax.broadcasted_iota(jnp.int32, (128, 128), 1)

    @pl.loop(0, views)
    def _(w):
        ahead = jnp.zeros((128, 128), jnp.float32)
        back = jnp.zeros((128, 128), jnp.float32)
        for t in range(taps):
            tap = tap_all[w, 2 * taps + t : 2 * taps + t + 1, :]
            ahead = jnp.where(apart == t - margin, tap, ahead)
            back = jnp.where(apart == margin - t, tap, back)
        for n, full in enumerate((ahead, back)):
            top = full.astype(jnp.bfloat16)
            kx[w, n, 0:128, 0:128] = top
            kx[w, n, 128:256, 0:128] = top
            kx[w, n, 0:128, 128:256] = (full - top.astype(jnp.float32)).astype(jnp.bfloat16)
            kx[w, n, 128:256, 128:256] = jnp.zeros((128, 128), jnp.bfloat16)

    fy, fx = [tap_in[3 * taps + n : 3 * taps + n + 1, :] for n in (1, 2)]
    last_row = lax.broadcasted_iota(jnp.int32, (rows, 128), 0) == rows - 1
    last_col = lax.broadcasted_iota(jnp.int32, (rows, 128), 1) == 127
    joined = joined_ref.at[0]
    mid = pl.ds(CZ, CZ)

    def planes_of(c):
        return pl.ds(c * CP, CP), pl.ds(CZ + c * CP, CP)

    def piece(i):
        lo, hi = max(i * strip - HALO, 0), min((i + 1) * strip + HALO, rows)
        return (lo, hi), (lo - i * strip + HALO, hi - i * strip + HALO)

    low_edge = ((rows - HALO, rows), (0, HALO))
    high_edge = ((0, HALO), (HALO + strip, wide))

    def part_copy(c, w, rows_of, target, send, recv):
        src_p, dst_p = planes_of(c)
        (lo, hi), (dlo, dhi) = rows_of
        return pltpu.make_async_remote_copy(
            src_ref=joined.at[src_p, pl.ds(lo, hi - lo), :], dst_ref=jx.at[w, dst_p, pl.ds(dlo, dhi - dlo), :],
            send_sem=send, recv_sem=recv, device_id=strip_dev(z, target), device_id_type=MESH)

    def sends(c):
        out = []
        for i in range(views):
            out.append((g * views + i, z >= 0, piece(i), ms.at[i, c], mr.at[v, c]))
        out.append(((g + 1) * views, g < bands - 1, low_edge, los.at[c], lor.at[v, c]))
        out.append((g * views - 1, g > 0, high_edge, his.at[c], hir.at[v, c]))
        return out

    def join(c):
        src_p, _ = planes_of(c)

        @pl.when(below)
        def _():
            up_copy(acc_ref, z, c).wait_recv()

        @pl.when(above)
        def _():
            down_copy(acc_ref, z, c).wait_recv()

        for p in range(c * CP, (c + 1) * CP):
            at = pl.ds(CZ + p * rows, rows)
            total = acc_ref[z, at, :] + ru[z, at, :] + rd[z, at, :]
            cnt = pl.ds(p, 1)
            covered = acc_ref[z, cnt, :] + ru[z, cnt, :] + rd[z, cnt, :]
            follow = jnp.where(last_row, total, pltpu.roll(total, rows - 1, 0))
            total = (1.0 - fy) * total + fy * follow
            follow = jnp.where(last_col, total, pltpu.roll(total, 127, 1))
            total = (1.0 - fx) * total + fx * follow
            joined_ref[0, p] = jnp.maximum(total / (covered + 1.0), DATA_FLOOR)
        for target, ok, rows_of, send, recv in sends(c):
            (lo, hi), (dlo, dhi) = rows_of

            @pl.when(ok & (target != me))
            def _(rows_of=rows_of, target=target, send=send, recv=recv):
                part_copy(c, v, rows_of, target, send, recv).start()

            @pl.when(ok & (target == me))
            def _(lo=lo, hi=hi, dlo=dlo, dhi=dhi):
                for p in range(c * CP, (c + 1) * CP):
                    jx[v, CZ + p, dlo:dhi, :] = joined_ref[0, p, lo:hi, :]

    def z_copy(ref, w, c, up, send, recv):
        dst = (0 if up else 2 * CZ) + c * CP
        src = CZ + c * CP
        a, b = ref.at[pl.ds(src, CP)], ref.at[pl.ds(dst, CP)]
        return pltpu.make_async_remote_copy(
            src_ref=a, dst_ref=b, send_sem=send, recv_sem=recv,
            device_id={"gz": z + 1 if up else z - 1}, device_id_type=MESH)

    def z_copies(c, up):
        side = 1 if up else 0
        near = c * CP >= CZ - margin if up else c * CP < margin
        if near:
            return [z_copy(jx.at[w], w, c, up, zs.at[side, w, c], zr.at[side, w, c]) for w in range(views)]
        return [z_copy(e0, 0, c, up, zs.at[side, 0, c], zr.at[side, 0, c])]

    def average(p):
        total = jx[0, p]
        for w in range(1, views):
            total = total + jx[w, p]
        e0[p] = total / views

    def spread(c):
        for w in range(views):
            for i in range(views):
                @pl.when((idx == i) & ((w != v) | (band != g)))
                def _(i=i, w=w):
                    part_copy(c, w, piece(i), me, ms.at[i, c], mr.at[w, c]).wait_recv()

            @pl.when((idx == 0) & (band > 0) & ((w != v) | (band - 1 != g)))
            def _(w=w):
                part_copy(c, w, low_edge, me, los.at[c], lor.at[w, c]).wait_recv()

            @pl.when((idx == views - 1) & (band < bands - 1) & ((w != v) | (band + 1 != g)))
            def _(w=w):
                part_copy(c, w, high_edge, me, his.at[c], hir.at[w, c]).wait_recv()

        for p in range(c * CP, (c + 1) * CP):
            average(CZ + p)
        for up, ok in ((True, above), (False, below)):
            @pl.when(ok)
            def _(up=up):
                for copy in z_copies(c, up):
                    copy.start()

    join(0)
    for c in range(1, NCH):
        join(c)
        spread(c - 1)
    spread(NCH - 1)

    for c in range(NCH):
        for up, ok in ((True, below), (False, above)):
            @pl.when(ok)
            def _(up=up, c=c):
                copies = z_copies(c, up)
                for copy in copies:
                    copy.wait_recv()
                if len(copies) == views and views > 1:
                    for p in range(c * CP, (c + 1) * CP):
                        average((0 if up else 2 * CZ) + p)

    planes_r = CZ + 2 * margin
    rows_r = strip + 2 * margin

    def along_x(u, w, n):
        top = u.astype(jnp.bfloat16)
        rest = (u - top.astype(jnp.float32)).astype(jnp.bfloat16)
        both = jnp.dot(jnp.concatenate([top, rest], axis=1), kx[w, n], preferred_element_type=jnp.float32)
        return both[:, 0:128] + both[:, 128:256]

    def weighted(terms, weights):
        total = weights[0] * terms[0]
        for term, weight in zip(terms[1:], weights[1:]):
            total = total + weight * term
        return total

    def correct(est, emit):
        for w in range(views):
            def tap(axis, t):
                at = axis * taps + t
                return tap_all[w, at : at + 1, :]

            @pl.loop(0, wide // 8, unroll=2)
            def _(r):
                at = pl.ds(pl.multiple_of(r * 8, 8), 8)
                column = [est[CZ - 2 * margin + p, at, :] for p in range(planes_r + 2 * margin)]
                for p in range(planes_r):
                    za[p, at, :] = weighted(column[p : p + taps], [tap(0, t) for t in range(taps)])

            @pl.loop(0, planes_r, unroll=4)
            def _(p):
                base = HALO - 2 * margin
                zb[p] = weighted([za[p, base + t : base + t + rows_r, :] for t in range(taps)],
                                 [tap(1, t) for t in range(taps)])

            @pl.loop(0, planes_r // 4)
            def _(c):
                at = pl.ds(c * 4, 4)
                blurred = along_x(zb[at].reshape(4 * rows_r, 128), w, 0).reshape(4, rows_r, 128)
                data = jx[w, pl.ds(c * 4 + CZ - margin, 4), HALO - margin : HALO - margin + rows_r, :]
                rt[at] = jnp.where(data > 0.0, data / blurred, 0.0)

            @pl.loop(0, rows_r // 8, unroll=True)
            def _(r):
                at = pl.ds(pl.multiple_of(r * 8, 8), 8)
                column = [rt[p, at, :] for p in range(planes_r)]
                for p in range(CZ):
                    za[p, at, :] = weighted(column[p : p + taps], [tap(0, taps - 1 - t) for t in range(taps)])

            @pl.loop(0, CZ, unroll=4)
            def _(p):
                yb[p] = weighted([za[p, t : t + strip, :] for t in range(taps)],
                                 [tap(1, taps - 1 - t) for t in range(taps)])

            for c in range(NOUT):
                at = pl.ds(c * OC, OC)
                logs = jnp.log(along_x(yb[at].reshape(OC * strip, 128), w, 1)).reshape(OC, strip, 128)
                if w > 0:
                    logs = lg[at] + logs
                if w < views - 1:
                    lg[at] = logs
                else:
                    emit(c, est[pl.ds(CZ + c * OC, OC), HALO : HALO + strip, :] * jnp.exp(logs / views))

    inner = pl.ds(HALO, strip)
    near = []
    for n, (dz, ds) in enumerate([(a, b) for a in (-1, 1, 0) for b in (0, -1, 1) if a or b]):
        zok = {-1: below, 0: z >= 0, 1: above}[dz]
        sok = {-1: left, 0: z >= 0, 1: right}[ds]
        far_z = {-1: above, 0: z >= 0, 1: below}[dz]
        far_s = {-1: right, 0: z >= 0, 1: left}[ds]
        near.append((n, dz, ds, zok & sok, far_z & far_s))

    def near_copy(n, dz, ds, c):
        src_r = {-1: pl.ds(HALO, HALO), 0: inner, 1: pl.ds(strip, HALO)}[ds]
        dst_r = {-1: pl.ds(HALO + strip, HALO), 0: inner, 1: pl.ds(0, HALO)}[ds]
        dst = {-1: 2 * CZ, 0: CZ, 1: 0}[dz] + c * OC
        return pltpu.make_async_remote_copy(
            src_ref=e1.at[pl.ds(CZ + c * OC, OC), src_r, :], dst_ref=e1.at[pl.ds(dst, OC), dst_r, :],
            send_sem=es.at[n, c], recv_sem=er.at[n, c], device_id=strip_dev(z + dz, me + ds), device_id_type=MESH)

    def emit_step(c, new):
        e1[pl.ds(CZ + c * OC, OC), HALO : HALO + strip, :] = new
        for n, dz, ds, ok, _ in near:
            @pl.when(ok)
            def _(n=n, dz=dz, ds=ds):
                near_copy(n, dz, ds, c).start()

    correct(e0, emit_step)
    for c in range(NOUT):
        for n, dz, ds, _, ok in near:
            @pl.when(ok)
            def _(n=n, dz=dz, ds=ds, c=c):
                near_copy(n, dz, ds, c).wait_recv()

    def out_copy(c, w, target_g, i):
        at = pl.ds(pl.multiple_of(i * strip, 8), strip)
        part = pl.ds(c * OC, OC)
        return pltpu.make_async_remote_copy(
            src_ref=lg.at[part], dst_ref=est_ref.at[part, at, :], send_sem=out_s.at[w, c],
            recv_sem=out_r.at[i, c], device_id=dev(z, w, target_g), device_id_type=MESH)

    def emit_last(c, new):
        lg[pl.ds(c * OC, OC)] = new
        for w in range(views):
            away = (w != v) | (band != g)

            @pl.when(away)
            def _(w=w):
                out_copy(c, w, band, idx).start()

            @pl.when(jnp.logical_not(away))
            def _():
                est_ref[pl.ds(c * OC, OC), pl.ds(pl.multiple_of(idx * strip, 8), strip), :] = new

    correct(e1, emit_last)
    for c in range(NOUT):
        for i in range(views):
            @pl.when(g * views + i != me)
            def _(i=i, c=c):
                out_copy(c, 0, g, i).wait_recv()

    for c in range(NOUT):
        for w in range(views):
            @pl.when((w != v) | (band != g))
            def _(w=w, c=c):
                out_copy(c, w, band, idx).wait_send()

    @pl.loop(0, slabs)
    def _(t):
        for c in range(NCH):
            @pl.when(t > z)
            def _():
                up_copy(acc_ref, t, c).wait_send()

            @pl.when(t < z)
            def _():
                down_copy(acc_ref, t, c).wait_send()

    for c in range(NCH):
        for target, ok, rows_of, send, recv in sends(c):
            @pl.when(ok & (target != me))
            def _(rows_of=rows_of, target=target, send=send, recv=recv, c=c):
                part_copy(c, v, rows_of, target, send, recv).wait_send()

        for up, ok in ((True, above), (False, below)):
            @pl.when(ok)
            def _(up=up, c=c):
                for copy in z_copies(c, up):
                    copy.wait_send()

    for c in range(NOUT):
        for n, dz, ds, ok, _ in near:
            @pl.when(ok)
            def _(n=n, dz=dz, ds=ds, c=c):
                near_copy(n, dz, ds, c).wait_send()


def on_device(dims, camera, background, destination, offsets, shift_frac, psf_taps):
    slabs, views, bands = dims
    blocks, planes, rows, cols = camera.shape[1:]
    taps = psf_taps.shape[-1]
    margin = taps // 2
    tall = CZ * rows + CZ
    strip = rows // views
    wide = strip + 2 * HALO
    tap_rows = -(-3 * (taps + 1) // 8) * 8
    vmem = pl.BlockSpec(memory_space=pltpu.VMEM)
    hbm = functools.partial(pltpu.with_memory_space_constraint, memory_space=pltpu.HBM)
    cell = 4 * cols
    room = 2 * 1024 * 1024
    acc, tap_rows_all = pl.pallas_call(
        functools.partial(deposit_kernel, rows),
        in_specs=[pl.BlockSpec(memory_space=pltpu.HBM)] * 6,
        out_specs=(vmem, vmem),
        out_shape=(
            pltpu.VMEM((slabs, tall, cols), jnp.float32),
            pltpu.VMEM((tap_rows, cols), jnp.float32),
        ),
        scratch_shapes=[
            pltpu.SMEM((blocks,), jnp.int32),
            pltpu.SMEM((blocks,), jnp.int32),
            pltpu.SMEM((1, 1, 1), jnp.int32),
            pltpu.SMEM((3,), jnp.float32),
            pltpu.VMEM((3, 1, taps), jnp.float32),
            pltpu.VMEM((blocks, planes, rows, cols), jnp.float32),
            pltpu.SemaphoreType.DMA((blocks // CHUNK,)),
            pltpu.SemaphoreType.DMA((5,)),
        ],
        compiler_params=pltpu.CompilerParams(
            vmem_limit_bytes=cell * (blocks * planes * rows + slabs * tall) + room),
        name="deposit",
    )(hbm(destination.reshape(-1)), hbm(offsets.reshape(-1)), background, hbm(shift_frac[0]),
      hbm(jnp.transpose(psf_taps, (1, 0, 2))), hbm(camera[0]))

    dma = pltpu.SemaphoreType.DMA
    f32 = jnp.float32
    shapes = [
        (slabs, tall, cols), (slabs, tall, cols), (views, tap_rows, cols),
        (views, 3 * CZ, wide, cols), (3 * CZ, wide, cols), (3 * CZ, wide, cols),
    ]
    late = [
        (CZ + 2 * margin, wide, cols),
        (CZ + 2 * margin, strip + 2 * margin, cols), (CZ + 2 * margin, strip + 2 * margin, cols),
        (CZ, strip, cols), (CZ, strip, cols),
    ]
    total = sum([functools.reduce(lambda a, b: a * b, s) for s in shapes + late])
    total = total + cols * (slabs * tall + 2 * CZ * rows + views * 4 * cols)
    estimate, joined = pl.pallas_call(
        functools.partial(world_kernel, dims, rows, taps),
        in_specs=[vmem, vmem],
        out_specs=(vmem, vmem),
        out_shape=(
            jax.ShapeDtypeStruct((CZ, rows, cols), f32),
            jax.ShapeDtypeStruct((1, CZ, rows, cols), f32),
        ),
        scratch_shapes=[pltpu.VMEM(s, f32) for s in shapes]
        + [pltpu.VMEM((views, 2, 2 * cols, 2 * cols), jnp.bfloat16)]
        + [pltpu.VMEM(s, f32) for s in late]
        + [
            dma((slabs, NCH)), dma((slabs, NCH)), dma((slabs, NCH)), dma((slabs, NCH)),
            dma((views,)), dma((views,)), dma,
            dma((views, NCH)), dma((views, NCH)), dma((NCH,)), dma((views, NCH)), dma((NCH,)), dma((views, NCH)),
            dma((2, views, NCH)), dma((2, views, NCH)), dma((8, NOUT)), dma((8, NOUT)),
            dma((views, NOUT)), dma((views, NOUT)),
        ],
        compiler_params=pltpu.CompilerParams(
            collective_id=0, has_side_effects=True, vmem_limit_bytes=4 * total + room),
        name="world",
    )(acc, tap_rows_all)
    return estimate, joined


def solution(mesh):
    dims = (mesh.shape["gz"], mesh.shape["view"], mesh.shape["gy"])
    return jax.shard_map(
        functools.partial(on_device, dims),
        mesh=mesh,
        in_specs=(
            P("view", ("groups", "gz"), None, "gy", None),
            P("view", "gy", ("groups", "gz")),
            P("view", "gy", ("groups", "gz"), None),
            P("view", "gy", ("groups", "gz")),
            P("view", None),
            P("view", None, None),
        ),
        out_specs=(P(("groups", "gz"), "gy", None), P("view", ("groups", "gz"), "gy", None)),
        check_vma=False,
    )
```

```python
import functools

import jax
import jax.numpy as jnp
from jax import lax
from jax.experimental import pallas as pl
from jax.experimental.pallas import tpu as pltpu
from jax.sharding import PartitionSpec as P

CZ = 8
ITERS = 2
HALO = 8
CHUNK = 4
CP = 2
NCH = CZ // CP
OC = 4
NOUT = CZ // OC

DATA_FLOOR = 0.25
MESH = pl.DeviceIdType.MESH


def deposit_kernel(
    rows, dest_in, offs_in, level_in, frac_in, psf_in, cam_ref, acc_ref, tap_ref,
    dest, offs, level, frac, psf, cam, sems, small,
):
    taps = psf.shape[2]
    blocks, planes = cam_ref.shape[:2]
    pairs = ((dest_in, dest), (offs_in, offs), (level_in, level), (frac_in, frac), (psf_in, psf))
    copies = [pltpu.make_async_copy(a, b, small.at[n]) for n, (a, b) in enumerate(pairs)]
    for copy in copies:
        copy.start()

    def fetch(c):
        at = pl.ds(c * CHUNK, CHUNK)
        return pltpu.make_async_copy(cam_ref.at[at], cam.at[at], sems.at[c])

    for c in range(blocks // CHUNK):
        fetch(c).start()

    @pl.loop(0, acc_ref.shape[0])
    def _(s):
        acc_ref[s] = jnp.zeros(acc_ref.shape[1:], jnp.float32)

    for copy in copies:
        copy.wait()

    tap_ref[...] = jnp.zeros(tap_ref.shape, jnp.float32)
    for axis in range(3):
        scale = jnp.sum(psf[axis], axis=1, keepdims=True)
        share = psf[axis] / scale
        for t in range(taps):
            at = axis * taps + t
            tap_ref[at : at + 1, :] = jnp.broadcast_to(share[:, t : t + 1], (1, 128))
        at = 3 * taps + axis
        tap_ref[at : at + 1, :] = jnp.zeros((1, 128), jnp.float32) + frac[axis]

    fz = frac[0]
    base = level[0, 0, 0].astype(jnp.float32)

    @pl.loop(0, blocks // CHUNK)
    def _(c):
        fetch(c).wait()
        for i in range(CHUNK):
            b = c * CHUNK + i
            s = dest[b]
            o = offs[b]
            lower = cam[b, 0] - base
            for k in range(planes - 1):
                upper = cam[b, k + 1] - base
                at = pl.ds(pl.multiple_of(CZ + (o + k) * rows, 8), rows)
                acc_ref[s, at, :] = acc_ref[s, at, :] + ((1.0 - fz) * lower + fz * upper)
                cnt = pl.ds(o + k, 1)
                acc_ref[s, cnt, :] = acc_ref[s, cnt, :] + 1.0
                lower = upper


def world_kernel(
    dims, rows, taps,
    acc_ref, tap_in, est_ref, joined_ref,
    ru, rd, tap_all, jx, e0, e1, kx, za, zb, rt, yb, lg,
    us, ur, ds_, dr, tap_s, tap_r, loc_sem, ms, mr, los, lor, his, hir,
    zs, zr, es, er, out_s, out_r,
):
    slabs, views, bands = dims
    strip = rows // views
    wide = strip + 2 * HALO
    margin = taps // 2
    z = lax.axis_index("gz")
    v = lax.axis_index("view")
    g = lax.axis_index("gy")
    strips = views * bands
    me = v * bands + g
    band, idx = me // views, me % views

    def dev(zz, vv, gg):
        return {"gz": zz, "view": vv, "gy": gg}

    def strip_dev(zz, ss):
        return dev(zz, ss // bands, ss % bands)

    below, above = z > 0, z < slabs - 1
    left, right = me > 0, me < strips - 1

    barrier = pltpu.get_barrier_semaphore()

    def greet(target):
        pl.semaphore_signal(barrier, inc=1, device_id=target, device_id_type=MESH)

    amount = strips - 1
    for dz, zok in ((-1, below), (1, above)):
        for ds, sok in ((-1, left), (0, z >= 0), (1, right)):
            ok = zok & sok
            amount = amount + ok.astype(jnp.int32)

            @pl.when(ok)
            def _(dz=dz, ds=ds):
                greet(strip_dev(z + dz, me + ds))

    for d in range(1, strips):
        greet(strip_dev(z, (me + d) % strips))

    def clear(ref, planes, lo, hi):
        @pl.loop(planes[0], planes[1])
        def _(p):
            ref[p, lo:hi, :] = jnp.zeros((hi - lo, 128), jnp.float32)

    for edge, flow, halo in ((z == 0, ru, (0, CZ)), (z == slabs - 1, rd, (2 * CZ, 3 * CZ))):
        @pl.when(edge)
        def _(flow=flow, halo=halo):
            flow[z] = jnp.zeros(flow.shape[1:], jnp.float32)
            for ref in [e0, e1] + [jx.at[w] for w in range(views)]:
                clear(ref, halo, 0, wide)

    for edge, lo, hi in ((me == 0, 0, HALO), (me == strips - 1, HALO + strip, wide)):
        @pl.when(edge)
        def _(lo=lo, hi=hi):
            clear(e1, (0, 3 * CZ), lo, hi)
            for w in range(views):
                clear(jx.at[w], (CZ, 2 * CZ), lo, hi)

    pl.semaphore_wait(barrier, amount)

    def span(c):
        start = 0 if c == 0 else CZ + c * CP * rows
        return pl.ds(start, CZ + (c + 1) * CP * rows - start)

    def up_copy(src, t, c):
        return pltpu.make_async_remote_copy(
            src_ref=src.at[t, span(c)], dst_ref=ru.at[t, span(c)], send_sem=us.at[t, c],
            recv_sem=ur.at[t, c], device_id={"gz": z + 1}, device_id_type=MESH)

    def down_copy(src, t, c):
        return pltpu.make_async_remote_copy(
            src_ref=src.at[t, span(c)], dst_ref=rd.at[t, span(c)], send_sem=ds_.at[t, c],
            recv_sem=dr.at[t, c], device_id={"gz": z - 1}, device_id_type=MESH)

    @pl.when(z == 0)
    def _():
        @pl.loop(0, slabs - 1)
        def _(k):
            for c in range(NCH):
                up_copy(acc_ref, slabs - 1 - k, c).start()

    @pl.when(z == slabs - 1)
    def _():
        @pl.loop(0, slabs - 1)
        def _(k):
            for c in range(NCH):
                down_copy(acc_ref, k, c).start()

    own_tap = pltpu.make_async_copy(tap_in, tap_all.at[v], loc_sem)
    own_tap.start()

    def tap_copy(d):
        return pltpu.make_async_remote_copy(
            src_ref=tap_in, dst_ref=tap_all.at[v], send_sem=tap_s.at[d - 1],
            recv_sem=tap_r.at[d - 1], device_id={"view": (v + d) % views}, device_id_type=MESH)

    for d in range(1, views):
        tap_copy(d).start()

    def pass_on(copy, ref, t, ok):
        @pl.when(ok)
        def _():
            for c in range(NCH):
                at = span(c)
                copy(ref, t, c).wait_recv()
                ref[t, at] = ref[t, at] + acc_ref[t, at]
                copy(ref, t, c).start()

    def pass_up(k):
        t = slabs - 1 - k
        pass_on(up_copy, ru, t, below & (t > z))

    def pass_down(k):
        pass_on(down_copy, rd, k, above & (k < z))

    @pl.loop(0, slabs - 1)
    def _(k):
        low = 2 * z < slabs

        @pl.when(low)
        def _():
            pass_up(k)
            pass_down(k)

        @pl.when(jnp.logical_not(low))
        def _():
            pass_down(k)
            pass_up(k)

    own_tap.wait()
    for d in range(1, views):
        tap_copy(d).wait()

    apart = lax.broadcasted_iota(jnp.int32, (128, 128), 0) - lax.broadcasted_iota(jnp.int32, (128, 128), 1)

    @pl.loop(0, views)
    def _(w):
        ahead = jnp.zeros((128, 128), jnp.float32)
        back = jnp.zeros((128, 128), jnp.float32)
        for t in range(taps):
            tap = tap_all[w, 2 * taps + t : 2 * taps + t + 1, :]
            ahead = jnp.where(apart == t - margin, tap, ahead)
            back = jnp.where(apart == margin - t, tap, back)
        for n, full in enumerate((ahead, back)):
            top = full.astype(jnp.bfloat16)
            kx[w, n, 0:128, 0:128] = top
            kx[w, n, 128:256, 0:128] = top
            kx[w, n, 0:128, 128:256] = (full - top.astype(jnp.float32)).astype(jnp.bfloat16)
            kx[w, n, 128:256, 128:256] = jnp.zeros((128, 128), jnp.bfloat16)

    fy, fx = [tap_in[3 * taps + n : 3 * taps + n + 1, :] for n in (1, 2)]
    last_row = lax.broadcasted_iota(jnp.int32, (rows, 128), 0) == rows - 1
    last_col = lax.broadcasted_iota(jnp.int32, (rows, 128), 1) == 127
    joined = joined_ref.at[0]
    mid = pl.ds(CZ, CZ)

    def planes_of(c):
        return pl.ds(c * CP, CP), pl.ds(CZ + c * CP, CP)

    def piece(i):
        lo, hi = max(i * strip - HALO, 0), min((i + 1) * strip + HALO, rows)
        return (lo, hi), (lo - i * strip + HALO, hi - i * strip + HALO)

    low_edge = ((rows - HALO, rows), (0, HALO))
    high_edge = ((0, HALO), (HALO + strip, wide))

    def part_copy(c, w, rows_of, target, send, recv):
        src_p, dst_p = planes_of(c)
        (lo, hi), (dlo, dhi) = rows_of
        return pltpu.make_async_remote_copy(
            src_ref=joined.at[src_p, pl.ds(lo, hi - lo), :], dst_ref=jx.at[w, dst_p, pl.ds(dlo, dhi - dlo), :],
            send_sem=send, recv_sem=recv, device_id=strip_dev(z, target), device_id_type=MESH)

    def sends(c):
        out = []
        for i in range(views):
            out.append((g * views + i, z >= 0, piece(i), ms.at[i, c], mr.at[v, c]))
        out.append(((g + 1) * views, g < bands - 1, low_edge, los.at[c], lor.at[v, c]))
        out.append((g * views - 1, g > 0, high_edge, his.at[c], hir.at[v, c]))
        return out

    def join(c):
        src_p, _ = planes_of(c)

        @pl.when(below)
        def _():
            up_copy(acc_ref, z, c).wait_recv()

        @pl.when(above)
        def _():
            down_copy(acc_ref, z, c).wait_recv()

        for p in range(c * CP, (c + 1) * CP):
            at = pl.ds(CZ + p * rows, rows)
            total = acc_ref[z, at, :] + ru[z, at, :] + rd[z, at, :]
            cnt = pl.ds(p, 1)
            covered = acc_ref[z, cnt, :] + ru[z, cnt, :] + rd[z, cnt, :]
            follow = jnp.where(last_row, total, pltpu.roll(total, rows - 1, 0))
            total = (1.0 - fy) * total + fy * follow
            follow = jnp.where(last_col, total, pltpu.roll(total, 127, 1))
            total = (1.0 - fx) * total + fx * follow
            joined_ref[0, p] = jnp.maximum(total / (covered + 1.0), DATA_FLOOR)
        for target, ok, rows_of, send, recv in sends(c):
            (lo, hi), (dlo, dhi) = rows_of

            @pl.when(ok & (target != me))
            def _(rows_of=rows_of, target=target, send=send, recv=recv):
                part_copy(c, v, rows_of, target, send, recv).start()

            @pl.when(ok & (target == me))
            def _(lo=lo, hi=hi, dlo=dlo, dhi=dhi):
                for p in range(c * CP, (c + 1) * CP):
                    jx[v, CZ + p, dlo:dhi, :] = joined_ref[0, p, lo:hi, :]

    def z_copy(ref, w, c, up, send, recv):
        dst = (0 if up else 2 * CZ) + c * CP
        src = CZ + c * CP
        a, b = ref.at[pl.ds(src, CP)], ref.at[pl.ds(dst, CP)]
        return pltpu.make_async_remote_copy(
            src_ref=a, dst_ref=b, send_sem=send, recv_sem=recv,
            device_id={"gz": z + 1 if up else z - 1}, device_id_type=MESH)

    def z_copies(c, up):
        side = 1 if up else 0
        near = c * CP >= CZ - margin if up else c * CP < margin
        if near:
            return [z_copy(jx.at[w], w, c, up, zs.at[side, w, c], zr.at[side, w, c]) for w in range(views)]
        return [z_copy(e0, 0, c, up, zs.at[side, 0, c], zr.at[side, 0, c])]

    def average(p):
        total = jx[0, p]
        for w in range(1, views):
            total = total + jx[w, p]
        e0[p] = total / views

    def spread(c):
        for w in range(views):
            for i in range(views):
                @pl.when((idx == i) & ((w != v) | (band != g)))
                def _(i=i, w=w):
                    part_copy(c, w, piece(i), me, ms.at[i, c], mr.at[w, c]).wait_recv()

            @pl.when((idx == 0) & (band > 0) & ((w != v) | (band - 1 != g)))
            def _(w=w):
                part_copy(c, w, low_edge, me, los.at[c], lor.at[w, c]).wait_recv()

            @pl.when((idx == views - 1) & (band < bands - 1) & ((w != v) | (band + 1 != g)))
            def _(w=w):
                part_copy(c, w, high_edge, me, his.at[c], hir.at[w, c]).wait_recv()

        for p in range(c * CP, (c + 1) * CP):
            average(CZ + p)
        for up, ok in ((True, above), (False, below)):
            @pl.when(ok)
            def _(up=up):
                for copy in z_copies(c, up):
                    copy.start()

    join(0)
    for c in range(1, NCH):
        join(c)
        spread(c - 1)
    spread(NCH - 1)

    for c in range(NCH):
        for up, ok in ((True, below), (False, above)):
            @pl.when(ok)
            def _(up=up, c=c):
                copies = z_copies(c, up)
                for copy in copies:
                    copy.wait_recv()
                if len(copies) == views and views > 1:
                    for p in range(c * CP, (c + 1) * CP):
                        average((0 if up else 2 * CZ) + p)

    planes_r = CZ + 2 * margin
    rows_r = strip + 2 * margin

    def along_x(u, w, n):
        top = u.astype(jnp.bfloat16)
        rest = (u - top.astype(jnp.float32)).astype(jnp.bfloat16)
        both = jnp.dot(jnp.concatenate([top, rest], axis=1), kx[w, n], preferred_element_type=jnp.float32)
        return both[:, 0:128] + both[:, 128:256]

    def weighted(terms, weights):
        total = weights[0] * terms[0]
        for term, weight in zip(terms[1:], weights[1:]):
            total = total + weight * term
        return total

    def correct(est, emit):
        for w in range(views):
            def tap(axis, t):
                at = axis * taps + t
                return tap_all[w, at : at + 1, :]

            @pl.loop(0, wide // 8, unroll=2)
            def _(r):
                at = pl.ds(pl.multiple_of(r * 8, 8), 8)
                column = [est[CZ - 2 * margin + p, at, :] for p in range(planes_r + 2 * margin)]
                for p in range(planes_r):
                    za[p, at, :] = weighted(column[p : p + taps], [tap(0, t) for t in range(taps)])

            @pl.loop(0, planes_r, unroll=4)
            def _(p):
                base = HALO - 2 * margin
                zb[p] = weighted([za[p, base + t : base + t + rows_r, :] for t in range(taps)],
                                 [tap(1, t) for t in range(taps)])

            @pl.loop(0, planes_r // 4)
            def _(c):
                at = pl.ds(c * 4, 4)
                blurred = along_x(zb[at].reshape(4 * rows_r, 128), w, 0).reshape(4, rows_r, 128)
                data = jx[w, pl.ds(c * 4 + CZ - margin, 4), HALO - margin : HALO - margin + rows_r, :]
                rt[at] = jnp.where(data > 0.0, data / blurred, 0.0)

            @pl.loop(0, rows_r // 8, unroll=True)
            def _(r):
                at = pl.ds(pl.multiple_of(r * 8, 8), 8)
                column = [rt[p, at, :] for p in range(planes_r)]
                for p in range(CZ):
                    za[p, at, :] = weighted(column[p : p + taps], [tap(0, taps - 1 - t) for t in range(taps)])

            @pl.loop(0, CZ, unroll=4)
            def _(p):
                yb[p] = weighted([za[p, t : t + strip, :] for t in range(taps)],
                                 [tap(1, taps - 1 - t) for t in range(taps)])

            for c in range(NOUT):
                at = pl.ds(c * OC, OC)
                logs = jnp.log(along_x(yb[at].reshape(OC * strip, 128), w, 1)).reshape(OC, strip, 128)
                if w > 0:
                    logs = lg[at] + logs
                if w < views - 1:
                    lg[at] = logs
                else:
                    emit(c, est[pl.ds(CZ + c * OC, OC), HALO : HALO + strip, :] * jnp.exp(logs / views))

    inner = pl.ds(HALO, strip)
    near = []
    for n, (dz, ds) in enumerate([(a, b) for a in (-1, 1, 0) for b in (0, -1, 1) if a or b]):
        zok = {-1: below, 0: z >= 0, 1: above}[dz]
        sok = {-1: left, 0: z >= 0, 1: right}[ds]
        far_z = {-1: above, 0: z >= 0, 1: below}[dz]
        far_s = {-1: right, 0: z >= 0, 1: left}[ds]
        near.append((n, dz, ds, zok & sok, far_z & far_s))

    def near_copy(n, dz, ds, c):
        src_r = {-1: pl.ds(HALO, HALO), 0: inner, 1: pl.ds(strip, HALO)}[ds]
        dst_r = {-1: pl.ds(HALO + strip, HALO), 0: inner, 1: pl.ds(0, HALO)}[ds]
        dst = {-1: 2 * CZ, 0: CZ, 1: 0}[dz] + c * OC
        return pltpu.make_async_remote_copy(
            src_ref=e1.at[pl.ds(CZ + c * OC, OC), src_r, :], dst_ref=e1.at[pl.ds(dst, OC), dst_r, :],
            send_sem=es.at[n, c], recv_sem=er.at[n, c], device_id=strip_dev(z + dz, me + ds), device_id_type=MESH)

    def emit_step(c, new):
        e1[pl.ds(CZ + c * OC, OC), HALO : HALO + strip, :] = new
        for n, dz, ds, ok, _ in near:
            @pl.when(ok)
            def _(n=n, dz=dz, ds=ds):
                near_copy(n, dz, ds, c).start()

    correct(e0, emit_step)
    for c in range(NOUT):
        for n, dz, ds, _, ok in near:
            @pl.when(ok)
            def _(n=n, dz=dz, ds=ds, c=c):
                near_copy(n, dz, ds, c).wait_recv()

    def out_copy(c, w, target_g, i):
        at = pl.ds(pl.multiple_of(i * strip, 8), strip)
        part = pl.ds(c * OC, OC)
        return pltpu.make_async_remote_copy(
            src_ref=lg.at[part], dst_ref=est_ref.at[part, at, :], send_sem=out_s.at[w, c],
            recv_sem=out_r.at[i, c], device_id=dev(z, w, target_g), device_id_type=MESH)

    def emit_last(c, new):
        lg[pl.ds(c * OC, OC)] = new
        for w in range(views):
            away = (w != v) | (band != g)

            @pl.when(away)
            def _(w=w):
                out_copy(c, w, band, idx).start()

            @pl.when(jnp.logical_not(away))
            def _():
                est_ref[pl.ds(c * OC, OC), pl.ds(pl.multiple_of(idx * strip, 8), strip), :] = new

    correct(e1, emit_last)
    for c in range(NOUT):
        for i in range(views):
            @pl.when(g * views + i != me)
            def _(i=i, c=c):
                out_copy(c, 0, g, i).wait_recv()

    for c in range(NOUT):
        for w in range(views):
            @pl.when((w != v) | (band != g))
            def _(w=w, c=c):
                out_copy(c, w, band, idx).wait_send()

    @pl.loop(0, slabs)
    def _(t):
        for c in range(NCH):
            @pl.when(t > z)
            def _():
                up_copy(acc_ref, t, c).wait_send()

            @pl.when(t < z)
            def _():
                down_copy(acc_ref, t, c).wait_send()

    for c in range(NCH):
        for target, ok, rows_of, send, recv in sends(c):
            @pl.when(ok & (target != me))
            def _(rows_of=rows_of, target=target, send=send, recv=recv, c=c):
                part_copy(c, v, rows_of, target, send, recv).wait_send()

        for up, ok in ((True, above), (False, below)):
            @pl.when(ok)
            def _(up=up, c=c):
                for copy in z_copies(c, up):
                    copy.wait_send()

    for c in range(NOUT):
        for n, dz, ds, ok, _ in near:
            @pl.when(ok)
            def _(n=n, dz=dz, ds=ds, c=c):
                near_copy(n, dz, ds, c).wait_send()


def on_device(dims, camera, background, destination, offsets, shift_frac, psf_taps):
    slabs, views, bands = dims
    blocks, planes, rows, cols = camera.shape[1:]
    taps = psf_taps.shape[-1]
    margin = taps // 2
    tall = CZ * rows + CZ
    strip = rows // views
    wide = strip + 2 * HALO
    tap_rows = -(-3 * (taps + 1) // 8) * 8
    vmem = pl.BlockSpec(memory_space=pltpu.VMEM)
    hbm = functools.partial(pltpu.with_memory_space_constraint, memory_space=pltpu.HBM)
    cell = 4 * cols
    room = 2 * 1024 * 1024
    acc, tap_rows_all = pl.pallas_call(
        functools.partial(deposit_kernel, rows),
        in_specs=[pl.BlockSpec(memory_space=pltpu.HBM)] * 6,
        out_specs=(vmem, vmem),
        out_shape=(
            pltpu.VMEM((slabs, tall, cols), jnp.float32),
            pltpu.VMEM((tap_rows, cols), jnp.float32),
        ),
        scratch_shapes=[
            pltpu.SMEM((blocks,), jnp.int32),
            pltpu.SMEM((blocks,), jnp.int32),
            pltpu.SMEM((1, 1, 1), jnp.int32),
            pltpu.SMEM((3,), jnp.float32),
            pltpu.VMEM((3, 1, taps), jnp.float32),
            pltpu.VMEM((blocks, planes, rows, cols), jnp.float32),
            pltpu.SemaphoreType.DMA((blocks // CHUNK,)),
            pltpu.SemaphoreType.DMA((5,)),
        ],
        compiler_params=pltpu.CompilerParams(
            vmem_limit_bytes=cell * (blocks * planes * rows + slabs * tall) + room),
        name="deposit",
    )(hbm(destination.reshape(-1)), hbm(offsets.reshape(-1)), background, hbm(shift_frac[0]),
      hbm(jnp.transpose(psf_taps, (1, 0, 2))), hbm(camera[0]))

    dma = pltpu.SemaphoreType.DMA
    f32 = jnp.float32
    shapes = [
        (slabs, tall, cols), (slabs, tall, cols), (views, tap_rows, cols),
        (views, 3 * CZ, wide, cols), (3 * CZ, wide, cols), (3 * CZ, wide, cols),
    ]
    late = [
        (CZ + 2 * margin, wide, cols),
        (CZ + 2 * margin, strip + 2 * margin, cols), (CZ + 2 * margin, strip + 2 * margin, cols),
        (CZ, strip, cols), (CZ, strip, cols),
    ]
    total = sum([functools.reduce(lambda a, b: a * b, s) for s in shapes + late])
    total = total + cols * (slabs * tall + 2 * CZ * rows + views * 4 * cols)
    estimate, joined = pl.pallas_call(
        functools.partial(world_kernel, dims, rows, taps),
        in_specs=[vmem, vmem],
        out_specs=(vmem, vmem),
        out_shape=(
            jax.ShapeDtypeStruct((CZ, rows, cols), f32),
            jax.ShapeDtypeStruct((1, CZ, rows, cols), f32),
        ),
        scratch_shapes=[pltpu.VMEM(s, f32) for s in shapes]
        + [pltpu.VMEM((views, 2, 2 * cols, 2 * cols), jnp.bfloat16)]
        + [pltpu.VMEM(s, f32) for s in late]
        + [
            dma((slabs, NCH)), dma((slabs, NCH)), dma((slabs, NCH)), dma((slabs, NCH)),
            dma((views,)), dma((views,)), dma,
            dma((views, NCH)), dma((views, NCH)), dma((NCH,)), dma((views, NCH)), dma((NCH,)), dma((views, NCH)),
            dma((2, views, NCH)), dma((2, views, NCH)), dma((8, NOUT)), dma((8, NOUT)),
            dma((views, NOUT)), dma((views, NOUT)),
        ],
        compiler_params=pltpu.CompilerParams(
            collective_id=0, has_side_effects=True, vmem_limit_bytes=4 * total + room),
        name="world",
    )(acc, tap_rows_all)
    return estimate, joined


def solution(mesh):
    dims = (mesh.shape["gz"], mesh.shape["view"], mesh.shape["gy"])
    return jax.shard_map(
        functools.partial(on_device, dims),
        mesh=mesh,
        in_specs=(
            P("view", ("groups", "gz"), None, "gy", None),
            P("view", "gy", ("groups", "gz")),
            P("view", "gy", ("groups", "gz"), None),
            P("view", "gy", ("groups", "gz")),
            P("view", None),
            P("view", None, None),
        ),
        out_specs=(P(("groups", "gz"), "gy", None), P("view", ("groups", "gz"), "gy", None)),
        check_vma=False,
    )
```

```python
import functools

import jax
import jax.numpy as jnp
from jax import lax
from jax.experimental import pallas as pl
from jax.experimental.pallas import tpu as pltpu
from jax.sharding import PartitionSpec as P

CZ = 8
ITERS = 2
HALO = 8
CHUNK = 4
CP = 2
NCH = CZ // CP
OC = 4
NOUT = CZ // OC

DATA_FLOOR = 0.25
TINY = 1e-30
MESH = pl.DeviceIdType.MESH


def deposit_kernel(
    rows, dest_in, offs_in, level_in, frac_in, psf_in, cam_ref, acc_ref, tap_ref,
    dest, offs, level, frac, psf, cam, sems, small,
):
    taps = psf.shape[2]
    blocks, planes = cam_ref.shape[:2]
    pairs = ((dest_in, dest), (offs_in, offs), (level_in, level), (frac_in, frac), (psf_in, psf))
    copies = [pltpu.make_async_copy(a, b, small.at[n]) for n, (a, b) in enumerate(pairs)]
    for copy in copies:
        copy.start()

    def fetch(c):
        at = pl.ds(c * CHUNK, CHUNK)
        return pltpu.make_async_copy(cam_ref.at[at], cam.at[at], sems.at[c])

    for c in range(blocks // CHUNK):
        fetch(c).start()

    @pl.loop(0, acc_ref.shape[0])
    def _(s):
        acc_ref[s] = jnp.zeros(acc_ref.shape[1:], jnp.float32)

    for copy in copies:
        copy.wait()

    tap_ref[...] = jnp.zeros(tap_ref.shape, jnp.float32)
    for axis in range(3):
        scale = jnp.sum(psf[axis], axis=1, keepdims=True)
        share = psf[axis] / scale
        for t in range(taps):
            at = axis * taps + t
            tap_ref[at : at + 1, :] = jnp.broadcast_to(share[:, t : t + 1], (1, 128))
        at = 3 * taps + axis
        tap_ref[at : at + 1, :] = jnp.zeros((1, 128), jnp.float32) + frac[axis]

    fz = frac[0]
    base = level[0, 0, 0].astype(jnp.float32)

    @pl.loop(0, blocks // CHUNK)
    def _(c):
        fetch(c).wait()
        for i in range(CHUNK):
            b = c * CHUNK + i
            s = dest[b]
            o = offs[b]
            lower = cam[b, 0] - base
            for k in range(planes - 1):
                upper = cam[b, k + 1] - base
                at = pl.ds(pl.multiple_of(CZ + (o + k) * rows, 8), rows)
                acc_ref[s, at, :] = acc_ref[s, at, :] + ((1.0 - fz) * lower + fz * upper)
                cnt = pl.ds(o + k, 1)
                acc_ref[s, cnt, :] = acc_ref[s, cnt, :] + 1.0
                lower = upper


def world_kernel(
    dims, rows, taps,
    acc_ref, tap_in, est_ref, joined_ref,
    ru, rd, tap_all, jx, e0, e1, kx, za, zb, rt, yb, part, lg,
    us, ur, ds_, dr, tap_s, tap_r, loc_sem, ms, mr, los, lor, his, hir,
    zs, zr, es, er, out_s, out_r,
):
    slabs, views, bands = dims
    strip = rows // views
    wide = strip + 2 * HALO
    margin = taps // 2
    z = lax.axis_index("gz")
    v = lax.axis_index("view")
    g = lax.axis_index("gy")
    strips = views * bands
    me = v * bands + g
    band, idx = me // views, me % views

    def dev(zz, vv, gg):
        return {"gz": zz, "view": vv, "gy": gg}

    def strip_dev(zz, ss):
        return dev(zz, ss // bands, ss % bands)

    below, above = z > 0, z < slabs - 1
    left, right = me > 0, me < strips - 1

    barrier = pltpu.get_barrier_semaphore()

    def greet(target):
        pl.semaphore_signal(barrier, inc=1, device_id=target, device_id_type=MESH)

    amount = strips - 1
    for dz, zok in ((-1, below), (1, above)):
        for ds, sok in ((-1, left), (0, z >= 0), (1, right)):
            ok = zok & sok
            amount = amount + ok.astype(jnp.int32)

            @pl.when(ok)
            def _(dz=dz, ds=ds):
                greet(strip_dev(z + dz, me + ds))

    for d in range(1, strips):
        greet(strip_dev(z, (me + d) % strips))

    def clear(ref, planes, lo, hi):
        @pl.loop(planes[0], planes[1])
        def _(p):
            ref[p, lo:hi, :] = jnp.zeros((hi - lo, 128), jnp.float32)

    for edge, flow, halo in ((z == 0, ru, (0, CZ)), (z == slabs - 1, rd, (2 * CZ, 3 * CZ))):
        @pl.when(edge)
        def _(flow=flow, halo=halo):
            flow[z] = jnp.zeros(flow.shape[1:], jnp.float32)
            for ref in [e0, e1] + [jx.at[w] for w in range(views)]:
                clear(ref, halo, 0, wide)

    for edge, lo, hi in ((me == 0, 0, HALO), (me == strips - 1, HALO + strip, wide)):
        @pl.when(edge)
        def _(lo=lo, hi=hi):
            clear(e1, (0, 3 * CZ), lo, hi)
            for w in range(views):
                clear(jx.at[w], (CZ, 2 * CZ), lo, hi)

    pl.semaphore_wait(barrier, amount)

    def span(c):
        start = 0 if c == 0 else CZ + c * CP * rows
        return pl.ds(start, CZ + (c + 1) * CP * rows - start)

    def up_copy(src, t, c):
        return pltpu.make_async_remote_copy(
            src_ref=src.at[t, span(c)], dst_ref=ru.at[t, span(c)], send_sem=us.at[t, c],
            recv_sem=ur.at[t, c], device_id={"gz": z + 1}, device_id_type=MESH)

    def down_copy(src, t, c):
        return pltpu.make_async_remote_copy(
            src_ref=src.at[t, span(c)], dst_ref=rd.at[t, span(c)], send_sem=ds_.at[t, c],
            recv_sem=dr.at[t, c], device_id={"gz": z - 1}, device_id_type=MESH)

    @pl.when(z == 0)
    def _():
        @pl.loop(0, slabs - 1)
        def _(k):
            for c in range(NCH):
                up_copy(acc_ref, slabs - 1 - k, c).start()

    @pl.when(z == slabs - 1)
    def _():
        @pl.loop(0, slabs - 1)
        def _(k):
            for c in range(NCH):
                down_copy(acc_ref, k, c).start()

    own_tap = pltpu.make_async_copy(tap_in, tap_all.at[v], loc_sem)
    own_tap.start()

    def tap_copy(d):
        return pltpu.make_async_remote_copy(
            src_ref=tap_in, dst_ref=tap_all.at[v], send_sem=tap_s.at[d - 1],
            recv_sem=tap_r.at[d - 1], device_id={"view": (v + d) % views}, device_id_type=MESH)

    for d in range(1, views):
        tap_copy(d).start()

    def pass_on(copy, ref, t, ok):
        @pl.when(ok)
        def _():
            for c in range(NCH):
                at = span(c)
                copy(ref, t, c).wait_recv()
                ref[t, at] = ref[t, at] + acc_ref[t, at]
                copy(ref, t, c).start()

    def pass_up(k):
        t = slabs - 1 - k
        pass_on(up_copy, ru, t, below & (t > z))

    def pass_down(k):
        pass_on(down_copy, rd, k, above & (k < z))

    @pl.loop(0, slabs - 1)
    def _(k):
        low = 2 * z < slabs

        @pl.when(low)
        def _():
            pass_up(k)
            pass_down(k)

        @pl.when(jnp.logical_not(low))
        def _():
            pass_down(k)
            pass_up(k)

    own_tap.wait()
    for d in range(1, views):
        tap_copy(d).wait()

    apart = lax.broadcasted_iota(jnp.int32, (128, 128), 0) - lax.broadcasted_iota(jnp.int32, (128, 128), 1)

    @pl.loop(0, views)
    def _(w):
        ahead = jnp.zeros((128, 128), jnp.float32)
        back = jnp.zeros((128, 128), jnp.float32)
        for t in range(taps):
            tap = tap_all[w, 2 * taps + t : 2 * taps + t + 1, :]
            ahead = jnp.where(apart == t - margin, tap, ahead)
            back = jnp.where(apart == margin - t, tap, back)
        for n, full in enumerate((ahead, back)):
            top = full.astype(jnp.bfloat16)
            kx[w, n, 0:128, 0:128] = top
            kx[w, n, 128:256, 0:128] = top
            kx[w, n, 0:128, 128:256] = (full - top.astype(jnp.float32)).astype(jnp.bfloat16)
            kx[w, n, 128:256, 128:256] = jnp.zeros((128, 128), jnp.bfloat16)

    fy, fx = [tap_in[3 * taps + n : 3 * taps + n + 1, :] for n in (1, 2)]
    last_row = lax.broadcasted_iota(jnp.int32, (rows, 128), 0) == rows - 1
    last_col = lax.broadcasted_iota(jnp.int32, (rows, 128), 1) == 127
    joined = joined_ref.at[0]
    mid = pl.ds(CZ, CZ)

    def planes_of(c):
        return pl.ds(c * CP, CP), pl.ds(CZ + c * CP, CP)

    def piece(i):
        lo, hi = max(i * strip - HALO, 0), min((i + 1) * strip + HALO, rows)
        return (lo, hi), (lo - i * strip + HALO, hi - i * strip + HALO)

    low_edge = ((rows - HALO, rows), (0, HALO))
    high_edge = ((0, HALO), (HALO + strip, wide))

    def part_copy(c, w, rows_of, target, send, recv):
        src_p, dst_p = planes_of(c)
        (lo, hi), (dlo, dhi) = rows_of
        return pltpu.make_async_remote_copy(
            src_ref=joined.at[src_p, pl.ds(lo, hi - lo), :], dst_ref=jx.at[w, dst_p, pl.ds(dlo, dhi - dlo), :],
            send_sem=send, recv_sem=recv, device_id=strip_dev(z, target), device_id_type=MESH)

    def sends(c):
        out = []
        for i in range(views):
            out.append((g * views + i, z >= 0, piece(i), ms.at[i, c], mr.at[v, c]))
        out.append(((g + 1) * views, g < bands - 1, low_edge, los.at[c], lor.at[v, c]))
        out.append((g * views - 1, g > 0, high_edge, his.at[c], hir.at[v, c]))
        return out

    def join(c):
        src_p, _ = planes_of(c)

        @pl.when(below)
        def _():
            up_copy(acc_ref, z, c).wait_recv()

        @pl.when(above)
        def _():
            down_copy(acc_ref, z, c).wait_recv()

        for p in range(c * CP, (c + 1) * CP):
            at = pl.ds(CZ + p * rows, rows)
            total = acc_ref[z, at, :] + ru[z, at, :] + rd[z, at, :]
            cnt = pl.ds(p, 1)
            covered = acc_ref[z, cnt, :] + ru[z, cnt, :] + rd[z, cnt, :]
            follow = jnp.where(last_row, total, pltpu.roll(total, rows - 1, 0))
            total = (1.0 - fy) * total + fy * follow
            follow = jnp.where(last_col, total, pltpu.roll(total, 127, 1))
            total = (1.0 - fx) * total + fx * follow
            joined_ref[0, p] = jnp.maximum(total / (covered + 1.0), DATA_FLOOR)
        for target, ok, rows_of, send, recv in sends(c):
            (lo, hi), (dlo, dhi) = rows_of

            @pl.when(ok & (target != me))
            def _(rows_of=rows_of, target=target, send=send, recv=recv):
                part_copy(c, v, rows_of, target, send, recv).start()

            @pl.when(ok & (target == me))
            def _(lo=lo, hi=hi, dlo=dlo, dhi=dhi):
                for p in range(c * CP, (c + 1) * CP):
                    jx[v, CZ + p, dlo:dhi, :] = joined_ref[0, p, lo:hi, :]

    def z_copy(ref, w, c, up, send, recv):
        dst = (0 if up else 2 * CZ) + c * CP
        src = CZ + c * CP
        a, b = ref.at[pl.ds(src, CP)], ref.at[pl.ds(dst, CP)]
        return pltpu.make_async_remote_copy(
            src_ref=a, dst_ref=b, send_sem=send, recv_sem=recv,
            device_id={"gz": z + 1 if up else z - 1}, device_id_type=MESH)

    def z_copies(c, up):
        side = 1 if up else 0
        near = c * CP >= CZ - margin if up else c * CP < margin
        if near:
            return [z_copy(jx.at[w], w, c, up, zs.at[side, w, c], zr.at[side, w, c]) for w in range(views)]
        return [z_copy(e0, 0, c, up, zs.at[side, 0, c], zr.at[side, 0, c])]

    def average(p):
        total = jx[0, p]
        for w in range(1, views):
            total = total + jx[w, p]
        e0[p] = total / views

    def spread(c):
        for w in range(views):
            for i in range(views):
                @pl.when((idx == i) & ((w != v) | (band != g)))
                def _(i=i, w=w):
                    part_copy(c, w, piece(i), me, ms.at[i, c], mr.at[w, c]).wait_recv()

            @pl.when((idx == 0) & (band > 0) & ((w != v) | (band - 1 != g)))
            def _(w=w):
                part_copy(c, w, low_edge, me, los.at[c], lor.at[w, c]).wait_recv()

            @pl.when((idx == views - 1) & (band < bands - 1) & ((w != v) | (band + 1 != g)))
            def _(w=w):
                part_copy(c, w, high_edge, me, his.at[c], hir.at[w, c]).wait_recv()

        for p in range(c * CP, (c + 1) * CP):
            average(CZ + p)
        for up, ok in ((True, above), (False, below)):
            @pl.when(ok)
            def _(up=up):
                for copy in z_copies(c, up):
                    copy.start()

    join(0)
    for c in range(1, NCH):
        join(c)
        spread(c - 1)
    spread(NCH - 1)

    for c in range(NCH):
        for up, ok in ((True, below), (False, above)):
            @pl.when(ok)
            def _(up=up, c=c):
                copies = z_copies(c, up)
                for copy in copies:
                    copy.wait_recv()
                if len(copies) == views and views > 1:
                    for p in range(c * CP, (c + 1) * CP):
                        average((0 if up else 2 * CZ) + p)

    planes_r = CZ + 2 * margin
    rows_r = strip + 2 * margin

    def along_x(u, w, n):
        top = u.astype(jnp.bfloat16)
        rest = (u - top.astype(jnp.float32)).astype(jnp.bfloat16)
        both = jnp.dot(jnp.concatenate([top, rest], axis=1), kx[w, n], preferred_element_type=jnp.float32)
        return both[:, 0:128] + both[:, 128:256]

    def weighted(terms, weights):
        total = weights[0] * terms[0]
        for term, weight in zip(terms[1:], weights[1:]):
            total = total + weight * term
        return total

    def root(terms):
        if len(terms) == 1:
            return terms[0]
        if len(terms) % 2:
            total = jnp.log(terms[0])
            for term in terms[1:]:
                total = total + jnp.log(term)
            return jnp.exp(total / len(terms))
        return root([jnp.sqrt(a * b) for a, b in zip(terms[0::2], terms[1::2])])

    def correct(est, emit):
        for w in range(views):
            def tap(axis, t, w=w):
                at = axis * taps + t
                return tap_all[w, at : at + 1, :]

            @pl.loop(0, wide // 8, unroll=2)
            def _(r):
                at = pl.ds(pl.multiple_of(r * 8, 8), 8)
                column = [est[CZ - 2 * margin + p, at, :] for p in range(planes_r + 2 * margin)]
                for p in range(planes_r):
                    za[p, at, :] = weighted(column[p : p + taps], [tap(0, t) for t in range(taps)])

            @pl.loop(0, planes_r, unroll=4)
            def _(p):
                base = HALO - 2 * margin
                zb[p] = weighted([za[p, base + t : base + t + rows_r, :] for t in range(taps)],
                                 [tap(1, t) for t in range(taps)])

            @pl.loop(0, planes_r // 4)
            def _(c):
                at = pl.ds(c * 4, 4)
                blurred = along_x(zb[at].reshape(4 * rows_r, 128), w, 0).reshape(4, rows_r, 128)
                data = jx[w, pl.ds(c * 4 + CZ - margin, 4), HALO - margin : HALO - margin + rows_r, :]
                blurred = jnp.maximum(blurred, TINY)
                inverse = pl.reciprocal(blurred, approx=True)
                inverse = inverse * (2.0 - blurred * inverse)
                rt[w, at] = data * inverse

        for c in range(NOUT):
            for w in range(views):
                def tap(axis, t, w=w):
                    at = axis * taps + taps - 1 - t
                    return tap_all[w, at : at + 1, :]

                for r in range(rows_r // 8):
                    at = pl.ds(r * 8, 8)
                    column = [rt[w, c * OC + p, at, :] for p in range(OC + 2 * margin)]
                    for p in range(OC):
                        za[p, at, :] = weighted(column[p : p + taps], [tap(0, t) for t in range(taps)])
                for p in range(OC):
                    yb[p] = weighted([za[p, t : t + strip, :] for t in range(taps)], [tap(1, t) for t in range(taps)])
                part[w] = along_x(yb[...].reshape(OC * strip, 128), w, 1).reshape(OC, strip, 128)
            emit(c, est[pl.ds(CZ + c * OC, OC), HALO : HALO + strip, :] * root([part[w] for w in range(views)]))

    inner = pl.ds(HALO, strip)
    near = []
    for n, (dz, ds) in enumerate([(a, b) for a in (-1, 1, 0) for b in (0, -1, 1) if a or b]):
        zok = {-1: below, 0: z >= 0, 1: above}[dz]
        sok = {-1: left, 0: z >= 0, 1: right}[ds]
        far_z = {-1: above, 0: z >= 0, 1: below}[dz]
        far_s = {-1: right, 0: z >= 0, 1: left}[ds]
        near.append((n, dz, ds, zok & sok, far_z & far_s))

    def near_copy(n, dz, ds, c):
        src_r = {-1: pl.ds(HALO, HALO), 0: inner, 1: pl.ds(strip, HALO)}[ds]
        dst_r = {-1: pl.ds(HALO + strip, HALO), 0: inner, 1: pl.ds(0, HALO)}[ds]
        dst = {-1: 2 * CZ, 0: CZ, 1: 0}[dz] + c * OC
        return pltpu.make_async_remote_copy(
            src_ref=e1.at[pl.ds(CZ + c * OC, OC), src_r, :], dst_ref=e1.at[pl.ds(dst, OC), dst_r, :],
            send_sem=es.at[n, c], recv_sem=er.at[n, c], device_id=strip_dev(z + dz, me + ds), device_id_type=MESH)

    def emit_step(c, new):
        e1[pl.ds(CZ + c * OC, OC), HALO : HALO + strip, :] = new
        for n, dz, ds, ok, _ in near:
            @pl.when(ok)
            def _(n=n, dz=dz, ds=ds):
                near_copy(n, dz, ds, c).start()

    correct(e0, emit_step)

    @pl.loop(0, slabs)
    def _(t):
        for c in range(NCH):
            @pl.when(t > z)
            def _():
                up_copy(acc_ref, t, c).wait_send()

            @pl.when(t < z)
            def _():
                down_copy(acc_ref, t, c).wait_send()

    for c in range(NCH):
        for target, ok, rows_of, send, recv in sends(c):
            @pl.when(ok & (target != me))
            def _(rows_of=rows_of, target=target, send=send, recv=recv, c=c):
                part_copy(c, v, rows_of, target, send, recv).wait_send()

        for up, ok in ((True, above), (False, below)):
            @pl.when(ok)
            def _(up=up, c=c):
                for copy in z_copies(c, up):
                    copy.wait_send()

    for c in range(NOUT):
        for n, dz, ds, _, ok in near:
            @pl.when(ok)
            def _(n=n, dz=dz, ds=ds, c=c):
                near_copy(n, dz, ds, c).wait_recv()

    def out_copy(c, w, target_g, i):
        at = pl.ds(pl.multiple_of(i * strip, 8), strip)
        part = pl.ds(c * OC, OC)
        return pltpu.make_async_remote_copy(
            src_ref=lg.at[part], dst_ref=est_ref.at[part, at, :], send_sem=out_s.at[w, c],
            recv_sem=out_r.at[i, c], device_id=dev(z, w, target_g), device_id_type=MESH)

    def emit_last(c, new):
        lg[pl.ds(c * OC, OC)] = new
        for w in range(views):
            away = (w != v) | (band != g)

            @pl.when(away)
            def _(w=w):
                out_copy(c, w, band, idx).start()

            @pl.when(jnp.logical_not(away))
            def _():
                est_ref[pl.ds(c * OC, OC), pl.ds(pl.multiple_of(idx * strip, 8), strip), :] = new

    correct(e1, emit_last)

    for c in range(NOUT):
        for n, dz, ds, ok, _ in near:
            @pl.when(ok)
            def _(n=n, dz=dz, ds=ds, c=c):
                near_copy(n, dz, ds, c).wait_send()

    for c in range(NOUT):
        for i in range(views):
            @pl.when(g * views + i != me)
            def _(i=i, c=c):
                out_copy(c, 0, g, i).wait_recv()

    for c in range(NOUT):
        for w in range(views):
            @pl.when((w != v) | (band != g))
            def _(w=w, c=c):
                out_copy(c, w, band, idx).wait_send()


def on_device(dims, camera, background, destination, offsets, shift_frac, psf_taps):
    slabs, views, bands = dims
    blocks, planes, rows, cols = camera.shape[1:]
    taps = psf_taps.shape[-1]
    margin = taps // 2
    tall = CZ * rows + CZ
    strip = rows // views
    wide = strip + 2 * HALO
    tap_rows = -(-3 * (taps + 1) // 8) * 8
    vmem = pl.BlockSpec(memory_space=pltpu.VMEM)
    hbm = functools.partial(pltpu.with_memory_space_constraint, memory_space=pltpu.HBM)
    cell = 4 * cols
    room = 2 * 1024 * 1024
    acc, tap_rows_all = pl.pallas_call(
        functools.partial(deposit_kernel, rows),
        in_specs=[pl.BlockSpec(memory_space=pltpu.HBM)] * 6,
        out_specs=(vmem, vmem),
        out_shape=(
            pltpu.VMEM((slabs, tall, cols), jnp.float32),
            pltpu.VMEM((tap_rows, cols), jnp.float32),
        ),
        scratch_shapes=[
            pltpu.SMEM((blocks,), jnp.int32),
            pltpu.SMEM((blocks,), jnp.int32),
            pltpu.SMEM((1, 1, 1), jnp.int32),
            pltpu.SMEM((3,), jnp.float32),
            pltpu.VMEM((3, 1, taps), jnp.float32),
            pltpu.VMEM((blocks, planes, rows, cols), jnp.float32),
            pltpu.SemaphoreType.DMA((blocks // CHUNK,)),
            pltpu.SemaphoreType.DMA((5,)),
        ],
        compiler_params=pltpu.CompilerParams(
            vmem_limit_bytes=cell * (blocks * planes * rows + slabs * tall) + room),
        name="deposit",
    )(hbm(destination.reshape(-1)), hbm(offsets.reshape(-1)), background, hbm(shift_frac[0]),
      hbm(jnp.transpose(psf_taps, (1, 0, 2))), hbm(camera[0]))

    dma = pltpu.SemaphoreType.DMA
    f32 = jnp.float32
    shapes = [
        (slabs, tall, cols), (slabs, tall, cols), (views, tap_rows, cols),
        (views, 3 * CZ, wide, cols), (3 * CZ, wide, cols), (3 * CZ, wide, cols),
    ]
    late = [
        (CZ + 2 * margin, wide, cols),
        (CZ + 2 * margin, strip + 2 * margin, cols), (views, CZ + 2 * margin, strip + 2 * margin, cols),
        (OC, strip, cols), (views, OC, strip, cols), (CZ, strip, cols),
    ]
    total = sum([functools.reduce(lambda a, b: a * b, s) for s in shapes + late])
    total = total + cols * (slabs * tall + 2 * CZ * rows + views * 4 * cols)
    estimate, joined = pl.pallas_call(
        functools.partial(world_kernel, dims, rows, taps),
        in_specs=[vmem, vmem],
        out_specs=(vmem, vmem),
        out_shape=(
            jax.ShapeDtypeStruct((CZ, rows, cols), f32),
            jax.ShapeDtypeStruct((1, CZ, rows, cols), f32),
        ),
        scratch_shapes=[pltpu.VMEM(s, f32) for s in shapes]
        + [pltpu.VMEM((views, 2, 2 * cols, 2 * cols), jnp.bfloat16)]
        + [pltpu.VMEM(s, f32) for s in late]
        + [
            dma((slabs, NCH)), dma((slabs, NCH)), dma((slabs, NCH)), dma((slabs, NCH)),
            dma((views,)), dma((views,)), dma,
            dma((views, NCH)), dma((views, NCH)), dma((NCH,)), dma((views, NCH)), dma((NCH,)), dma((views, NCH)),
            dma((2, views, NCH)), dma((2, views, NCH)), dma((8, NOUT)), dma((8, NOUT)),
            dma((views, NOUT)), dma((views, NOUT)),
        ],
        compiler_params=pltpu.CompilerParams(
            collective_id=0, has_side_effects=True, vmem_limit_bytes=4 * total + room),
        name="world",
    )(acc, tap_rows_all)
    return estimate, joined


def solution(mesh):
    dims = (mesh.shape["gz"], mesh.shape["view"], mesh.shape["gy"])
    return jax.shard_map(
        functools.partial(on_device, dims),
        mesh=mesh,
        in_specs=(
            P("view", ("groups", "gz"), None, "gy", None),
            P("view", "gy", ("groups", "gz")),
            P("view", "gy", ("groups", "gz"), None),
            P("view", "gy", ("groups", "gz")),
            P("view", None),
            P("view", None, None),
        ),
        out_specs=(P(("groups", "gz"), "gy", None), P("view", ("groups", "gz"), "gy", None)),
        check_vma=False,
    )
```

```python
import functools

import jax
import jax.numpy as jnp
from jax import lax
from jax.experimental import pallas as pl
from jax.experimental.pallas import tpu as pltpu
from jax.sharding import PartitionSpec as P

CZ = 8
ITERS = 2
HALO = 8
BAND = 8
CP = 2
NCH = CZ // CP
OC = 4
NOUT = CZ // OC

DATA_FLOOR = 0.25
TINY = 1e-30
MESH = pl.DeviceIdType.MESH


def world_kernel(
    dims, rows, taps,
    dest_in, offs_in, level_in, frac_in, psf_in, cam_ref, est_ref, joined_ref,
    dest, offs, level, frac, psf, cam, acc_ref, tap_in, ru, rd, tap_all, jx, e0, e1, kx, za, zb, rt, yb, part, lg,
    small, cam_sem, us, ur, ds_, dr, tap_s, tap_r, loc_sem, ms, mr, los, lor, his, hir,
    zs, zr, es, er, out_s, out_r,
):
    pairs = ((dest_in, dest), (offs_in, offs), (level_in, level), (frac_in, frac), (psf_in, psf))
    loads = [pltpu.make_async_copy(a, b, small.at[n]) for n, (a, b) in enumerate(pairs)]
    for load in loads:
        load.start()

    def fetch(n):
        at = pl.ds(n * BAND, BAND)
        return pltpu.make_async_copy(cam_ref.at[:, :, at, :], cam.at[:, :, at, :], cam_sem.at[n])

    for n in range(rows // BAND):
        fetch(n).start()

    slabs, views, bands = dims
    strip = rows // views
    wide = strip + 2 * HALO
    margin = taps // 2
    z = lax.axis_index("gz")
    v = lax.axis_index("view")
    g = lax.axis_index("gy")
    strips = views * bands
    me = v * bands + g
    band, idx = me // views, me % views

    def dev(zz, vv, gg):
        return {"gz": zz, "view": vv, "gy": gg}

    def strip_dev(zz, ss):
        return dev(zz, ss // bands, ss % bands)

    below, above = z > 0, z < slabs - 1
    left, right = me > 0, me < strips - 1

    barrier = pltpu.get_barrier_semaphore()

    def greet(target):
        pl.semaphore_signal(barrier, inc=1, device_id=target, device_id_type=MESH)

    amount = strips - 1
    for dz, zok in ((-1, below), (1, above)):
        for ds, sok in ((-1, left), (0, z >= 0), (1, right)):
            ok = zok & sok
            amount = amount + ok.astype(jnp.int32)

            @pl.when(ok)
            def _(dz=dz, ds=ds):
                greet(strip_dev(z + dz, me + ds))

    for d in range(1, strips):
        greet(strip_dev(z, (me + d) % strips))

    for load in loads:
        load.wait()

    blocks, planes = cam.shape[:2]
    tall = acc_ref.shape[1]
    lanes = 4 * blocks
    lane = lax.broadcasted_iota(jnp.int32, (CZ, lanes), 1)
    plane = lax.broadcasted_iota(jnp.int32, (CZ, lanes), 0)
    block, later = lane % blocks, lane // blocks % 2
    first = jnp.zeros((CZ, lanes), jnp.int32)
    for b in range(blocks):
        first = jnp.where(block == b, dest[b] * CZ + offs[b], first)
    lands = [(first + later == plane + s * CZ).astype(jnp.float32) for s in range(slabs)]
    for s in range(slabs):
        hits = jnp.sum(jnp.where(lane < 2 * blocks, lands[s], 0.0), axis=1, keepdims=True)
        acc_ref[s, 0:CZ, :] = jnp.broadcast_to(hits, (CZ, 128))
    lands = jnp.concatenate(lands, axis=0).astype(jnp.bfloat16)

    fz = frac[0]
    base = level[0, 0, 0].astype(jnp.float32)
    flat = cam.reshape(blocks * planes * rows, 128)
    out = acc_ref.reshape(slabs * tall, 128)

    def row_planes(r):
        at = [flat[pl.ds(k * rows + r, blocks, stride=planes * rows), :] for k in range(planes)]
        mixed = [(1.0 - fz) * at[k] + (fz * at[k + 1] - base) for k in range(planes - 1)]
        top = [m.astype(jnp.bfloat16) for m in mixed]
        rest = [(m - t.astype(jnp.float32)).astype(jnp.bfloat16) for m, t in zip(mixed, top)]
        return jnp.concatenate(top + rest, axis=0)

    @pl.loop(0, rows // BAND)
    def _(n):
        fetch(n).wait()
        for j in range(0, BAND, 2):
            r = n * BAND + j
            both = jnp.concatenate([row_planes(r), row_planes(r + 1)], axis=1)
            sums = jnp.dot(lands, both, preferred_element_type=jnp.float32)
            for s in range(slabs):
                for i in range(2):
                    at = pl.ds(s * tall + CZ + r + i, CZ, stride=rows)
                    out[at, :] = sums[s * CZ : (s + 1) * CZ, i * 128 : (i + 1) * 128]

    def clear(ref, planes, lo, hi):
        @pl.loop(planes[0], planes[1])
        def _(p):
            ref[p, lo:hi, :] = jnp.zeros((hi - lo, 128), jnp.float32)

    for edge, flow, halo in ((z == 0, ru, (0, CZ)), (z == slabs - 1, rd, (2 * CZ, 3 * CZ))):
        @pl.when(edge)
        def _(flow=flow, halo=halo):
            flow[z] = jnp.zeros(flow.shape[1:], jnp.float32)
            for ref in [e0, e1] + [jx.at[w] for w in range(views)]:
                clear(ref, halo, 0, wide)

    for edge, lo, hi in ((me == 0, 0, HALO), (me == strips - 1, HALO + strip, wide)):
        @pl.when(edge)
        def _(lo=lo, hi=hi):
            clear(e1, (0, 3 * CZ), lo, hi)
            for w in range(views):
                clear(jx.at[w], (CZ, 2 * CZ), lo, hi)

    pl.semaphore_wait(barrier, amount)

    def span(c):
        start = 0 if c == 0 else CZ + c * CP * rows
        return pl.ds(start, CZ + (c + 1) * CP * rows - start)

    def up_copy(src, t, c):
        return pltpu.make_async_remote_copy(
            src_ref=src.at[t, span(c)], dst_ref=ru.at[t, span(c)], send_sem=us.at[t, c],
            recv_sem=ur.at[t, c], device_id={"gz": z + 1}, device_id_type=MESH)

    def down_copy(src, t, c):
        return pltpu.make_async_remote_copy(
            src_ref=src.at[t, span(c)], dst_ref=rd.at[t, span(c)], send_sem=ds_.at[t, c],
            recv_sem=dr.at[t, c], device_id={"gz": z - 1}, device_id_type=MESH)

    @pl.when(z == 0)
    def _():
        @pl.loop(0, slabs - 1)
        def _(k):
            for c in range(NCH):
                up_copy(acc_ref, slabs - 1 - k, c).start()

    @pl.when(z == slabs - 1)
    def _():
        @pl.loop(0, slabs - 1)
        def _(k):
            for c in range(NCH):
                down_copy(acc_ref, k, c).start()

    for axis in range(3):
        scale = jnp.sum(psf[axis], axis=1, keepdims=True)
        share = psf[axis] / scale
        for t in range(taps):
            at = axis * taps + t
            tap_in[at : at + 1, :] = jnp.broadcast_to(share[:, t : t + 1], (1, 128))

    own_tap = pltpu.make_async_copy(tap_in, tap_all.at[v], loc_sem)
    own_tap.start()

    def tap_copy(d):
        return pltpu.make_async_remote_copy(
            src_ref=tap_in, dst_ref=tap_all.at[v], send_sem=tap_s.at[d - 1],
            recv_sem=tap_r.at[d - 1], device_id={"view": (v + d) % views}, device_id_type=MESH)

    for d in range(1, views):
        tap_copy(d).start()

    def pass_on(copy, ref, t, ok):
        @pl.when(ok)
        def _():
            for c in range(NCH):
                at = span(c)
                copy(ref, t, c).wait_recv()
                ref[t, at] = ref[t, at] + acc_ref[t, at]
                copy(ref, t, c).start()

    def pass_up(k):
        t = slabs - 1 - k
        pass_on(up_copy, ru, t, below & (t > z))

    def pass_down(k):
        pass_on(down_copy, rd, k, above & (k < z))

    @pl.loop(0, slabs - 1)
    def _(k):
        low = 2 * z < slabs

        @pl.when(low)
        def _():
            pass_up(k)
            pass_down(k)

        @pl.when(jnp.logical_not(low))
        def _():
            pass_down(k)
            pass_up(k)

    own_tap.wait()
    for d in range(1, views):
        tap_copy(d).wait()

    apart = lax.broadcasted_iota(jnp.int32, (128, 128), 0) - lax.broadcasted_iota(jnp.int32, (128, 128), 1)

    @pl.loop(0, views)
    def _(w):
        ahead = jnp.zeros((128, 128), jnp.float32)
        back = jnp.zeros((128, 128), jnp.float32)
        for t in range(taps):
            tap = tap_all[w, 2 * taps + t : 2 * taps + t + 1, :]
            ahead = jnp.where(apart == t - margin, tap, ahead)
            back = jnp.where(apart == margin - t, tap, back)
        for n, full in enumerate((ahead, back)):
            top = full.astype(jnp.bfloat16)
            kx[w, n, 0:128, 0:128] = top
            kx[w, n, 128:256, 0:128] = top
            kx[w, n, 0:128, 128:256] = (full - top.astype(jnp.float32)).astype(jnp.bfloat16)
            kx[w, n, 128:256, 128:256] = jnp.zeros((128, 128), jnp.bfloat16)

    fy, fx = frac[1], frac[2]
    last_row = lax.broadcasted_iota(jnp.int32, (rows, 128), 0) == rows - 1
    last_col = lax.broadcasted_iota(jnp.int32, (rows, 128), 1) == 127
    joined = joined_ref.at[0]
    mid = pl.ds(CZ, CZ)

    def planes_of(c):
        return pl.ds(c * CP, CP), pl.ds(CZ + c * CP, CP)

    def piece(i):
        lo, hi = max(i * strip - HALO, 0), min((i + 1) * strip + HALO, rows)
        return (lo, hi), (lo - i * strip + HALO, hi - i * strip + HALO)

    low_edge = ((rows - HALO, rows), (0, HALO))
    high_edge = ((0, HALO), (HALO + strip, wide))

    def part_copy(c, w, rows_of, target, send, recv):
        src_p, dst_p = planes_of(c)
        (lo, hi), (dlo, dhi) = rows_of
        return pltpu.make_async_remote_copy(
            src_ref=joined.at[src_p, pl.ds(lo, hi - lo), :], dst_ref=jx.at[w, dst_p, pl.ds(dlo, dhi - dlo), :],
            send_sem=send, recv_sem=recv, device_id=strip_dev(z, target), device_id_type=MESH)

    def sends(c):
        out = []
        for i in range(views):
            out.append((g * views + i, z >= 0, piece(i), ms.at[i, c], mr.at[v, c]))
        out.append(((g + 1) * views, g < bands - 1, low_edge, los.at[c], lor.at[v, c]))
        out.append((g * views - 1, g > 0, high_edge, his.at[c], hir.at[v, c]))
        return out

    def join(c):
        src_p, _ = planes_of(c)

        @pl.when(below)
        def _():
            up_copy(acc_ref, z, c).wait_recv()

        @pl.when(above)
        def _():
            down_copy(acc_ref, z, c).wait_recv()

        for p in range(c * CP, (c + 1) * CP):
            at = pl.ds(CZ + p * rows, rows)
            total = acc_ref[z, at, :] + ru[z, at, :] + rd[z, at, :]
            cnt = pl.ds(p, 1)
            covered = acc_ref[z, cnt, :] + ru[z, cnt, :] + rd[z, cnt, :]
            follow = jnp.where(last_row, total, pltpu.roll(total, rows - 1, 0))
            total = (1.0 - fy) * total + fy * follow
            follow = jnp.where(last_col, total, pltpu.roll(total, 127, 1))
            total = (1.0 - fx) * total + fx * follow
            joined_ref[0, p] = jnp.maximum(total / (covered + 1.0), DATA_FLOOR)
        for target, ok, rows_of, send, recv in sends(c):
            (lo, hi), (dlo, dhi) = rows_of

            @pl.when(ok & (target != me))
            def _(rows_of=rows_of, target=target, send=send, recv=recv):
                part_copy(c, v, rows_of, target, send, recv).start()

            @pl.when(ok & (target == me))
            def _(lo=lo, hi=hi, dlo=dlo, dhi=dhi):
                for p in range(c * CP, (c + 1) * CP):
                    jx[v, CZ + p, dlo:dhi, :] = joined_ref[0, p, lo:hi, :]

    def z_copy(ref, w, c, up, send, recv):
        dst = (0 if up else 2 * CZ) + c * CP
        src = CZ + c * CP
        a, b = ref.at[pl.ds(src, CP)], ref.at[pl.ds(dst, CP)]
        return pltpu.make_async_remote_copy(
            src_ref=a, dst_ref=b, send_sem=send, recv_sem=recv,
            device_id={"gz": z + 1 if up else z - 1}, device_id_type=MESH)

    def z_copies(c, up):
        side = 1 if up else 0
        near = c * CP >= CZ - margin if up else c * CP < margin
        if near:
            return [z_copy(jx.at[w], w, c, up, zs.at[side, w, c], zr.at[side, w, c]) for w in range(views)]
        return [z_copy(e0, 0, c, up, zs.at[side, 0, c], zr.at[side, 0, c])]

    def average(p):
        total = jx[0, p]
        for w in range(1, views):
            total = total + jx[w, p]
        e0[p] = total / views

    def spread(c):
        for w in range(views):
            for i in range(views):
                @pl.when((idx == i) & ((w != v) | (band != g)))
                def _(i=i, w=w):
                    part_copy(c, w, piece(i), me, ms.at[i, c], mr.at[w, c]).wait_recv()

            @pl.when((idx == 0) & (band > 0) & ((w != v) | (band - 1 != g)))
            def _(w=w):
                part_copy(c, w, low_edge, me, los.at[c], lor.at[w, c]).wait_recv()

            @pl.when((idx == views - 1) & (band < bands - 1) & ((w != v) | (band + 1 != g)))
            def _(w=w):
                part_copy(c, w, high_edge, me, his.at[c], hir.at[w, c]).wait_recv()

        for p in range(c * CP, (c + 1) * CP):
            average(CZ + p)
        for up, ok in ((True, above), (False, below)):
            @pl.when(ok)
            def _(up=up):
                for copy in z_copies(c, up):
                    copy.start()

    join(0)
    for c in range(1, NCH):
        join(c)
        spread(c - 1)
    spread(NCH - 1)

    for c in range(NCH):
        for up, ok in ((True, below), (False, above)):
            @pl.when(ok)
            def _(up=up, c=c):
                copies = z_copies(c, up)
                for copy in copies:
                    copy.wait_recv()
                if len(copies) == views and views > 1:
                    for p in range(c * CP, (c + 1) * CP):
                        average((0 if up else 2 * CZ) + p)

    planes_r = CZ + 2 * margin
    rows_r = strip + 2 * margin

    def along_x(u, w, n):
        top = u.astype(jnp.bfloat16)
        rest = (u - top.astype(jnp.float32)).astype(jnp.bfloat16)
        both = jnp.dot(jnp.concatenate([top, rest], axis=1), kx[w, n], preferred_element_type=jnp.float32)
        return both[:, 0:128] + both[:, 128:256]

    def weighted(terms, weights):
        total = weights[0] * terms[0]
        for term, weight in zip(terms[1:], weights[1:]):
            total = total + weight * term
        return total

    def root(terms):
        if len(terms) == 1:
            return terms[0]
        if len(terms) % 2:
            total = jnp.log(terms[0])
            for term in terms[1:]:
                total = total + jnp.log(term)
            return jnp.exp(total / len(terms))
        return root([jnp.sqrt(a * b) for a, b in zip(terms[0::2], terms[1::2])])

    def correct(est, emit):
        for w in range(views):
            def tap(axis, t, w=w):
                at = axis * taps + t
                return tap_all[w, at : at + 1, :]

            @pl.loop(0, wide // 8, unroll=2)
            def _(r):
                at = pl.ds(pl.multiple_of(r * 8, 8), 8)
                column = [est[CZ - 2 * margin + p, at, :] for p in range(planes_r + 2 * margin)]
                for p in range(planes_r):
                    za[p, at, :] = weighted(column[p : p + taps], [tap(0, t) for t in range(taps)])

            @pl.loop(0, planes_r, unroll=4)
            def _(p):
                base = HALO - 2 * margin
                zb[p] = weighted([za[p, base + t : base + t + rows_r, :] for t in range(taps)],
                                 [tap(1, t) for t in range(taps)])

            @pl.loop(0, planes_r // 4)
            def _(c):
                at = pl.ds(c * 4, 4)
                blurred = along_x(zb[at].reshape(4 * rows_r, 128), w, 0).reshape(4, rows_r, 128)
                data = jx[w, pl.ds(c * 4 + CZ - margin, 4), HALO - margin : HALO - margin + rows_r, :]
                blurred = jnp.maximum(blurred, TINY)
                inverse = pl.reciprocal(blurred, approx=True)
                inverse = inverse * (2.0 - blurred * inverse)
                rt[w, at] = data * inverse

        for c in range(NOUT):
            for w in range(views):
                def tap(axis, t, w=w):
                    at = axis * taps + taps - 1 - t
                    return tap_all[w, at : at + 1, :]

                for r in range(rows_r // 8):
                    at = pl.ds(r * 8, 8)
                    column = [rt[w, c * OC + p, at, :] for p in range(OC + 2 * margin)]
                    for p in range(OC):
                        za[p, at, :] = weighted(column[p : p + taps], [tap(0, t) for t in range(taps)])
                for p in range(OC):
                    yb[p] = weighted([za[p, t : t + strip, :] for t in range(taps)], [tap(1, t) for t in range(taps)])
                part[w] = along_x(yb[...].reshape(OC * strip, 128), w, 1).reshape(OC, strip, 128)
            emit(c, est[pl.ds(CZ + c * OC, OC), HALO : HALO + strip, :] * root([part[w] for w in range(views)]))

    inner = pl.ds(HALO, strip)
    near = []
    for n, (dz, ds) in enumerate([(a, b) for a in (-1, 1, 0) for b in (0, -1, 1) if a or b]):
        zok = {-1: below, 0: z >= 0, 1: above}[dz]
        sok = {-1: left, 0: z >= 0, 1: right}[ds]
        far_z = {-1: above, 0: z >= 0, 1: below}[dz]
        far_s = {-1: right, 0: z >= 0, 1: left}[ds]
        near.append((n, dz, ds, zok & sok, far_z & far_s))

    def near_copy(n, dz, ds, c):
        src_r = {-1: pl.ds(HALO, HALO), 0: inner, 1: pl.ds(strip, HALO)}[ds]
        dst_r = {-1: pl.ds(HALO + strip, HALO), 0: inner, 1: pl.ds(0, HALO)}[ds]
        dst = {-1: 2 * CZ, 0: CZ, 1: 0}[dz] + c * OC
        return pltpu.make_async_remote_copy(
            src_ref=e1.at[pl.ds(CZ + c * OC, OC), src_r, :], dst_ref=e1.at[pl.ds(dst, OC), dst_r, :],
            send_sem=es.at[n, c], recv_sem=er.at[n, c], device_id=strip_dev(z + dz, me + ds), device_id_type=MESH)

    def emit_step(c, new):
        e1[pl.ds(CZ + c * OC, OC), HALO : HALO + strip, :] = new
        for n, dz, ds, ok, _ in near:
            @pl.when(ok)
            def _(n=n, dz=dz, ds=ds):
                near_copy(n, dz, ds, c).start()

    correct(e0, emit_step)

    @pl.loop(0, slabs)
    def _(t):
        for c in range(NCH):
            @pl.when(t > z)
            def _():
                up_copy(acc_ref, t, c).wait_send()

            @pl.when(t < z)
            def _():
                down_copy(acc_ref, t, c).wait_send()

    for c in range(NCH):
        for target, ok, rows_of, send, recv in sends(c):
            @pl.when(ok & (target != me))
            def _(rows_of=rows_of, target=target, send=send, recv=recv, c=c):
                part_copy(c, v, rows_of, target, send, recv).wait_send()

        for up, ok in ((True, above), (False, below)):
            @pl.when(ok)
            def _(up=up, c=c):
                for copy in z_copies(c, up):
                    copy.wait_send()

    for c in range(NOUT):
        for n, dz, ds, _, ok in near:
            @pl.when(ok)
            def _(n=n, dz=dz, ds=ds, c=c):
                near_copy(n, dz, ds, c).wait_recv()

    def out_copy(c, w, target_g, i):
        at = pl.ds(pl.multiple_of(i * strip, 8), strip)
        part = pl.ds(c * OC, OC)
        return pltpu.make_async_remote_copy(
            src_ref=lg.at[part], dst_ref=est_ref.at[part, at, :], send_sem=out_s.at[w, c],
            recv_sem=out_r.at[i, c], device_id=dev(z, w, target_g), device_id_type=MESH)

    def emit_last(c, new):
        lg[pl.ds(c * OC, OC)] = new
        for w in range(views):
            away = (w != v) | (band != g)

            @pl.when(away)
            def _(w=w):
                out_copy(c, w, band, idx).start()

            @pl.when(jnp.logical_not(away))
            def _():
                est_ref[pl.ds(c * OC, OC), pl.ds(pl.multiple_of(idx * strip, 8), strip), :] = new

    correct(e1, emit_last)

    for c in range(NOUT):
        for n, dz, ds, ok, _ in near:
            @pl.when(ok)
            def _(n=n, dz=dz, ds=ds, c=c):
                near_copy(n, dz, ds, c).wait_send()

    for c in range(NOUT):
        for i in range(views):
            @pl.when(g * views + i != me)
            def _(i=i, c=c):
                out_copy(c, 0, g, i).wait_recv()

    for c in range(NOUT):
        for w in range(views):
            @pl.when((w != v) | (band != g))
            def _(w=w, c=c):
                out_copy(c, w, band, idx).wait_send()


def store_kernel(est_in, joined_in, est_out, joined_out, sems):
    copies = [pltpu.make_async_copy(a, b, sems.at[n]) for n, (a, b) in enumerate(((est_in, est_out), (joined_in, joined_out)))]
    for copy in copies:
        copy.start()
    for copy in copies:
        copy.wait()


def on_device(dims, camera, background, destination, offsets, shift_frac, psf_taps):
    slabs, views, bands = dims
    blocks, planes, rows, cols = camera.shape[1:]
    taps = psf_taps.shape[-1]
    margin = taps // 2
    tall = CZ * rows + CZ
    strip = rows // views
    wide = strip + 2 * HALO
    tap_rows = -(-3 * taps // 8) * 8
    vmem = pl.BlockSpec(memory_space=pltpu.VMEM)
    hbm = functools.partial(pltpu.with_memory_space_constraint, memory_space=pltpu.HBM)
    room = 2 * 1024 * 1024
    dma = pltpu.SemaphoreType.DMA
    f32 = jnp.float32
    shapes = [
        (blocks, planes, rows, cols), (slabs, tall, cols), (tap_rows, cols),
        (slabs, tall, cols), (slabs, tall, cols), (views, tap_rows, cols),
        (views, 3 * CZ, wide, cols), (3 * CZ, wide, cols), (3 * CZ, wide, cols),
    ]
    late = [
        (CZ + 2 * margin, wide, cols),
        (CZ + 2 * margin, strip + 2 * margin, cols), (views, CZ + 2 * margin, strip + 2 * margin, cols),
        (OC, strip, cols), (views, OC, strip, cols), (CZ, strip, cols),
    ]
    total = sum([functools.reduce(lambda a, b: a * b, s) for s in shapes + late])
    total = total + cols * (2 * CZ * rows + views * 4 * cols)
    estimate, joined = pl.pallas_call(
        functools.partial(world_kernel, dims, rows, taps),
        in_specs=[pl.BlockSpec(memory_space=pltpu.HBM)] * 6,
        out_specs=(vmem, vmem),
        out_shape=(
            pltpu.VMEM((CZ, rows, cols), f32),
            pltpu.VMEM((1, CZ, rows, cols), f32),
        ),
        scratch_shapes=[
            pltpu.SMEM((blocks,), jnp.int32), pltpu.SMEM((blocks,), jnp.int32),
            pltpu.SMEM((1, 1, 1), jnp.int32), pltpu.SMEM((3,), f32), pltpu.VMEM((3, 1, taps), f32),
        ]
        + [pltpu.VMEM(s, f32) for s in shapes]
        + [pltpu.VMEM((views, 2, 2 * cols, 2 * cols), jnp.bfloat16)]
        + [pltpu.VMEM(s, f32) for s in late]
        + [
            dma((5,)), dma((rows // BAND,)),
            dma((slabs, NCH)), dma((slabs, NCH)), dma((slabs, NCH)), dma((slabs, NCH)),
            dma((views,)), dma((views,)), dma,
            dma((views, NCH)), dma((views, NCH)), dma((NCH,)), dma((views, NCH)), dma((NCH,)), dma((views, NCH)),
            dma((2, views, NCH)), dma((2, views, NCH)), dma((8, NOUT)), dma((8, NOUT)),
            dma((views, NOUT)), dma((views, NOUT)),
        ],
        compiler_params=pltpu.CompilerParams(
            collective_id=0, has_side_effects=True, vmem_limit_bytes=4 * total + room),
        name="world",
    )(hbm(destination.reshape(-1)), hbm(offsets.reshape(-1)), background, hbm(shift_frac[0]),
      hbm(jnp.transpose(psf_taps, (1, 0, 2))), hbm(camera[0]))
    return pl.pallas_call(
        store_kernel,
        in_specs=[vmem, vmem],
        out_specs=(pl.BlockSpec(memory_space=pltpu.HBM), pl.BlockSpec(memory_space=pltpu.HBM)),
        out_shape=(jax.ShapeDtypeStruct(estimate.shape, f32), jax.ShapeDtypeStruct(joined.shape, f32)),
        scratch_shapes=[dma((2,))],
        name="store",
    )(pltpu.with_memory_space_constraint(estimate, pltpu.VMEM), pltpu.with_memory_space_constraint(joined, pltpu.VMEM))


def solution(mesh):
    dims = (mesh.shape["gz"], mesh.shape["view"], mesh.shape["gy"])
    return jax.shard_map(
        functools.partial(on_device, dims),
        mesh=mesh,
        in_specs=(
            P("view", ("groups", "gz"), None, "gy", None),
            P("view", "gy", ("groups", "gz")),
            P("view", "gy", ("groups", "gz"), None),
            P("view", "gy", ("groups", "gz")),
            P("view", None),
            P("view", None, None),
        ),
        out_specs=(P(("groups", "gz"), "gy", None), P("view", ("groups", "gz"), "gy", None)),
        check_vma=False,
    )
```

```python
import functools

import jax
import jax.numpy as jnp
from jax import lax
from jax.experimental import pallas as pl
from jax.experimental.pallas import tpu as pltpu
from jax.sharding import PartitionSpec as P

CZ = 8
ITERS = 2
HALO = 8
CHUNK = 4
CP = 2
NCH = CZ // CP
OC = 4
NOUT = CZ // OC

DATA_FLOOR = 0.25
TINY = 1e-30
MESH = pl.DeviceIdType.MESH


def deposit_kernel(
    rows, dest_in, offs_in, level_in, frac_in, psf_in, cam_ref, acc_ref, tap_ref,
    dest, offs, level, frac, psf, cam, sems, small,
):
    taps = psf.shape[2]
    blocks, planes = cam_ref.shape[:2]
    pairs = ((dest_in, dest), (offs_in, offs), (level_in, level), (frac_in, frac), (psf_in, psf))
    copies = [pltpu.make_async_copy(a, b, small.at[n]) for n, (a, b) in enumerate(pairs)]
    for copy in copies:
        copy.start()

    def fetch(c):
        at = pl.ds(c * CHUNK, CHUNK)
        return pltpu.make_async_copy(cam_ref.at[at], cam.at[at], sems.at[c])

    for c in range(blocks // CHUNK):
        fetch(c).start()

    @pl.loop(0, acc_ref.shape[0])
    def _(s):
        acc_ref[s] = jnp.zeros(acc_ref.shape[1:], jnp.float32)

    for copy in copies:
        copy.wait()

    tap_ref[...] = jnp.zeros(tap_ref.shape, jnp.float32)
    for axis in range(3):
        scale = jnp.sum(psf[axis], axis=1, keepdims=True)
        share = psf[axis] / scale
        for t in range(taps):
            at = axis * taps + t
            tap_ref[at : at + 1, :] = jnp.broadcast_to(share[:, t : t + 1], (1, 128))
        at = 3 * taps + axis
        tap_ref[at : at + 1, :] = jnp.zeros((1, 128), jnp.float32) + frac[axis]

    fz = frac[0]
    base = level[0, 0, 0].astype(jnp.float32)

    @pl.loop(0, blocks // CHUNK)
    def _(c):
        fetch(c).wait()
        for i in range(CHUNK):
            b = c * CHUNK + i
            s = dest[b]
            o = offs[b]
            lower = cam[b, 0] - base
            for k in range(planes - 1):
                upper = cam[b, k + 1] - base
                at = pl.ds(pl.multiple_of(CZ + (o + k) * rows, 8), rows)
                acc_ref[s, at, :] = acc_ref[s, at, :] + ((1.0 - fz) * lower + fz * upper)
                cnt = pl.ds(o + k, 1)
                acc_ref[s, cnt, :] = acc_ref[s, cnt, :] + 1.0
                lower = upper


def world_kernel(
    dims, rows, taps,
    acc_ref, tap_in, est_ref, joined_ref,
    ru, rd, tap_all, jx, e0, e1, kx, za, zb, rt, yb, part, lg,
    us, ur, ds_, dr, tap_s, tap_r, loc_sem, ms, mr, los, lor, his, hir,
    zs, zr, es, er, out_s, out_r,
):
    slabs, views, bands = dims
    strip = rows // views
    wide = strip + 2 * HALO
    margin = taps // 2
    z = lax.axis_index("gz")
    v = lax.axis_index("view")
    g = lax.axis_index("gy")
    strips = views * bands
    me = v * bands + g
    band, idx = me // views, me % views

    def dev(zz, vv, gg):
        return {"gz": zz, "view": vv, "gy": gg}

    def strip_dev(zz, ss):
        return dev(zz, ss // bands, ss % bands)

    below, above = z > 0, z < slabs - 1
    left, right = me > 0, me < strips - 1

    barrier = pltpu.get_barrier_semaphore()

    def greet(target):
        pl.semaphore_signal(barrier, inc=1, device_id=target, device_id_type=MESH)

    amount = strips - 1 + below.astype(jnp.int32) + above.astype(jnp.int32)
    for dz, ok in ((1, above), (-1, below)):
        @pl.when(ok)
        def _(dz=dz):
            greet(dev(z + dz, v, g))

    for d in range(1, strips):
        greet(strip_dev(z, (me + d) % strips))

    def clear(ref, planes, lo, hi):
        @pl.loop(planes[0], planes[1])
        def _(p):
            ref[p, lo:hi, :] = jnp.zeros((hi - lo, 128), jnp.float32)

    pl.semaphore_wait(barrier, amount)

    def span(c):
        start = 0 if c == 0 else CZ + c * CP * rows
        return pl.ds(start, CZ + (c + 1) * CP * rows - start)

    def up_copy(src, t, c):
        return pltpu.make_async_remote_copy(
            src_ref=src.at[t, span(c)], dst_ref=ru.at[t, span(c)], send_sem=us.at[t, c],
            recv_sem=ur.at[t, c], device_id={"gz": z + 1}, device_id_type=MESH)

    def down_copy(src, t, c):
        return pltpu.make_async_remote_copy(
            src_ref=src.at[t, span(c)], dst_ref=rd.at[t, span(c)], send_sem=ds_.at[t, c],
            recv_sem=dr.at[t, c], device_id={"gz": z - 1}, device_id_type=MESH)

    @pl.when(z == 0)
    def _():
        @pl.loop(0, slabs - 1)
        def _(k):
            for c in range(NCH):
                up_copy(acc_ref, slabs - 1 - k, c).start()

    @pl.when(z == slabs - 1)
    def _():
        @pl.loop(0, slabs - 1)
        def _(k):
            for c in range(NCH):
                down_copy(acc_ref, k, c).start()

    for edge, flow, halo in ((z == 0, ru, (0, CZ)), (z == slabs - 1, rd, (2 * CZ, 3 * CZ))):
        @pl.when(edge)
        def _(flow=flow, halo=halo):
            flow[z] = jnp.zeros(flow.shape[1:], jnp.float32)
            for ref in [e0, e1] + [jx.at[w] for w in range(views)]:
                clear(ref, halo, 0, wide)

    for edge, lo, hi in ((me == 0, 0, HALO), (me == strips - 1, HALO + strip, wide)):
        @pl.when(edge)
        def _(lo=lo, hi=hi):
            clear(e1, (0, 3 * CZ), lo, hi)
            for w in range(views):
                clear(jx.at[w], (CZ, 2 * CZ), lo, hi)

    own_tap = pltpu.make_async_copy(tap_in, tap_all.at[v], loc_sem)
    own_tap.start()

    def tap_copy(d):
        return pltpu.make_async_remote_copy(
            src_ref=tap_in, dst_ref=tap_all.at[v], send_sem=tap_s.at[d - 1],
            recv_sem=tap_r.at[d - 1], device_id={"view": (v + d) % views}, device_id_type=MESH)

    for d in range(1, views):
        tap_copy(d).start()

    def pass_on(copy, ref, t, ok):
        @pl.when(ok)
        def _():
            for c in range(NCH):
                at = span(c)
                copy(ref, t, c).wait_recv()
                ref[t, at] = ref[t, at] + acc_ref[t, at]
                copy(ref, t, c).start()

    def pass_up(k):
        t = slabs - 1 - k
        pass_on(up_copy, ru, t, below & (t > z))

    def pass_down(k):
        pass_on(down_copy, rd, k, above & (k < z))

    @pl.loop(0, slabs - 1)
    def _(k):
        low = 2 * z < slabs

        @pl.when(low)
        def _():
            pass_up(k)
            pass_down(k)

        @pl.when(jnp.logical_not(low))
        def _():
            pass_down(k)
            pass_up(k)

    own_tap.wait()
    for d in range(1, views):
        tap_copy(d).wait()

    apart = lax.broadcasted_iota(jnp.int32, (128, 128), 0) - lax.broadcasted_iota(jnp.int32, (128, 128), 1)

    @pl.loop(0, views)
    def _(w):
        ahead = jnp.zeros((128, 128), jnp.float32)
        back = jnp.zeros((128, 128), jnp.float32)
        for t in range(taps):
            tap = tap_all[w, 2 * taps + t : 2 * taps + t + 1, :]
            ahead = jnp.where(apart == t - margin, tap, ahead)
            back = jnp.where(apart == margin - t, tap, back)
        for n, full in enumerate((ahead, back)):
            top = full.astype(jnp.bfloat16)
            kx[w, n, 0:128, 0:128] = top
            kx[w, n, 128:256, 0:128] = top
            kx[w, n, 0:128, 128:256] = (full - top.astype(jnp.float32)).astype(jnp.bfloat16)
            kx[w, n, 128:256, 128:256] = jnp.zeros((128, 128), jnp.bfloat16)

    fy, fx = [tap_in[3 * taps + n : 3 * taps + n + 1, :] for n in (1, 2)]
    last_row = lax.broadcasted_iota(jnp.int32, (rows, 128), 0) == rows - 1
    last_col = lax.broadcasted_iota(jnp.int32, (rows, 128), 1) == 127
    joined = joined_ref.at[0]
    mid = pl.ds(CZ, CZ)

    def planes_of(c):
        return pl.ds(c * CP, CP), pl.ds(CZ + c * CP, CP)

    def piece(i):
        lo, hi = max(i * strip - HALO, 0), min((i + 1) * strip + HALO, rows)
        return (lo, hi), (lo - i * strip + HALO, hi - i * strip + HALO)

    low_edge = ((rows - HALO, rows), (0, HALO))
    high_edge = ((0, HALO), (HALO + strip, wide))

    def part_copy(c, w, rows_of, target, send, recv):
        src_p, dst_p = planes_of(c)
        (lo, hi), (dlo, dhi) = rows_of
        return pltpu.make_async_remote_copy(
            src_ref=joined.at[src_p, pl.ds(lo, hi - lo), :], dst_ref=jx.at[w, dst_p, pl.ds(dlo, dhi - dlo), :],
            send_sem=send, recv_sem=recv, device_id=strip_dev(z, target), device_id_type=MESH)

    def sends(c):
        out = []
        for i in range(views):
            out.append((g * views + i, z >= 0, piece(i), ms.at[i, c], mr.at[v, c]))
        out.append(((g + 1) * views, g < bands - 1, low_edge, los.at[c], lor.at[v, c]))
        out.append((g * views - 1, g > 0, high_edge, his.at[c], hir.at[v, c]))
        return out

    def join(c):
        src_p, _ = planes_of(c)

        @pl.when(below)
        def _():
            up_copy(acc_ref, z, c).wait_recv()

        @pl.when(above)
        def _():
            down_copy(acc_ref, z, c).wait_recv()

        for p in range(c * CP, (c + 1) * CP):
            at = pl.ds(CZ + p * rows, rows)
            total = acc_ref[z, at, :] + ru[z, at, :] + rd[z, at, :]
            cnt = pl.ds(p, 1)
            covered = acc_ref[z, cnt, :] + ru[z, cnt, :] + rd[z, cnt, :]
            follow = jnp.where(last_row, total, pltpu.roll(total, rows - 1, 0))
            total = (1.0 - fy) * total + fy * follow
            follow = jnp.where(last_col, total, pltpu.roll(total, 127, 1))
            total = (1.0 - fx) * total + fx * follow
            joined_ref[0, p] = jnp.maximum(total / (covered + 1.0), DATA_FLOOR)
        for target, ok, rows_of, send, recv in sends(c):
            (lo, hi), (dlo, dhi) = rows_of

            @pl.when(ok & (target != me))
            def _(rows_of=rows_of, target=target, send=send, recv=recv):
                part_copy(c, v, rows_of, target, send, recv).start()

            @pl.when(ok & (target == me))
            def _(lo=lo, hi=hi, dlo=dlo, dhi=dhi):
                for p in range(c * CP, (c + 1) * CP):
                    jx[v, CZ + p, dlo:dhi, :] = joined_ref[0, p, lo:hi, :]

    def z_copy(ref, w, c, up, send, recv):
        dst = (0 if up else 2 * CZ) + c * CP
        src = CZ + c * CP
        a, b = ref.at[pl.ds(src, CP)], ref.at[pl.ds(dst, CP)]
        return pltpu.make_async_remote_copy(
            src_ref=a, dst_ref=b, send_sem=send, recv_sem=recv,
            device_id={"gz": z + 1 if up else z - 1}, device_id_type=MESH)

    def z_copies(c, up):
        side = 1 if up else 0
        near = c * CP >= CZ - margin if up else c * CP < margin
        if near:
            return [z_copy(jx.at[w], w, c, up, zs.at[side, w, c], zr.at[side, w, c]) for w in range(views)]
        return [z_copy(e0, 0, c, up, zs.at[side, 0, c], zr.at[side, 0, c])]

    def average(p):
        total = jx[0, p]
        for w in range(1, views):
            total = total + jx[w, p]
        e0[p] = total / views

    def spread(c):
        for w in range(views):
            for i in range(views):
                @pl.when((idx == i) & ((w != v) | (band != g)))
                def _(i=i, w=w):
                    part_copy(c, w, piece(i), me, ms.at[i, c], mr.at[w, c]).wait_recv()

            @pl.when((idx == 0) & (band > 0) & ((w != v) | (band - 1 != g)))
            def _(w=w):
                part_copy(c, w, low_edge, me, los.at[c], lor.at[w, c]).wait_recv()

            @pl.when((idx == views - 1) & (band < bands - 1) & ((w != v) | (band + 1 != g)))
            def _(w=w):
                part_copy(c, w, high_edge, me, his.at[c], hir.at[w, c]).wait_recv()

        for p in range(c * CP, (c + 1) * CP):
            average(CZ + p)
        for up, ok in ((True, above), (False, below)):
            @pl.when(ok)
            def _(up=up):
                for copy in z_copies(c, up):
                    copy.start()

    join(0)
    for c in range(1, NCH):
        join(c)
        spread(c - 1)
    spread(NCH - 1)

    for c in range(NCH):
        for up, ok in ((True, below), (False, above)):
            @pl.when(ok)
            def _(up=up, c=c):
                copies = z_copies(c, up)
                for copy in copies:
                    copy.wait_recv()
                if len(copies) == views and views > 1:
                    for p in range(c * CP, (c + 1) * CP):
                        average((0 if up else 2 * CZ) + p)

    planes_r = CZ + 2 * margin
    rows_r = strip + 2 * margin

    def along_x(u, w, n):
        top = u.astype(jnp.bfloat16)
        rest = (u - top.astype(jnp.float32)).astype(jnp.bfloat16)
        both = jnp.dot(jnp.concatenate([top, rest], axis=1), kx[w, n], preferred_element_type=jnp.float32)
        return both[:, 0:128] + both[:, 128:256]

    def weighted(terms, weights):
        total = weights[0] * terms[0]
        for term, weight in zip(terms[1:], weights[1:]):
            total = total + weight * term
        return total

    def root(terms):
        if len(terms) == 1:
            return terms[0]
        if len(terms) % 2:
            total = jnp.log(terms[0])
            for term in terms[1:]:
                total = total + jnp.log(term)
            return jnp.exp(total / len(terms))
        return root([jnp.sqrt(a * b) for a, b in zip(terms[0::2], terms[1::2])])

    def correct(est, emit):
        for w in range(views):
            def tap(axis, t, w=w):
                at = axis * taps + t
                return tap_all[w, at : at + 1, :]

            @pl.loop(0, wide // 8, unroll=2)
            def _(r):
                at = pl.ds(pl.multiple_of(r * 8, 8), 8)
                column = [est[CZ - 2 * margin + p, at, :] for p in range(planes_r + 2 * margin)]
                for p in range(planes_r):
                    za[p, at, :] = weighted(column[p : p + taps], [tap(0, t) for t in range(taps)])

            @pl.loop(0, planes_r, unroll=4)
            def _(p):
                base = HALO - 2 * margin
                zb[p] = weighted([za[p, base + t : base + t + rows_r, :] for t in range(taps)],
                                 [tap(1, t) for t in range(taps)])

            @pl.loop(0, planes_r // 4)
            def _(c):
                at = pl.ds(c * 4, 4)
                blurred = along_x(zb[at].reshape(4 * rows_r, 128), w, 0).reshape(4, rows_r, 128)
                data = jx[w, pl.ds(c * 4 + CZ - margin, 4), HALO - margin : HALO - margin + rows_r, :]
                blurred = jnp.maximum(blurred, TINY)
                inverse = pl.reciprocal(blurred, approx=True)
                inverse = inverse * (2.0 - blurred * inverse)
                rt[w, at] = data * inverse

        for c in range(NOUT):
            for w in range(views):
                def tap(axis, t, w=w):
                    at = axis * taps + taps - 1 - t
                    return tap_all[w, at : at + 1, :]

                for r in range(rows_r // 8):
                    at = pl.ds(r * 8, 8)
                    column = [rt[w, c * OC + p, at, :] for p in range(OC + 2 * margin)]
                    for p in range(OC):
                        za[p, at, :] = weighted(column[p : p + taps], [tap(0, t) for t in range(taps)])
                for p in range(OC):
                    yb[p] = weighted([za[p, t : t + strip, :] for t in range(taps)], [tap(1, t) for t in range(taps)])
                part[w] = along_x(yb[...].reshape(OC * strip, 128), w, 1).reshape(OC, strip, 128)
            emit(c, est[pl.ds(CZ + c * OC, OC), HALO : HALO + strip, :] * root([part[w] for w in range(views)]))

    inner = pl.ds(HALO, strip)
    near = []
    for n, (dz, ds) in enumerate([(a, b) for a in (-1, 1, 0) for b in (0, -1, 1) if a or b]):
        zok = {-1: below, 0: z >= 0, 1: above}[dz]
        sok = {-1: left, 0: z >= 0, 1: right}[ds]
        far_z = {-1: above, 0: z >= 0, 1: below}[dz]
        far_s = {-1: right, 0: z >= 0, 1: left}[ds]
        near.append((n, dz, ds, zok & sok, far_z & far_s))

    def near_copy(n, dz, ds, c):
        src_r = {-1: pl.ds(HALO, HALO), 0: inner, 1: pl.ds(strip, HALO)}[ds]
        dst_r = {-1: pl.ds(HALO + strip, HALO), 0: inner, 1: pl.ds(0, HALO)}[ds]
        dst = {-1: 2 * CZ, 0: CZ, 1: 0}[dz] + c * OC
        return pltpu.make_async_remote_copy(
            src_ref=e1.at[pl.ds(CZ + c * OC, OC), src_r, :], dst_ref=e1.at[pl.ds(dst, OC), dst_r, :],
            send_sem=es.at[n, c], recv_sem=er.at[n, c], device_id=strip_dev(z + dz, me + ds), device_id_type=MESH)

    def emit_step(c, new):
        e1[pl.ds(CZ + c * OC, OC), HALO : HALO + strip, :] = new
        for n, dz, ds, ok, _ in near:
            @pl.when(ok)
            def _(n=n, dz=dz, ds=ds):
                near_copy(n, dz, ds, c).start()

    correct(e0, emit_step)

    @pl.loop(0, slabs)
    def _(t):
        for c in range(NCH):
            @pl.when(t > z)
            def _():
                up_copy(acc_ref, t, c).wait_send()

            @pl.when(t < z)
            def _():
                down_copy(acc_ref, t, c).wait_send()

    for c in range(NCH):
        for target, ok, rows_of, send, recv in sends(c):
            @pl.when(ok & (target != me))
            def _(rows_of=rows_of, target=target, send=send, recv=recv, c=c):
                part_copy(c, v, rows_of, target, send, recv).wait_send()

        for up, ok in ((True, above), (False, below)):
            @pl.when(ok)
            def _(up=up, c=c):
                for copy in z_copies(c, up):
                    copy.wait_send()

    for c in range(NOUT):
        for n, dz, ds, _, ok in near:
            @pl.when(ok)
            def _(n=n, dz=dz, ds=ds, c=c):
                near_copy(n, dz, ds, c).wait_recv()

    def out_copy(c, w, target_g, i):
        at = pl.ds(pl.multiple_of(i * strip, 8), strip)
        part = pl.ds(c * OC, OC)
        return pltpu.make_async_remote_copy(
            src_ref=lg.at[part], dst_ref=est_ref.at[part, at, :], send_sem=out_s.at[w, c],
            recv_sem=out_r.at[i, c], device_id=dev(z, w, target_g), device_id_type=MESH)

    def emit_last(c, new):
        lg[pl.ds(c * OC, OC)] = new
        for w in range(views):
            away = (w != v) | (band != g)

            @pl.when(away)
            def _(w=w):
                out_copy(c, w, band, idx).start()

            @pl.when(jnp.logical_not(away))
            def _():
                est_ref[pl.ds(c * OC, OC), pl.ds(pl.multiple_of(idx * strip, 8), strip), :] = new

    correct(e1, emit_last)

    for c in range(NOUT):
        for n, dz, ds, ok, _ in near:
            @pl.when(ok)
            def _(n=n, dz=dz, ds=ds, c=c):
                near_copy(n, dz, ds, c).wait_send()

    for c in range(NOUT):
        for i in range(views):
            @pl.when(g * views + i != me)
            def _(i=i, c=c):
                out_copy(c, 0, g, i).wait_recv()

    for c in range(NOUT):
        for w in range(views):
            @pl.when((w != v) | (band != g))
            def _(w=w, c=c):
                out_copy(c, w, band, idx).wait_send()


def store_kernel(est_in, joined_in, est_out, joined_out, sems):
    copies = [pltpu.make_async_copy(a, b, sems.at[n]) for n, (a, b) in enumerate(((est_in, est_out), (joined_in, joined_out)))]
    for copy in copies:
        copy.start()
    for copy in copies:
        copy.wait()


def on_device(dims, camera, background, destination, offsets, shift_frac, psf_taps):
    slabs, views, bands = dims
    blocks, planes, rows, cols = camera.shape[1:]
    taps = psf_taps.shape[-1]
    margin = taps // 2
    tall = CZ * rows + CZ
    strip = rows // views
    wide = strip + 2 * HALO
    tap_rows = -(-3 * (taps + 1) // 8) * 8
    vmem = pl.BlockSpec(memory_space=pltpu.VMEM)
    hbm = functools.partial(pltpu.with_memory_space_constraint, memory_space=pltpu.HBM)
    cell = 4 * cols
    room = 2 * 1024 * 1024
    acc, tap_rows_all = pl.pallas_call(
        functools.partial(deposit_kernel, rows),
        in_specs=[pl.BlockSpec(memory_space=pltpu.HBM)] * 6,
        out_specs=(vmem, vmem),
        out_shape=(
            pltpu.VMEM((slabs, tall, cols), jnp.float32),
            pltpu.VMEM((tap_rows, cols), jnp.float32),
        ),
        scratch_shapes=[
            pltpu.SMEM((blocks,), jnp.int32),
            pltpu.SMEM((blocks,), jnp.int32),
            pltpu.SMEM((1, 1, 1), jnp.int32),
            pltpu.SMEM((3,), jnp.float32),
            pltpu.VMEM((3, 1, taps), jnp.float32),
            pltpu.VMEM((blocks, planes, rows, cols), jnp.float32),
            pltpu.SemaphoreType.DMA((blocks // CHUNK,)),
            pltpu.SemaphoreType.DMA((5,)),
        ],
        compiler_params=pltpu.CompilerParams(
            vmem_limit_bytes=cell * (blocks * planes * rows + slabs * tall) + room),
        name="deposit",
    )(hbm(destination.reshape(-1)), hbm(offsets.reshape(-1)), background, hbm(shift_frac[0]),
      hbm(jnp.transpose(psf_taps, (1, 0, 2))), hbm(camera[0]))

    dma = pltpu.SemaphoreType.DMA
    f32 = jnp.float32
    shapes = [
        (slabs, tall, cols), (slabs, tall, cols), (views, tap_rows, cols),
        (views, 3 * CZ, wide, cols), (3 * CZ, wide, cols), (3 * CZ, wide, cols),
    ]
    late = [
        (CZ + 2 * margin, wide, cols),
        (CZ + 2 * margin, strip + 2 * margin, cols), (views, CZ + 2 * margin, strip + 2 * margin, cols),
        (OC, strip, cols), (views, OC, strip, cols), (CZ, strip, cols),
    ]
    total = sum([functools.reduce(lambda a, b: a * b, s) for s in shapes + late])
    total = total + cols * (slabs * tall + 2 * CZ * rows + views * 4 * cols)
    estimate, joined = pl.pallas_call(
        functools.partial(world_kernel, dims, rows, taps),
        in_specs=[vmem, vmem],
        out_specs=(vmem, vmem),
        out_shape=(
            pltpu.VMEM((CZ, rows, cols), f32),
            pltpu.VMEM((1, CZ, rows, cols), f32),
        ),
        scratch_shapes=[pltpu.VMEM(s, f32) for s in shapes]
        + [pltpu.VMEM((views, 2, 2 * cols, 2 * cols), jnp.bfloat16)]
        + [pltpu.VMEM(s, f32) for s in late]
        + [
            dma((slabs, NCH)), dma((slabs, NCH)), dma((slabs, NCH)), dma((slabs, NCH)),
            dma((views,)), dma((views,)), dma,
            dma((views, NCH)), dma((views, NCH)), dma((NCH,)), dma((views, NCH)), dma((NCH,)), dma((views, NCH)),
            dma((2, views, NCH)), dma((2, views, NCH)), dma((8, NOUT)), dma((8, NOUT)),
            dma((views, NOUT)), dma((views, NOUT)),
        ],
        compiler_params=pltpu.CompilerParams(
            collective_id=0, has_side_effects=True, vmem_limit_bytes=4 * total + room),
        name="world",
    )(acc, tap_rows_all)
    return pl.pallas_call(
        store_kernel,
        in_specs=[vmem, vmem],
        out_specs=(pl.BlockSpec(memory_space=pltpu.HBM), pl.BlockSpec(memory_space=pltpu.HBM)),
        out_shape=(jax.ShapeDtypeStruct(estimate.shape, f32), jax.ShapeDtypeStruct(joined.shape, f32)),
        scratch_shapes=[dma((2,))],
        name="store",
    )(pltpu.with_memory_space_constraint(estimate, pltpu.VMEM), pltpu.with_memory_space_constraint(joined, pltpu.VMEM))


def solution(mesh):
    dims = (mesh.shape["gz"], mesh.shape["view"], mesh.shape["gy"])
    return jax.shard_map(
        functools.partial(on_device, dims),
        mesh=mesh,
        in_specs=(
            P("view", ("groups", "gz"), None, "gy", None),
            P("view", "gy", ("groups", "gz")),
            P("view", "gy", ("groups", "gz"), None),
            P("view", "gy", ("groups", "gz")),
            P("view", None),
            P("view", None, None),
        ),
        out_specs=(P(("groups", "gz"), "gy", None), P("view", ("groups", "gz"), "gy", None)),
        check_vma=False,
    )
```

```python
import functools

import jax
import jax.numpy as jnp
from jax import lax
from jax.experimental import pallas as pl
from jax.experimental.pallas import tpu as pltpu
from jax.sharding import PartitionSpec as P

CZ = 8
ITERS = 2
HALO = 8
CHUNK = 4
CP = 2
NCH = CZ // CP
OC = 4
NOUT = CZ // OC

DATA_FLOOR = 0.25
TINY = 1e-30
MESH = pl.DeviceIdType.MESH


def deposit_kernel(
    rows, dest_in, offs_in, level_in, frac_in, psf_in, cam_ref, acc_ref, tap_ref,
    dest, offs, level, frac, psf, cam, sems, small,
):
    taps = psf.shape[2]
    blocks, planes = cam_ref.shape[:2]
    pairs = ((dest_in, dest), (offs_in, offs), (level_in, level), (frac_in, frac), (psf_in, psf))
    copies = [pltpu.make_async_copy(a, b, small.at[n]) for n, (a, b) in enumerate(pairs)]
    for copy in copies:
        copy.start()

    def fetch(c):
        at = pl.ds(c * CHUNK, CHUNK)
        return pltpu.make_async_copy(cam_ref.at[at], cam.at[at], sems.at[c])

    for c in range(blocks // CHUNK):
        fetch(c).start()

    @pl.loop(0, acc_ref.shape[0])
    def _(s):
        acc_ref[s] = jnp.zeros(acc_ref.shape[1:], jnp.float32)

    for copy in copies:
        copy.wait()

    tap_ref[...] = jnp.zeros(tap_ref.shape, jnp.float32)
    for axis in range(3):
        scale = jnp.sum(psf[axis], axis=1, keepdims=True)
        share = psf[axis] / scale
        for t in range(taps):
            at = axis * taps + t
            tap_ref[at : at + 1, :] = jnp.broadcast_to(share[:, t : t + 1], (1, 128))
        at = 3 * taps + axis
        tap_ref[at : at + 1, :] = jnp.zeros((1, 128), jnp.float32) + frac[axis]

    fz = frac[0]
    base = level[0, 0, 0].astype(jnp.float32)

    @pl.loop(0, blocks // CHUNK)
    def _(c):
        fetch(c).wait()
        for i in range(CHUNK):
            b = c * CHUNK + i
            s = dest[b]
            o = offs[b]
            lower = cam[b, 0] - base
            for k in range(planes - 1):
                upper = cam[b, k + 1] - base
                at = pl.ds(pl.multiple_of(CZ + (o + k) * rows, 8), rows)
                acc_ref[s, at, :] = acc_ref[s, at, :] + ((1.0 - fz) * lower + fz * upper)
                cnt = pl.ds(o + k, 1)
                acc_ref[s, cnt, :] = acc_ref[s, cnt, :] + 1.0
                lower = upper


def world_kernel(
    dims, rows, taps,
    acc_ref, tap_in, est_ref, joined_ref,
    ru, rd, tap_all, jx, e0, e1, kx, xb, za, zb, yb, lg,
    us, ur, ds_, dr, tap_s, tap_r, loc_sem, ms, mr, los, lor, his, hir,
    zs, zr, es, er, out_s, out_r,
):
    slabs, views, bands = dims
    strip = rows // views
    wide = strip + 2 * HALO
    margin = taps // 2
    z = lax.axis_index("gz")
    v = lax.axis_index("view")
    g = lax.axis_index("gy")
    strips = views * bands
    me = v * bands + g
    band, idx = me // views, me % views

    def dev(zz, vv, gg):
        return {"gz": zz, "view": vv, "gy": gg}

    def strip_dev(zz, ss):
        return dev(zz, ss // bands, ss % bands)

    below, above = z > 0, z < slabs - 1
    left, right = me > 0, me < strips - 1

    barrier = pltpu.get_barrier_semaphore()

    def greet(target):
        pl.semaphore_signal(barrier, inc=1, device_id=target, device_id_type=MESH)

    amount = strips - 1 + below.astype(jnp.int32) + above.astype(jnp.int32)
    for dz, ok in ((1, above), (-1, below)):
        @pl.when(ok)
        def _(dz=dz):
            greet(dev(z + dz, v, g))

    for d in range(1, strips):
        greet(strip_dev(z, (me + d) % strips))

    def clear(ref, planes, lo, hi):
        @pl.loop(planes[0], planes[1])
        def _(p):
            ref[p, lo:hi, :] = jnp.zeros((hi - lo, 128), jnp.float32)

    pl.semaphore_wait(barrier, amount)

    def span(c):
        start = 0 if c == 0 else CZ + c * CP * rows
        return pl.ds(start, CZ + (c + 1) * CP * rows - start)

    def up_copy(src, t, c):
        return pltpu.make_async_remote_copy(
            src_ref=src.at[t, span(c)], dst_ref=ru.at[t, span(c)], send_sem=us.at[t, c],
            recv_sem=ur.at[t, c], device_id={"gz": z + 1}, device_id_type=MESH)

    def down_copy(src, t, c):
        return pltpu.make_async_remote_copy(
            src_ref=src.at[t, span(c)], dst_ref=rd.at[t, span(c)], send_sem=ds_.at[t, c],
            recv_sem=dr.at[t, c], device_id={"gz": z - 1}, device_id_type=MESH)

    @pl.when(z == 0)
    def _():
        @pl.loop(0, slabs - 1)
        def _(k):
            for c in range(NCH):
                up_copy(acc_ref, slabs - 1 - k, c).start()

    @pl.when(z == slabs - 1)
    def _():
        @pl.loop(0, slabs - 1)
        def _(k):
            for c in range(NCH):
                down_copy(acc_ref, k, c).start()

    for edge, flow, halo in ((z == 0, ru, (0, CZ)), (z == slabs - 1, rd, (2 * CZ, 3 * CZ))):
        @pl.when(edge)
        def _(flow=flow, halo=halo):
            flow[z] = jnp.zeros(flow.shape[1:], jnp.float32)
            for ref in [e0, e1] + [jx.at[w] for w in range(views)]:
                clear(ref, halo, 0, wide)

    for edge, lo, hi in ((me == 0, 0, HALO), (me == strips - 1, HALO + strip, wide)):
        @pl.when(edge)
        def _(lo=lo, hi=hi):
            clear(e1, (0, 3 * CZ), lo, hi)
            for w in range(views):
                clear(jx.at[w], (CZ, 2 * CZ), lo, hi)

    own_tap = pltpu.make_async_copy(tap_in, tap_all.at[v], loc_sem)
    own_tap.start()

    def tap_copy(d):
        return pltpu.make_async_remote_copy(
            src_ref=tap_in, dst_ref=tap_all.at[v], send_sem=tap_s.at[d - 1],
            recv_sem=tap_r.at[d - 1], device_id={"view": (v + d) % views}, device_id_type=MESH)

    for d in range(1, views):
        tap_copy(d).start()

    def pass_on(copy, ref, t, ok):
        @pl.when(ok)
        def _():
            for c in range(NCH):
                at = span(c)
                copy(ref, t, c).wait_recv()
                ref[t, at] = ref[t, at] + acc_ref[t, at]
                copy(ref, t, c).start()

    def pass_up(k):
        t = slabs - 1 - k
        pass_on(up_copy, ru, t, below & (t > z))

    def pass_down(k):
        pass_on(down_copy, rd, k, above & (k < z))

    @pl.loop(0, slabs - 1)
    def _(k):
        low = 2 * z < slabs

        @pl.when(low)
        def _():
            pass_up(k)
            pass_down(k)

        @pl.when(jnp.logical_not(low))
        def _():
            pass_down(k)
            pass_up(k)

    own_tap.wait()
    for d in range(1, views):
        tap_copy(d).wait()

    apart = lax.broadcasted_iota(jnp.int32, (128, 128), 0) - lax.broadcasted_iota(jnp.int32, (128, 128), 1)

    @pl.loop(0, views)
    def _(w):
        ahead = jnp.zeros((128, 128), jnp.float32)
        back = jnp.zeros((128, 128), jnp.float32)
        for t in range(taps):
            tap = tap_all[w, 2 * taps + t : 2 * taps + t + 1, :]
            ahead = jnp.where(apart == t - margin, tap, ahead)
            back = jnp.where(apart == margin - t, tap, back)
        for n, full in enumerate((ahead, back)):
            top = full.astype(jnp.bfloat16)
            kx[w, n, 0:128, 0:128] = top
            kx[w, n, 128:256, 0:128] = top
            kx[w, n, 0:128, 128:256] = (full - top.astype(jnp.float32)).astype(jnp.bfloat16)
            kx[w, n, 128:256, 128:256] = jnp.zeros((128, 128), jnp.bfloat16)

    fy, fx = [tap_in[3 * taps + n : 3 * taps + n + 1, :] for n in (1, 2)]
    last_row = lax.broadcasted_iota(jnp.int32, (rows, 128), 0) == rows - 1
    last_col = lax.broadcasted_iota(jnp.int32, (rows, 128), 1) == 127
    joined = joined_ref.at[0]
    mid = pl.ds(CZ, CZ)

    def planes_of(c):
        return pl.ds(c * CP, CP), pl.ds(CZ + c * CP, CP)

    def piece(i):
        lo, hi = max(i * strip - HALO, 0), min((i + 1) * strip + HALO, rows)
        return (lo, hi), (lo - i * strip + HALO, hi - i * strip + HALO)

    low_edge = ((rows - HALO, rows), (0, HALO))
    high_edge = ((0, HALO), (HALO + strip, wide))

    def part_copy(c, w, rows_of, target, send, recv):
        src_p, dst_p = planes_of(c)
        (lo, hi), (dlo, dhi) = rows_of
        return pltpu.make_async_remote_copy(
            src_ref=joined.at[src_p, pl.ds(lo, hi - lo), :], dst_ref=jx.at[w, dst_p, pl.ds(dlo, dhi - dlo), :],
            send_sem=send, recv_sem=recv, device_id=strip_dev(z, target), device_id_type=MESH)

    def sends(c):
        out = []
        for i in range(views):
            out.append((g * views + i, z >= 0, piece(i), ms.at[i, c], mr.at[v, c]))
        out.append(((g + 1) * views, g < bands - 1, low_edge, los.at[c], lor.at[v, c]))
        out.append((g * views - 1, g > 0, high_edge, his.at[c], hir.at[v, c]))
        return out

    def join(c):
        src_p, _ = planes_of(c)

        @pl.when(below)
        def _():
            up_copy(acc_ref, z, c).wait_recv()

        @pl.when(above)
        def _():
            down_copy(acc_ref, z, c).wait_recv()

        for p in range(c * CP, (c + 1) * CP):
            at = pl.ds(CZ + p * rows, rows)
            total = acc_ref[z, at, :] + ru[z, at, :] + rd[z, at, :]
            cnt = pl.ds(p, 1)
            covered = acc_ref[z, cnt, :] + ru[z, cnt, :] + rd[z, cnt, :]
            follow = jnp.where(last_row, total, pltpu.roll(total, rows - 1, 0))
            total = (1.0 - fy) * total + fy * follow
            follow = jnp.where(last_col, total, pltpu.roll(total, 127, 1))
            total = (1.0 - fx) * total + fx * follow
            joined_ref[0, p] = jnp.maximum(total / (covered + 1.0), DATA_FLOOR)
        for target, ok, rows_of, send, recv in sends(c):
            (lo, hi), (dlo, dhi) = rows_of

            @pl.when(ok & (target != me))
            def _(rows_of=rows_of, target=target, send=send, recv=recv):
                part_copy(c, v, rows_of, target, send, recv).start()

            @pl.when(ok & (target == me))
            def _(lo=lo, hi=hi, dlo=dlo, dhi=dhi):
                for p in range(c * CP, (c + 1) * CP):
                    jx[v, CZ + p, dlo:dhi, :] = joined_ref[0, p, lo:hi, :]

    def z_copy(ref, w, c, up, send, recv):
        dst = (0 if up else 2 * CZ) + c * CP
        src = CZ + c * CP
        a, b = ref.at[pl.ds(src, CP)], ref.at[pl.ds(dst, CP)]
        return pltpu.make_async_remote_copy(
            src_ref=a, dst_ref=b, send_sem=send, recv_sem=recv,
            device_id={"gz": z + 1 if up else z - 1}, device_id_type=MESH)

    def z_copies(c, up):
        side = 1 if up else 0
        near = c * CP >= CZ - margin if up else c * CP < margin
        if near:
            return [z_copy(jx.at[w], w, c, up, zs.at[side, w, c], zr.at[side, w, c]) for w in range(views)]
        return [z_copy(e0, 0, c, up, zs.at[side, 0, c], zr.at[side, 0, c])]

    def average(p):
        total = jx[0, p]
        for w in range(1, views):
            total = total + jx[w, p]
        e0[p] = total / views

    def spread(c):
        for w in range(views):
            for i in range(views):
                @pl.when((idx == i) & ((w != v) | (band != g)))
                def _(i=i, w=w):
                    part_copy(c, w, piece(i), me, ms.at[i, c], mr.at[w, c]).wait_recv()

            @pl.when((idx == 0) & (band > 0) & ((w != v) | (band - 1 != g)))
            def _(w=w):
                part_copy(c, w, low_edge, me, los.at[c], lor.at[w, c]).wait_recv()

            @pl.when((idx == views - 1) & (band < bands - 1) & ((w != v) | (band + 1 != g)))
            def _(w=w):
                part_copy(c, w, high_edge, me, his.at[c], hir.at[w, c]).wait_recv()

        for p in range(c * CP, (c + 1) * CP):
            average(CZ + p)
        for up, ok in ((True, above), (False, below)):
            @pl.when(ok)
            def _(up=up):
                for copy in z_copies(c, up):
                    copy.start()

    planes_r = CZ + 2 * margin
    rows_r = strip + 2 * margin

    def along_x(u, w, n):
        top = u.astype(jnp.bfloat16)
        rest = (u - top.astype(jnp.float32)).astype(jnp.bfloat16)
        both = jnp.dot(jnp.concatenate([top, rest], axis=1), kx[w, n], preferred_element_type=jnp.float32)
        return both[:, 0:128] + both[:, 128:256]

    def weighted(terms, weights):
        total = weights[0] * terms[0]
        for term, weight in zip(terms[1:], weights[1:]):
            total = total + weight * term
        return total

    def root(terms):
        if len(terms) == 1:
            return terms[0]
        if len(terms) % 2:
            total = jnp.log(terms[0])
            for term in terms[1:]:
                total = total + jnp.log(term)
            return jnp.exp(total / len(terms))
        return root([jnp.sqrt(a * b) for a, b in zip(terms[0::2], terms[1::2])])

    def tap(w, axis, t):
        at = axis * taps + t
        return tap_all[w, at : at + 1, :]

    def blur_rows(est, first):
        for p in range(OC):
            terms = [est[first + p, t : t + rows_r, :] for t in range(taps)]
            for w in range(views):
                zb[w, p] = weighted(terms, [tap(w, 1, t) for t in range(taps)])
        for w in range(views):
            xb[w, pl.ds(first, OC)] = along_x(zb[w].reshape(OC * rows_r, 128), w, 0).reshape(OC, rows_r, 128)

    def correct(est, emit):
        @pl.loop(0, rows_r // 8)
        def _(r):
            at = pl.ds(pl.multiple_of(r * 8, 8), 8)
            for w in range(views):
                column = [xb[w, p, at, :] for p in range(3 * CZ)]
                ratio = []
                for p in range(planes_r):
                    first = CZ - 2 * margin + p
                    blurred = weighted(column[first : first + taps], [tap(w, 0, t) for t in range(taps)])
                    blurred = jnp.maximum(blurred, TINY)
                    inverse = pl.reciprocal(blurred, approx=True)
                    inverse = inverse * (2.0 - blurred * inverse)
                    ratio.append(jx[w, CZ - margin + p, pl.ds(r * 8 + HALO - margin, 8), :] * inverse)
                for p in range(CZ):
                    za[w, p, at, :] = weighted(ratio[p : p + taps], [tap(w, 0, taps - 1 - t) for t in range(taps)])

        for c in range(NOUT):
            factors = []
            for w in range(views):
                for p in range(OC):
                    yb[w, p] = weighted([za[w, c * OC + p, t : t + strip, :] for t in range(taps)],
                                        [tap(w, 1, taps - 1 - t) for t in range(taps)])
                factors.append(along_x(yb[w].reshape(OC * strip, 128), w, 1).reshape(OC, strip, 128))
            emit(c, est[pl.ds(CZ + c * OC, OC), HALO : HALO + strip, :] * root(factors))

    join(0)
    for c in range(1, NCH):
        join(c)
        spread(c - 1)
    for c in range(NOUT - 1):
        blur_rows(e0, CZ + c * OC)
    spread(NCH - 1)
    blur_rows(e0, 2 * CZ - OC)

    for group in range(NOUT):
        for up, ok in ((True, below), (False, above)):
            @pl.when(ok)
            def _(up=up, group=group):
                for c in range(group * OC // CP, (group + 1) * OC // CP):
                    copies = z_copies(c, up)
                    for copy in copies:
                        copy.wait_recv()
                    if len(copies) == views and views > 1:
                        for p in range(c * CP, (c + 1) * CP):
                            average((0 if up else 2 * CZ) + p)

            blur_rows(e0, (0 if up else 2 * CZ) + group * OC)

    inner = pl.ds(HALO, strip)
    near = []
    for n, (dz, ds) in enumerate([(a, b) for a in (-1, 1, 0) for b in (0, -1, 1) if a or b]):
        zok = {-1: below, 0: z >= 0, 1: above}[dz]
        sok = {-1: left, 0: z >= 0, 1: right}[ds]
        far_z = {-1: above, 0: z >= 0, 1: below}[dz]
        far_s = {-1: right, 0: z >= 0, 1: left}[ds]
        near.append((n, dz, ds, zok & sok, far_z & far_s))

    def near_copy(n, dz, ds, c):
        src_r = {-1: pl.ds(HALO, HALO), 0: inner, 1: pl.ds(strip, HALO)}[ds]
        dst_r = {-1: pl.ds(HALO + strip, HALO), 0: inner, 1: pl.ds(0, HALO)}[ds]
        dst = {-1: 2 * CZ, 0: CZ, 1: 0}[dz] + c * OC
        return pltpu.make_async_remote_copy(
            src_ref=e1.at[pl.ds(CZ + c * OC, OC), src_r, :], dst_ref=e1.at[pl.ds(dst, OC), dst_r, :],
            send_sem=es.at[n, c], recv_sem=er.at[n, c], device_id=strip_dev(z + dz, me + ds), device_id_type=MESH)

    def emit_step(c, new):
        e1[pl.ds(CZ + c * OC, OC), HALO : HALO + strip, :] = new
        for n, dz, ds, ok, _ in near:
            @pl.when(ok)
            def _(n=n, dz=dz, ds=ds):
                near_copy(n, dz, ds, c).start()

    correct(e0, emit_step)

    @pl.loop(0, slabs)
    def _(t):
        for c in range(NCH):
            @pl.when(t > z)
            def _():
                up_copy(acc_ref, t, c).wait_send()

            @pl.when(t < z)
            def _():
                down_copy(acc_ref, t, c).wait_send()

    for c in range(NCH):
        for target, ok, rows_of, send, recv in sends(c):
            @pl.when(ok & (target != me))
            def _(rows_of=rows_of, target=target, send=send, recv=recv, c=c):
                part_copy(c, v, rows_of, target, send, recv).wait_send()

        for up, ok in ((True, above), (False, below)):
            @pl.when(ok)
            def _(up=up, c=c):
                for copy in z_copies(c, up):
                    copy.wait_send()

    def near_wait(c, way):
        for n, dz, ds, _, ok in near:
            if dz == way:
                @pl.when(ok)
                def _(n=n, dz=dz, ds=ds):
                    near_copy(n, dz, ds, c).wait_recv()

    for c in range(NOUT):
        near_wait(c, 0)
        blur_rows(e1, CZ + c * OC)
    for c in range(NOUT):
        for way in (1, -1):
            near_wait(c, way)
            blur_rows(e1, CZ - way * CZ + c * OC)

    def out_copy(c, w, target_g, i):
        at = pl.ds(pl.multiple_of(i * strip, 8), strip)
        part = pl.ds(c * OC, OC)
        return pltpu.make_async_remote_copy(
            src_ref=lg.at[part], dst_ref=est_ref.at[part, at, :], send_sem=out_s.at[w, c],
            recv_sem=out_r.at[i, c], device_id=dev(z, w, target_g), device_id_type=MESH)

    def emit_last(c, new):
        lg[pl.ds(c * OC, OC)] = new
        for w in range(views):
            away = (w != v) | (band != g)

            @pl.when(away)
            def _(w=w):
                out_copy(c, w, band, idx).start()

            @pl.when(jnp.logical_not(away))
            def _():
                est_ref[pl.ds(c * OC, OC), pl.ds(pl.multiple_of(idx * strip, 8), strip), :] = new

    correct(e1, emit_last)

    for c in range(NOUT):
        for n, dz, ds, ok, _ in near:
            @pl.when(ok)
            def _(n=n, dz=dz, ds=ds, c=c):
                near_copy(n, dz, ds, c).wait_send()

    for c in range(NOUT):
        for i in range(views):
            @pl.when(g * views + i != me)
            def _(i=i, c=c):
                out_copy(c, 0, g, i).wait_recv()

    for c in range(NOUT):
        for w in range(views):
            @pl.when((w != v) | (band != g))
            def _(w=w, c=c):
                out_copy(c, w, band, idx).wait_send()


def store_kernel(est_in, joined_in, est_out, joined_out, sems):
    copies = [pltpu.make_async_copy(a, b, sems.at[n]) for n, (a, b) in enumerate(((est_in, est_out), (joined_in, joined_out)))]
    for copy in copies:
        copy.start()
    for copy in copies:
        copy.wait()


def on_device(dims, camera, background, destination, offsets, shift_frac, psf_taps):
    slabs, views, bands = dims
    blocks, planes, rows, cols = camera.shape[1:]
    taps = psf_taps.shape[-1]
    margin = taps // 2
    tall = CZ * rows + CZ
    strip = rows // views
    wide = strip + 2 * HALO
    tap_rows = -(-3 * (taps + 1) // 8) * 8
    vmem = pl.BlockSpec(memory_space=pltpu.VMEM)
    hbm = functools.partial(pltpu.with_memory_space_constraint, memory_space=pltpu.HBM)
    cell = 4 * cols
    room = 2 * 1024 * 1024
    acc, tap_rows_all = pl.pallas_call(
        functools.partial(deposit_kernel, rows),
        in_specs=[pl.BlockSpec(memory_space=pltpu.HBM)] * 6,
        out_specs=(vmem, vmem),
        out_shape=(
            pltpu.VMEM((slabs, tall, cols), jnp.float32),
            pltpu.VMEM((tap_rows, cols), jnp.float32),
        ),
        scratch_shapes=[
            pltpu.SMEM((blocks,), jnp.int32),
            pltpu.SMEM((blocks,), jnp.int32),
            pltpu.SMEM((1, 1, 1), jnp.int32),
            pltpu.SMEM((3,), jnp.float32),
            pltpu.VMEM((3, 1, taps), jnp.float32),
            pltpu.VMEM((blocks, planes, rows, cols), jnp.float32),
            pltpu.SemaphoreType.DMA((blocks // CHUNK,)),
            pltpu.SemaphoreType.DMA((5,)),
        ],
        compiler_params=pltpu.CompilerParams(
            vmem_limit_bytes=cell * (blocks * planes * rows + slabs * tall) + room),
        name="deposit",
    )(hbm(destination.reshape(-1)), hbm(offsets.reshape(-1)), background, hbm(shift_frac[0]),
      hbm(jnp.transpose(psf_taps, (1, 0, 2))), hbm(camera[0]))

    dma = pltpu.SemaphoreType.DMA
    f32 = jnp.float32
    shapes = [
        (slabs, tall, cols), (slabs, tall, cols), (views, tap_rows, cols),
        (views, 3 * CZ, wide, cols), (3 * CZ, wide, cols), (3 * CZ, wide, cols),
    ]
    late = [
        (views, 3 * CZ, strip + 2 * margin, cols), (views, CZ, strip + 2 * margin, cols),
        (views, OC, strip + 2 * margin, cols), (views, OC, strip, cols), (CZ, strip, cols),
    ]
    total = sum([functools.reduce(lambda a, b: a * b, s) for s in shapes + late])
    total = total + cols * (slabs * tall + 2 * CZ * rows + views * 4 * cols)
    estimate, joined = pl.pallas_call(
        functools.partial(world_kernel, dims, rows, taps),
        in_specs=[vmem, vmem],
        out_specs=(vmem, vmem),
        out_shape=(
            pltpu.VMEM((CZ, rows, cols), f32),
            pltpu.VMEM((1, CZ, rows, cols), f32),
        ),
        scratch_shapes=[pltpu.VMEM(s, f32) for s in shapes]
        + [pltpu.VMEM((views, 2, 2 * cols, 2 * cols), jnp.bfloat16)]
        + [pltpu.VMEM(s, f32) for s in late]
        + [
            dma((slabs, NCH)), dma((slabs, NCH)), dma((slabs, NCH)), dma((slabs, NCH)),
            dma((views,)), dma((views,)), dma,
            dma((views, NCH)), dma((views, NCH)), dma((NCH,)), dma((views, NCH)), dma((NCH,)), dma((views, NCH)),
            dma((2, views, NCH)), dma((2, views, NCH)), dma((8, NOUT)), dma((8, NOUT)),
            dma((views, NOUT)), dma((views, NOUT)),
        ],
        compiler_params=pltpu.CompilerParams(
            collective_id=0, has_side_effects=True, vmem_limit_bytes=4 * total + room),
        name="world",
    )(acc, tap_rows_all)
    return pl.pallas_call(
        store_kernel,
        in_specs=[vmem, vmem],
        out_specs=(pl.BlockSpec(memory_space=pltpu.HBM), pl.BlockSpec(memory_space=pltpu.HBM)),
        out_shape=(jax.ShapeDtypeStruct(estimate.shape, f32), jax.ShapeDtypeStruct(joined.shape, f32)),
        scratch_shapes=[dma((2,))],
        name="store",
    )(pltpu.with_memory_space_constraint(estimate, pltpu.VMEM), pltpu.with_memory_space_constraint(joined, pltpu.VMEM))


def solution(mesh):
    dims = (mesh.shape["gz"], mesh.shape["view"], mesh.shape["gy"])
    return jax.shard_map(
        functools.partial(on_device, dims),
        mesh=mesh,
        in_specs=(
            P("view", ("groups", "gz"), None, "gy", None),
            P("view", "gy", ("groups", "gz")),
            P("view", "gy", ("groups", "gz"), None),
            P("view", "gy", ("groups", "gz")),
            P("view", None),
            P("view", None, None),
        ),
        out_specs=(P(("groups", "gz"), "gy", None), P("view", ("groups", "gz"), "gy", None)),
        check_vma=False,
    )
```

```python
import functools

import jax
import jax.numpy as jnp
from jax import lax
from jax.experimental import pallas as pl
from jax.experimental.pallas import tpu as pltpu
from jax.sharding import PartitionSpec as P

CZ = 8
ITERS = 2
HALO = 8
CHUNK = 4
CP = 2
NCH = CZ // CP
OC = 4
NOUT = CZ // OC

DATA_FLOOR = 0.25
TINY = 1e-30
MESH = pl.DeviceIdType.MESH


def deposit_kernel(
    rows, dest_in, offs_in, level_in, frac_in, cam_ref, acc_ref,
    dest, offs, level, frac, hits, cam, sems, small,
):
    blocks, planes = cam_ref.shape[:2]
    slabs = acc_ref.shape[0]
    pairs = ((dest_in, dest), (offs_in, offs), (level_in, level), (frac_in, frac))
    copies = [pltpu.make_async_copy(a, b, small.at[n]) for n, (a, b) in enumerate(pairs)]
    for copy in copies:
        copy.start()

    def fetch(c):
        at = pl.ds(c * CHUNK, CHUNK)
        return pltpu.make_async_copy(cam_ref.at[at], cam.at[at], sems.at[c])

    for c in range(blocks // CHUNK):
        fetch(c).start()

    @pl.loop(0, slabs)
    def _(s):
        for p in range(CZ):
            hits[s * CZ + p] = 0
        acc_ref[s] = jnp.zeros(acc_ref.shape[1:], jnp.float32)

    for copy in copies:
        copy.wait()

    fz = frac[0]
    base = level[0, 0, 0].astype(jnp.float32)

    @pl.loop(0, blocks // CHUNK)
    def _(c):
        fetch(c).wait()
        for i in range(CHUNK):
            b = c * CHUNK + i
            s = dest[b]
            o = offs[b]
            mixed = (1.0 - fz) * cam[b, 0 : planes - 1] + (fz * cam[b, 1:planes] - base)
            at = pl.ds(pl.multiple_of(CZ + o * rows, 8), (planes - 1) * rows)
            acc_ref[s, at, :] = acc_ref[s, at, :] + mixed.reshape((planes - 1) * rows, 128)
            for k in range(planes - 1):
                hits[s * CZ + o + k] = hits[s * CZ + o + k] + 1

    @pl.loop(0, slabs, unroll=4)
    def _(s):
        for p in range(CZ):
            acc_ref[s, p : p + 1, :] = jnp.zeros((1, 128), jnp.float32) + hits[s * CZ + p].astype(jnp.float32)


def world_kernel(
    dims, rows, taps,
    acc_ref, frac_in, psf_in, est_ref, joined_ref,
    frac, psf, tap_in, ru, rd, tap_all, jx, e0, e1, kx, xb, rt, za, zb, yb, lg,
    small, us, ur, ds_, dr, tap_s, tap_r, loc_sem, ms, mr, los, lor, his, hir,
    zs, zr, es, er, out_s, out_r,
):
    loads = [pltpu.make_async_copy(a, b, small.at[n]) for n, (a, b) in enumerate(((frac_in, frac), (psf_in, psf)))]
    for load in loads:
        load.start()

    slabs, views, bands = dims
    strip = rows // views
    wide = strip + 2 * HALO
    margin = taps // 2
    z = lax.axis_index("gz")
    v = lax.axis_index("view")
    g = lax.axis_index("gy")
    strips = views * bands
    me = v * bands + g
    band, idx = me // views, me % views

    def dev(zz, vv, gg):
        return {"gz": zz, "view": vv, "gy": gg}

    def strip_dev(zz, ss):
        return dev(zz, ss // bands, ss % bands)

    below, above = z > 0, z < slabs - 1
    left, right = me > 0, me < strips - 1

    barrier = pltpu.get_barrier_semaphore()

    def greet(target):
        pl.semaphore_signal(barrier, inc=1, device_id=target, device_id_type=MESH)

    amount = strips - 1 + below.astype(jnp.int32) + above.astype(jnp.int32)
    for dz, ok in ((1, above), (-1, below)):
        @pl.when(ok)
        def _(dz=dz):
            greet(dev(z + dz, v, g))

    for d in range(1, strips):
        greet(strip_dev(z, (me + d) % strips))

    def clear(ref, planes, lo, hi):
        @pl.loop(planes[0], planes[1])
        def _(p):
            ref[p, lo:hi, :] = jnp.zeros((hi - lo, 128), jnp.float32)

    pl.semaphore_wait(barrier, amount)

    def span(c):
        start = 0 if c == 0 else CZ + c * CP * rows
        return pl.ds(start, CZ + (c + 1) * CP * rows - start)

    def up_copy(src, t, c):
        return pltpu.make_async_remote_copy(
            src_ref=src.at[t, span(c)], dst_ref=ru.at[t, span(c)], send_sem=us.at[t, c],
            recv_sem=ur.at[t, c], device_id={"gz": z + 1}, device_id_type=MESH)

    def down_copy(src, t, c):
        return pltpu.make_async_remote_copy(
            src_ref=src.at[t, span(c)], dst_ref=rd.at[t, span(c)], send_sem=ds_.at[t, c],
            recv_sem=dr.at[t, c], device_id={"gz": z - 1}, device_id_type=MESH)

    @pl.when(z == 0)
    def _():
        @pl.loop(0, slabs - 1)
        def _(k):
            for c in range(NCH):
                up_copy(acc_ref, slabs - 1 - k, c).start()

    @pl.when(z == slabs - 1)
    def _():
        @pl.loop(0, slabs - 1)
        def _(k):
            for c in range(NCH):
                down_copy(acc_ref, k, c).start()

    for edge, flow, halo in ((z == 0, ru, (0, CZ)), (z == slabs - 1, rd, (2 * CZ, 3 * CZ))):
        @pl.when(edge)
        def _(flow=flow, halo=halo):
            flow[z] = jnp.zeros(flow.shape[1:], jnp.float32)
            for ref in [e0, e1] + [jx.at[w] for w in range(views)]:
                clear(ref, halo, 0, wide)

    for edge, lo, hi in ((me == 0, 0, HALO), (me == strips - 1, HALO + strip, wide)):
        @pl.when(edge)
        def _(lo=lo, hi=hi):
            clear(e1, (0, 3 * CZ), lo, hi)
            for w in range(views):
                clear(jx.at[w], (CZ, 2 * CZ), lo, hi)

    for load in loads:
        load.wait()

    for axis in range(3):
        scale = jnp.sum(psf[axis], axis=1, keepdims=True)
        share = psf[axis] / scale
        for t in range(taps):
            at = axis * taps + t
            tap_in[at : at + 1, :] = jnp.broadcast_to(share[:, t : t + 1], (1, 128))

    own_tap = pltpu.make_async_copy(tap_in, tap_all.at[v], loc_sem)
    own_tap.start()

    def tap_copy(d):
        return pltpu.make_async_remote_copy(
            src_ref=tap_in, dst_ref=tap_all.at[v], send_sem=tap_s.at[d - 1],
            recv_sem=tap_r.at[d - 1], device_id={"view": (v + d) % views}, device_id_type=MESH)

    for d in range(1, views):
        tap_copy(d).start()

    def pass_on(copy, ref, t, ok):
        @pl.when(ok)
        def _():
            for c in range(NCH):
                at = span(c)
                copy(ref, t, c).wait_recv()
                ref[t, at] = ref[t, at] + acc_ref[t, at]
                copy(ref, t, c).start()

    def pass_up(k):
        t = slabs - 1 - k
        pass_on(up_copy, ru, t, below & (t > z))

    def pass_down(k):
        pass_on(down_copy, rd, k, above & (k < z))

    @pl.loop(0, slabs - 1)
    def _(k):
        low = 2 * z < slabs

        @pl.when(low)
        def _():
            pass_up(k)
            pass_down(k)

        @pl.when(jnp.logical_not(low))
        def _():
            pass_down(k)
            pass_up(k)

    own_tap.wait()
    for d in range(1, views):
        tap_copy(d).wait()

    apart = lax.broadcasted_iota(jnp.int32, (128, 128), 0) - lax.broadcasted_iota(jnp.int32, (128, 128), 1)

    @pl.loop(0, views)
    def _(w):
        ahead = jnp.zeros((128, 128), jnp.float32)
        back = jnp.zeros((128, 128), jnp.float32)
        for t in range(taps):
            tap = tap_all[w, 2 * taps + t : 2 * taps + t + 1, :]
            ahead = jnp.where(apart == t - margin, tap, ahead)
            back = jnp.where(apart == margin - t, tap, back)
        for n, full in enumerate((ahead, back)):
            top = full.astype(jnp.bfloat16)
            kx[w, n, 0:128, 0:128] = top
            kx[w, n, 128:256, 0:128] = top
            kx[w, n, 0:128, 128:256] = (full - top.astype(jnp.float32)).astype(jnp.bfloat16)
            kx[w, n, 128:256, 128:256] = jnp.zeros((128, 128), jnp.bfloat16)

    fy, fx = frac[1], frac[2]
    last_row = lax.broadcasted_iota(jnp.int32, (rows, 128), 0) == rows - 1
    last_col = lax.broadcasted_iota(jnp.int32, (rows, 128), 1) == 127
    joined = joined_ref.at[0]
    mid = pl.ds(CZ, CZ)

    def planes_of(c):
        return pl.ds(c * CP, CP), pl.ds(CZ + c * CP, CP)

    def piece(i):
        lo, hi = max(i * strip - HALO, 0), min((i + 1) * strip + HALO, rows)
        return (lo, hi), (lo - i * strip + HALO, hi - i * strip + HALO)

    low_edge = ((rows - HALO, rows), (0, HALO))
    high_edge = ((0, HALO), (HALO + strip, wide))

    def part_copy(c, w, rows_of, target, send, recv):
        src_p, dst_p = planes_of(c)
        (lo, hi), (dlo, dhi) = rows_of
        return pltpu.make_async_remote_copy(
            src_ref=joined.at[src_p, pl.ds(lo, hi - lo), :], dst_ref=jx.at[w, dst_p, pl.ds(dlo, dhi - dlo), :],
            send_sem=send, recv_sem=recv, device_id=strip_dev(z, target), device_id_type=MESH)

    def sends(c):
        out = []
        for i in range(views):
            out.append((g * views + i, z >= 0, piece(i), ms.at[i, c], mr.at[v, c]))
        out.append(((g + 1) * views, g < bands - 1, low_edge, los.at[c], lor.at[v, c]))
        out.append((g * views - 1, g > 0, high_edge, his.at[c], hir.at[v, c]))
        return out

    def join(c):
        src_p, _ = planes_of(c)

        @pl.when(below)
        def _():
            up_copy(acc_ref, z, c).wait_recv()

        @pl.when(above)
        def _():
            down_copy(acc_ref, z, c).wait_recv()

        for p in range(c * CP, (c + 1) * CP):
            at = pl.ds(CZ + p * rows, rows)
            total = acc_ref[z, at, :] + ru[z, at, :] + rd[z, at, :]
            cnt = pl.ds(p, 1)
            covered = acc_ref[z, cnt, :] + ru[z, cnt, :] + rd[z, cnt, :]
            follow = jnp.where(last_row, total, pltpu.roll(total, rows - 1, 0))
            total = (1.0 - fy) * total + fy * follow
            follow = jnp.where(last_col, total, pltpu.roll(total, 127, 1))
            total = (1.0 - fx) * total + fx * follow
            joined_ref[0, p] = jnp.maximum(total / (covered + 1.0), DATA_FLOOR)
        for target, ok, rows_of, send, recv in sends(c):
            (lo, hi), (dlo, dhi) = rows_of

            @pl.when(ok & (target != me))
            def _(rows_of=rows_of, target=target, send=send, recv=recv):
                part_copy(c, v, rows_of, target, send, recv).start()

            @pl.when(ok & (target == me))
            def _(lo=lo, hi=hi, dlo=dlo, dhi=dhi):
                for p in range(c * CP, (c + 1) * CP):
                    jx[v, CZ + p, dlo:dhi, :] = joined_ref[0, p, lo:hi, :]

    def z_copy(ref, w, c, up, send, recv):
        dst = (0 if up else 2 * CZ) + c * CP
        src = CZ + c * CP
        a, b = ref.at[pl.ds(src, CP)], ref.at[pl.ds(dst, CP)]
        return pltpu.make_async_remote_copy(
            src_ref=a, dst_ref=b, send_sem=send, recv_sem=recv,
            device_id={"gz": z + 1 if up else z - 1}, device_id_type=MESH)

    def z_copies(c, up):
        side = 1 if up else 0
        near = c * CP >= CZ - margin if up else c * CP < margin
        if near:
            return [z_copy(jx.at[w], w, c, up, zs.at[side, w, c], zr.at[side, w, c]) for w in range(views)]
        return [z_copy(e0, 0, c, up, zs.at[side, 0, c], zr.at[side, 0, c])]

    def average(p):
        total = jx[0, p]
        for w in range(1, views):
            total = total + jx[w, p]
        e0[p] = total / views

    def spread(c):
        for w in range(views):
            for i in range(views):
                @pl.when((idx == i) & ((w != v) | (band != g)))
                def _(i=i, w=w):
                    part_copy(c, w, piece(i), me, ms.at[i, c], mr.at[w, c]).wait_recv()

            @pl.when((idx == 0) & (band > 0) & ((w != v) | (band - 1 != g)))
            def _(w=w):
                part_copy(c, w, low_edge, me, los.at[c], lor.at[w, c]).wait_recv()

            @pl.when((idx == views - 1) & (band < bands - 1) & ((w != v) | (band + 1 != g)))
            def _(w=w):
                part_copy(c, w, high_edge, me, his.at[c], hir.at[w, c]).wait_recv()

        for p in range(c * CP, (c + 1) * CP):
            average(CZ + p)
        for up, ok in ((True, above), (False, below)):
            @pl.when(ok)
            def _(up=up):
                for copy in z_copies(c, up):
                    copy.start()

    planes_r = CZ + 2 * margin
    rows_r = strip + 2 * margin

    def along_x(u, w, n):
        top = u.astype(jnp.bfloat16)
        rest = (u - top.astype(jnp.float32)).astype(jnp.bfloat16)
        both = jnp.dot(jnp.concatenate([top, rest], axis=1), kx[w, n], preferred_element_type=jnp.float32)
        return both[:, 0:128] + both[:, 128:256]

    def weighted(terms, weights):
        total = weights[0] * terms[0]
        for term, weight in zip(terms[1:], weights[1:]):
            total = total + weight * term
        return total

    def root(terms):
        if len(terms) == 1:
            return terms[0]
        if len(terms) % 2:
            total = jnp.log(terms[0])
            for term in terms[1:]:
                total = total + jnp.log(term)
            return jnp.exp(total / len(terms))
        return root([jnp.sqrt(a * b) for a, b in zip(terms[0::2], terms[1::2])])

    def tap(w, axis, t):
        at = axis * taps + t
        return tap_all[w, at : at + 1, :]

    def blur_rows(est, first):
        for p in range(OC):
            terms = [est[first + p, t : t + rows_r, :] for t in range(taps)]
            for w in range(views):
                zb[w, p] = weighted(terms, [tap(w, 1, t) for t in range(taps)])
        for w in range(views):
            xb[w, pl.ds(first, OC)] = along_x(zb[w].reshape(OC * rows_r, 128), w, 0).reshape(OC, rows_r, 128)

    def ratios(r, at, w, lo, hi):
        base = CZ - 2 * margin
        column = [xb[w, base + p, at, :] for p in range(lo, hi + 2 * margin)]
        out = []
        for p in range(lo, hi):
            blurred = weighted(column[p - lo : p - lo + taps], [tap(w, 0, t) for t in range(taps)])
            blurred = jnp.maximum(blurred, TINY)
            inverse = pl.reciprocal(blurred, approx=True)
            inverse = inverse * (2.0 - blurred * inverse)
            out.append(jx[w, CZ - margin + p, pl.ds(r * 8 + HALO - margin, 8), :] * inverse)
        return out

    def correct(est, emit):
        for c in range(NOUT):
            done = c * OC + 2 * margin if c > 0 else 0
            stop = (c + 1) * OC + 2 * margin

            @pl.loop(0, rows_r // 8, unroll=True)
            def _(r, c=c, done=done, stop=stop):
                at = pl.ds(pl.multiple_of(r * 8, 8), 8)
                for w in range(views):
                    ratio = [rt[w, p, at, :] for p in range(c * OC, done)] + ratios(r, at, w, done, stop)
                    if c < NOUT - 1:
                        for p in range((c + 1) * OC, stop):
                            if p >= done:
                                rt[w, p, at, :] = ratio[p - c * OC]
                    for p in range(OC):
                        za[w, p, at, :] = weighted(ratio[p : p + taps], [tap(w, 0, taps - 1 - t) for t in range(taps)])

            factors = []
            for w in range(views):
                for p in range(OC):
                    yb[w, p] = weighted([za[w, p, t : t + strip, :] for t in range(taps)],
                                        [tap(w, 1, taps - 1 - t) for t in range(taps)])
                factors.append(along_x(yb[w].reshape(OC * strip, 128), w, 1).reshape(OC, strip, 128))
            emit(c, est[pl.ds(CZ + c * OC, OC), HALO : HALO + strip, :] * root(factors))

    join(0)
    for c in range(1, NCH):
        join(c)
        spread(c - 1)
    for c in range(NOUT - 1):
        blur_rows(e0, CZ + c * OC)
    spread(NCH - 1)
    blur_rows(e0, 2 * CZ - OC)

    for group in range(NOUT):
        for up, ok in ((True, below), (False, above)):
            @pl.when(ok)
            def _(up=up, group=group):
                for c in range(group * OC // CP, (group + 1) * OC // CP):
                    copies = z_copies(c, up)
                    for copy in copies:
                        copy.wait_recv()
                    if len(copies) == views and views > 1:
                        for p in range(c * CP, (c + 1) * CP):
                            average((0 if up else 2 * CZ) + p)

            blur_rows(e0, (0 if up else 2 * CZ) + group * OC)

    inner = pl.ds(HALO, strip)
    near = []
    for n, (dz, ds) in enumerate([(a, b) for a in (-1, 1, 0) for b in (0, -1, 1) if a or b]):
        zok = {-1: below, 0: z >= 0, 1: above}[dz]
        sok = {-1: left, 0: z >= 0, 1: right}[ds]
        far_z = {-1: above, 0: z >= 0, 1: below}[dz]
        far_s = {-1: right, 0: z >= 0, 1: left}[ds]
        near.append((n, dz, ds, zok & sok, far_z & far_s))

    def near_copy(n, dz, ds, c):
        src_r = {-1: pl.ds(HALO, HALO), 0: inner, 1: pl.ds(strip, HALO)}[ds]
        dst_r = {-1: pl.ds(HALO + strip, HALO), 0: inner, 1: pl.ds(0, HALO)}[ds]
        dst = {-1: 2 * CZ, 0: CZ, 1: 0}[dz] + c * OC
        return pltpu.make_async_remote_copy(
            src_ref=e1.at[pl.ds(CZ + c * OC, OC), src_r, :], dst_ref=e1.at[pl.ds(dst, OC), dst_r, :],
            send_sem=es.at[n, c], recv_sem=er.at[n, c], device_id=strip_dev(z + dz, me + ds), device_id_type=MESH)

    def emit_step(c, new):
        e1[pl.ds(CZ + c * OC, OC), HALO : HALO + strip, :] = new
        for n, dz, ds, ok, _ in near:
            @pl.when(ok)
            def _(n=n, dz=dz, ds=ds):
                near_copy(n, dz, ds, c).start()

    correct(e0, emit_step)

    @pl.loop(0, slabs)
    def _(t):
        for c in range(NCH):
            @pl.when(t > z)
            def _():
                up_copy(acc_ref, t, c).wait_send()

            @pl.when(t < z)
            def _():
                down_copy(acc_ref, t, c).wait_send()

    for c in range(NCH):
        for target, ok, rows_of, send, recv in sends(c):
            @pl.when(ok & (target != me))
            def _(rows_of=rows_of, target=target, send=send, recv=recv, c=c):
                part_copy(c, v, rows_of, target, send, recv).wait_send()

        for up, ok in ((True, above), (False, below)):
            @pl.when(ok)
            def _(up=up, c=c):
                for copy in z_copies(c, up):
                    copy.wait_send()

    def near_wait(c, way):
        for n, dz, ds, _, ok in near:
            if dz == way:
                @pl.when(ok)
                def _(n=n, dz=dz, ds=ds):
                    near_copy(n, dz, ds, c).wait_recv()

    for c in range(NOUT):
        near_wait(c, 0)
        blur_rows(e1, CZ + c * OC)
    for c in range(NOUT):
        for way in (1, -1):
            near_wait(c, way)
            blur_rows(e1, CZ - way * CZ + c * OC)

    def out_copy(c, w, target_g, i):
        at = pl.ds(pl.multiple_of(i * strip, 8), strip)
        part = pl.ds(c * OC, OC)
        return pltpu.make_async_remote_copy(
            src_ref=lg.at[part], dst_ref=est_ref.at[part, at, :], send_sem=out_s.at[w, c],
            recv_sem=out_r.at[i, c], device_id=dev(z, w, target_g), device_id_type=MESH)

    def emit_last(c, new):
        lg[pl.ds(c * OC, OC)] = new
        for w in range(views):
            away = (w != v) | (band != g)

            @pl.when(away)
            def _(w=w):
                out_copy(c, w, band, idx).start()

            @pl.when(jnp.logical_not(away))
            def _():
                est_ref[pl.ds(c * OC, OC), pl.ds(pl.multiple_of(idx * strip, 8), strip), :] = new

    correct(e1, emit_last)

    for c in range(NOUT):
        for n, dz, ds, ok, _ in near:
            @pl.when(ok)
            def _(n=n, dz=dz, ds=ds, c=c):
                near_copy(n, dz, ds, c).wait_send()

    for c in range(NOUT):
        for i in range(views):
            @pl.when(g * views + i != me)
            def _(i=i, c=c):
                out_copy(c, 0, g, i).wait_recv()

    for c in range(NOUT):
        for w in range(views):
            @pl.when((w != v) | (band != g))
            def _(w=w, c=c):
                out_copy(c, w, band, idx).wait_send()


def store_kernel(est_in, joined_in, est_out, joined_out, sems):
    copies = [pltpu.make_async_copy(a, b, sems.at[n]) for n, (a, b) in enumerate(((est_in, est_out), (joined_in, joined_out)))]
    for copy in copies:
        copy.start()
    for copy in copies:
        copy.wait()


def on_device(dims, camera, background, destination, offsets, shift_frac, psf_taps):
    slabs, views, bands = dims
    blocks, planes, rows, cols = camera.shape[1:]
    taps = psf_taps.shape[-1]
    margin = taps // 2
    tall = CZ * rows + CZ
    strip = rows // views
    wide = strip + 2 * HALO
    tap_rows = -(-3 * taps // 8) * 8
    vmem = pl.BlockSpec(memory_space=pltpu.VMEM)
    hbm = functools.partial(pltpu.with_memory_space_constraint, memory_space=pltpu.HBM)
    cell = 4 * cols
    room = 2 * 1024 * 1024
    any_hbm = pl.BlockSpec(memory_space=pltpu.HBM)
    frac, psf = hbm(shift_frac[0]), hbm(jnp.transpose(psf_taps, (1, 0, 2)))
    acc = pl.pallas_call(
        functools.partial(deposit_kernel, rows),
        in_specs=[any_hbm] * 5,
        out_specs=vmem,
        out_shape=pltpu.VMEM((slabs, tall, cols), jnp.float32),
        scratch_shapes=[
            pltpu.SMEM((blocks,), jnp.int32),
            pltpu.SMEM((blocks,), jnp.int32),
            pltpu.SMEM((1, 1, 1), jnp.int32),
            pltpu.SMEM((3,), jnp.float32),
            pltpu.SMEM((slabs * CZ,), jnp.int32),
            pltpu.VMEM((blocks, planes, rows, cols), jnp.float32),
            pltpu.SemaphoreType.DMA((blocks // CHUNK,)),
            pltpu.SemaphoreType.DMA((4,)),
        ],
        compiler_params=pltpu.CompilerParams(
            vmem_limit_bytes=cell * (blocks * planes * rows + slabs * tall) + room),
        name="deposit",
    )(hbm(destination.reshape(-1)), hbm(offsets.reshape(-1)), background, frac, hbm(camera[0]))

    dma = pltpu.SemaphoreType.DMA
    f32 = jnp.float32
    shapes = [
        (slabs, tall, cols), (slabs, tall, cols), (views, tap_rows, cols),
        (views, 3 * CZ, wide, cols), (3 * CZ, wide, cols), (3 * CZ, wide, cols),
    ]
    late = [
        (views, 3 * CZ, strip + 2 * margin, cols), (views, CZ + 2 * margin, strip + 2 * margin, cols),
        (views, OC, strip + 2 * margin, cols),
        (views, OC, strip + 2 * margin, cols), (views, OC, strip, cols), (CZ, strip, cols),
    ]
    total = sum([functools.reduce(lambda a, b: a * b, s) for s in shapes + late])
    total = total + cols * (slabs * tall + 2 * CZ * rows + views * 4 * cols)
    estimate, joined = pl.pallas_call(
        functools.partial(world_kernel, dims, rows, taps),
        in_specs=[vmem, any_hbm, any_hbm],
        out_specs=(vmem, vmem),
        out_shape=(
            pltpu.VMEM((CZ, rows, cols), f32),
            pltpu.VMEM((1, CZ, rows, cols), f32),
        ),
        scratch_shapes=[pltpu.SMEM((3,), f32), pltpu.VMEM((3, 1, taps), f32), pltpu.VMEM((tap_rows, cols), f32)]
        + [pltpu.VMEM(s, f32) for s in shapes]
        + [pltpu.VMEM((views, 2, 2 * cols, 2 * cols), jnp.bfloat16)]
        + [pltpu.VMEM(s, f32) for s in late]
        + [
            dma((2,)), dma((slabs, NCH)), dma((slabs, NCH)), dma((slabs, NCH)), dma((slabs, NCH)),
            dma((views,)), dma((views,)), dma,
            dma((views, NCH)), dma((views, NCH)), dma((NCH,)), dma((views, NCH)), dma((NCH,)), dma((views, NCH)),
            dma((2, views, NCH)), dma((2, views, NCH)), dma((8, NOUT)), dma((8, NOUT)),
            dma((views, NOUT)), dma((views, NOUT)),
        ],
        compiler_params=pltpu.CompilerParams(
            collective_id=0, has_side_effects=True, vmem_limit_bytes=4 * total + room),
        name="world",
    )(acc, frac, psf)
    return pl.pallas_call(
        store_kernel,
        in_specs=[vmem, vmem],
        out_specs=(pl.BlockSpec(memory_space=pltpu.HBM), pl.BlockSpec(memory_space=pltpu.HBM)),
        out_shape=(jax.ShapeDtypeStruct(estimate.shape, f32), jax.ShapeDtypeStruct(joined.shape, f32)),
        scratch_shapes=[dma((2,))],
        name="store",
    )(pltpu.with_memory_space_constraint(estimate, pltpu.VMEM), pltpu.with_memory_space_constraint(joined, pltpu.VMEM))


def solution(mesh):
    dims = (mesh.shape["gz"], mesh.shape["view"], mesh.shape["gy"])
    return jax.shard_map(
        functools.partial(on_device, dims),
        mesh=mesh,
        in_specs=(
            P("view", ("groups", "gz"), None, "gy", None),
            P("view", "gy", ("groups", "gz")),
            P("view", "gy", ("groups", "gz"), None),
            P("view", "gy", ("groups", "gz")),
            P("view", None),
            P("view", None, None),
        ),
        out_specs=(P(("groups", "gz"), "gy", None), P("view", ("groups", "gz"), "gy", None)),
        check_vma=False,
    )
```

```python
import functools

import jax
import jax.numpy as jnp
from jax import lax
from jax.experimental import pallas as pl
from jax.experimental.pallas import tpu as pltpu
from jax.sharding import PartitionSpec as P

CZ = 8
ITERS = 2
HALO = 8
CHUNK = 4
CP = 2
NCH = CZ // CP
CUTS = (0, 4, CZ)
NOUT = len(CUTS) - 1
MOST = max([b - a for a, b in zip(CUTS, CUTS[1:])])

DATA_FLOOR = 0.25
TINY = 1e-30
MESH = pl.DeviceIdType.MESH


def deposit_kernel(
    rows, dest_in, offs_in, level_in, frac_in, cam_ref, acc_ref,
    dest, offs, level, frac, hits, cam, sems, small,
):
    blocks, planes = cam_ref.shape[:2]
    slabs = acc_ref.shape[0]
    pairs = ((dest_in, dest), (offs_in, offs), (level_in, level), (frac_in, frac))
    copies = [pltpu.make_async_copy(a, b, small.at[n]) for n, (a, b) in enumerate(pairs)]
    for copy in copies:
        copy.start()

    def fetch(c):
        at = pl.ds(c * CHUNK, CHUNK)
        return pltpu.make_async_copy(cam_ref.at[at], cam.at[at], sems.at[c])

    for c in range(blocks // CHUNK):
        fetch(c).start()

    @pl.loop(0, slabs)
    def _(s):
        for p in range(CZ):
            hits[s * CZ + p] = 0
        acc_ref[s] = jnp.zeros(acc_ref.shape[1:], jnp.float32)

    for copy in copies:
        copy.wait()

    fz = frac[0]
    base = level[0, 0, 0].astype(jnp.float32)

    @pl.loop(0, blocks // CHUNK)
    def _(c):
        fetch(c).wait()
        for i in range(CHUNK):
            b = c * CHUNK + i
            s = dest[b]
            o = offs[b]
            mixed = (1.0 - fz) * cam[b, 0 : planes - 1] + (fz * cam[b, 1:planes] - base)
            at = pl.ds(pl.multiple_of(CZ + o * rows, 8), (planes - 1) * rows)
            acc_ref[s, at, :] = acc_ref[s, at, :] + mixed.reshape((planes - 1) * rows, 128)
            for k in range(planes - 1):
                hits[s * CZ + o + k] = hits[s * CZ + o + k] + 1

    @pl.loop(0, slabs, unroll=4)
    def _(s):
        for p in range(CZ):
            acc_ref[s, p : p + 1, :] = jnp.zeros((1, 128), jnp.float32) + hits[s * CZ + p].astype(jnp.float32)


def world_kernel(
    dims, rows, taps,
    acc_ref, frac_in, psf_in, est_ref, joined_ref,
    frac, psf, tap_in, ru, rd, tap_all, jx, e0, e1, kx, xb, rt, za, zb, yb, lg,
    small, us, ur, ds_, dr, tap_s, tap_r, loc_sem, ms, mr, los, lor, his, hir,
    zs, zr, es, er, out_s, out_r,
):
    loads = [pltpu.make_async_copy(a, b, small.at[n]) for n, (a, b) in enumerate(((frac_in, frac), (psf_in, psf)))]
    for load in loads:
        load.start()

    slabs, views, bands = dims
    strip = rows // views
    wide = strip + 2 * HALO
    margin = taps // 2
    z = lax.axis_index("gz")
    v = lax.axis_index("view")
    g = lax.axis_index("gy")
    strips = views * bands
    me = v * bands + g
    band, idx = lax.div(me, views), lax.rem(me, views)

    def dev(zz, vv, gg):
        return {"gz": zz, "view": vv, "gy": gg}

    def place(ss):
        return lax.div(ss, bands), lax.rem(ss, bands)

    around = {ds: place(jnp.clip(me + ds, 0, strips - 1)) for ds in (-1, 0, 1)}
    in_band = [g * views + i for i in range(views)]
    band_sides = (jnp.minimum((g + 1) * views, strips - 1), jnp.maximum(g * views - 1, 0))
    seats = [place(t) for t in in_band + list(band_sides)]

    below, above = z > 0, z < slabs - 1
    left, right = me > 0, me < strips - 1

    barrier = pltpu.get_barrier_semaphore()

    def greet(target):
        pl.semaphore_signal(barrier, inc=1, device_id=target, device_id_type=MESH)

    amount = strips - 1 + below.astype(jnp.int32) + above.astype(jnp.int32)
    for dz, ok in ((1, above), (-1, below)):
        @pl.when(ok)
        def _(dz=dz):
            greet(dev(z + dz, v, g))

    for t in range(strips):
        @pl.when(t != me)
        def _(t=t):
            greet(dev(z, t // bands, t % bands))

    def clear(ref, planes, lo, hi):
        @pl.loop(planes[0], planes[1])
        def _(p):
            ref[p, lo:hi, :] = jnp.zeros((hi - lo, 128), jnp.float32)

    pl.semaphore_wait(barrier, amount)

    def span(c):
        start = 0 if c == 0 else CZ + c * CP * rows
        return pl.ds(start, CZ + (c + 1) * CP * rows - start)

    def up_copy(src, t, c):
        return pltpu.make_async_remote_copy(
            src_ref=src.at[t, span(c)], dst_ref=ru.at[t, span(c)], send_sem=us.at[t, c],
            recv_sem=ur.at[t, c], device_id={"gz": z + 1}, device_id_type=MESH)

    def down_copy(src, t, c):
        return pltpu.make_async_remote_copy(
            src_ref=src.at[t, span(c)], dst_ref=rd.at[t, span(c)], send_sem=ds_.at[t, c],
            recv_sem=dr.at[t, c], device_id={"gz": z - 1}, device_id_type=MESH)

    @pl.when(z == 0)
    def _():
        @pl.loop(0, slabs - 1)
        def _(k):
            for c in range(NCH):
                up_copy(acc_ref, slabs - 1 - k, c).start()

    @pl.when(z == slabs - 1)
    def _():
        @pl.loop(0, slabs - 1)
        def _(k):
            for c in range(NCH):
                down_copy(acc_ref, k, c).start()

    for edge, flow, halo in ((z == 0, ru, (0, CZ)), (z == slabs - 1, rd, (2 * CZ, 3 * CZ))):
        @pl.when(edge)
        def _(flow=flow, halo=halo):
            flow[z] = jnp.zeros(flow.shape[1:], jnp.float32)
            for ref in [e0, e1] + [jx.at[w] for w in range(views)]:
                clear(ref, halo, 0, wide)

    for edge, lo, hi in ((me == 0, 0, HALO), (me == strips - 1, HALO + strip, wide)):
        @pl.when(edge)
        def _(lo=lo, hi=hi):
            clear(e1, (0, 3 * CZ), lo, hi)
            for w in range(views):
                clear(jx.at[w], (CZ, 2 * CZ), lo, hi)

    for load in loads:
        load.wait()

    for axis in range(3):
        scale = jnp.sum(psf[axis], axis=1, keepdims=True)
        share = psf[axis] / scale
        for t in range(taps):
            at = axis * taps + t
            tap_in[at : at + 1, :] = jnp.broadcast_to(share[:, t : t + 1], (1, 128))

    own_tap = pltpu.make_async_copy(tap_in, tap_all.at[v], loc_sem)
    own_tap.start()

    def tap_copy(d):
        return pltpu.make_async_remote_copy(
            src_ref=tap_in, dst_ref=tap_all.at[v], send_sem=tap_s.at[d - 1],
            recv_sem=tap_r.at[d - 1], device_id={"view": (v + d) % views}, device_id_type=MESH)

    for d in range(1, views):
        tap_copy(d).start()

    def pass_on(copy, ref, t, ok):
        @pl.when(ok)
        def _():
            for c in range(NCH):
                at = span(c)
                copy(ref, t, c).wait_recv()
                ref[t, at] = ref[t, at] + acc_ref[t, at]
                copy(ref, t, c).start()

    def pass_up(k):
        t = slabs - 1 - k
        pass_on(up_copy, ru, t, below & (t > z))

    def pass_down(k):
        pass_on(down_copy, rd, k, above & (k < z))

    @pl.loop(0, slabs - 1)
    def _(k):
        low = 2 * z < slabs

        @pl.when(low)
        def _():
            pass_up(k)
            pass_down(k)

        @pl.when(jnp.logical_not(low))
        def _():
            pass_down(k)
            pass_up(k)

    own_tap.wait()
    for d in range(1, views):
        tap_copy(d).wait()

    apart = lax.broadcasted_iota(jnp.int32, (128, 128), 0) - lax.broadcasted_iota(jnp.int32, (128, 128), 1)

    @pl.loop(0, views)
    def _(w):
        ahead = jnp.zeros((128, 128), jnp.float32)
        back = jnp.zeros((128, 128), jnp.float32)
        for t in range(taps):
            tap = tap_all[w, 2 * taps + t : 2 * taps + t + 1, :]
            ahead = jnp.where(apart == t - margin, tap, ahead)
            back = jnp.where(apart == margin - t, tap, back)
        for n, full in enumerate((ahead, back)):
            top = full.astype(jnp.bfloat16)
            kx[w, n, 0:128, 0:128] = top
            kx[w, n, 128:256, 0:128] = top
            kx[w, n, 0:128, 128:256] = (full - top.astype(jnp.float32)).astype(jnp.bfloat16)
            kx[w, n, 128:256, 128:256] = jnp.zeros((128, 128), jnp.bfloat16)

    fy, fx = frac[1], frac[2]
    last_row = lax.broadcasted_iota(jnp.int32, (rows, 128), 0) == rows - 1
    last_col = lax.broadcasted_iota(jnp.int32, (rows, 128), 1) == 127
    joined = joined_ref.at[0]
    mid = pl.ds(CZ, CZ)

    def planes_of(c):
        return pl.ds(c * CP, CP), pl.ds(CZ + c * CP, CP)

    def piece(i):
        lo, hi = max(i * strip - HALO, 0), min((i + 1) * strip + HALO, rows)
        return (lo, hi), (lo - i * strip + HALO, hi - i * strip + HALO)

    low_edge = ((rows - HALO, rows), (0, HALO))
    high_edge = ((0, HALO), (HALO + strip, wide))

    def part_copy(c, w, rows_of, seat, send, recv):
        src_p, dst_p = planes_of(c)
        (lo, hi), (dlo, dhi) = rows_of
        return pltpu.make_async_remote_copy(
            src_ref=joined.at[src_p, pl.ds(lo, hi - lo), :], dst_ref=jx.at[w, dst_p, pl.ds(dlo, dhi - dlo), :],
            send_sem=send, recv_sem=recv, device_id=dev(z, *seat), device_id_type=MESH)

    def sends(c):
        out = []
        for i in range(views):
            out.append((in_band[i], seats[i], z >= 0, piece(i), ms.at[i, c], mr.at[v, c]))
        out.append((band_sides[0], seats[views], g < bands - 1, low_edge, los.at[c], lor.at[v, c]))
        out.append((band_sides[1], seats[views + 1], g > 0, high_edge, his.at[c], hir.at[v, c]))
        return out

    def join(c):
        src_p, _ = planes_of(c)

        @pl.when(below)
        def _():
            up_copy(acc_ref, z, c).wait_recv()

        @pl.when(above)
        def _():
            down_copy(acc_ref, z, c).wait_recv()

        for p in range(c * CP, (c + 1) * CP):
            at = pl.ds(CZ + p * rows, rows)
            total = acc_ref[z, at, :] + ru[z, at, :] + rd[z, at, :]
            cnt = pl.ds(p, 1)
            covered = acc_ref[z, cnt, :] + ru[z, cnt, :] + rd[z, cnt, :]
            follow = jnp.where(last_row, total, pltpu.roll(total, rows - 1, 0))
            total = (1.0 - fy) * total + fy * follow
            follow = jnp.where(last_col, total, pltpu.roll(total, 127, 1))
            total = (1.0 - fx) * total + fx * follow
            joined_ref[0, p] = jnp.maximum(total / (covered + 1.0), DATA_FLOOR)
        for target, seat, ok, rows_of, send, recv in sends(c):
            (lo, hi), (dlo, dhi) = rows_of

            @pl.when(ok & (target != me))
            def _(rows_of=rows_of, seat=seat, send=send, recv=recv):
                part_copy(c, v, rows_of, seat, send, recv).start()

            @pl.when(ok & (target == me))
            def _(lo=lo, hi=hi, dlo=dlo, dhi=dhi):
                for p in range(c * CP, (c + 1) * CP):
                    jx[v, CZ + p, dlo:dhi, :] = joined_ref[0, p, lo:hi, :]

    def z_copy(ref, w, c, up, send, recv):
        dst = (0 if up else 2 * CZ) + c * CP
        src = CZ + c * CP
        a, b = ref.at[pl.ds(src, CP)], ref.at[pl.ds(dst, CP)]
        return pltpu.make_async_remote_copy(
            src_ref=a, dst_ref=b, send_sem=send, recv_sem=recv,
            device_id={"gz": z + 1 if up else z - 1}, device_id_type=MESH)

    def z_copies(c, up):
        side = 1 if up else 0
        near = c * CP >= CZ - margin if up else c * CP < margin
        if near:
            return [z_copy(jx.at[w], w, c, up, zs.at[side, w, c], zr.at[side, w, c]) for w in range(views)]
        return [z_copy(e0, 0, c, up, zs.at[side, 0, c], zr.at[side, 0, c])]

    def average(p):
        total = jx[0, p]
        for w in range(1, views):
            total = total + jx[w, p]
        e0[p] = total / views

    def spread(c):
        for w in range(views):
            for i in range(views):
                @pl.when((idx == i) & ((w != v) | (band != g)))
                def _(i=i, w=w):
                    part_copy(c, w, piece(i), (v, g), ms.at[i, c], mr.at[w, c]).wait_recv()

            @pl.when((idx == 0) & (band > 0) & ((w != v) | (band - 1 != g)))
            def _(w=w):
                part_copy(c, w, low_edge, (v, g), los.at[c], lor.at[w, c]).wait_recv()

            @pl.when((idx == views - 1) & (band < bands - 1) & ((w != v) | (band + 1 != g)))
            def _(w=w):
                part_copy(c, w, high_edge, (v, g), his.at[c], hir.at[w, c]).wait_recv()

        for p in range(c * CP, (c + 1) * CP):
            average(CZ + p)
        for up, ok in ((True, above), (False, below)):
            @pl.when(ok)
            def _(up=up):
                for copy in z_copies(c, up):
                    copy.start()

    planes_r = CZ + 2 * margin
    rows_r = strip + 2 * margin

    def along_x(u, w, n):
        top = u.astype(jnp.bfloat16)
        rest = (u - top.astype(jnp.float32)).astype(jnp.bfloat16)
        both = jnp.dot(jnp.concatenate([top, rest], axis=1), kx[w, n], preferred_element_type=jnp.float32)
        return both[:, 0:128] + both[:, 128:256]

    def weighted(terms, weights):
        total = weights[0] * terms[0]
        for term, weight in zip(terms[1:], weights[1:]):
            total = total + weight * term
        return total

    def root(terms):
        if len(terms) == 1:
            return terms[0]
        if len(terms) % 2:
            total = jnp.log(terms[0])
            for term in terms[1:]:
                total = total + jnp.log(term)
            return jnp.exp(total / len(terms))
        return root([jnp.sqrt(a * b) for a, b in zip(terms[0::2], terms[1::2])])

    def tap(w, axis, t):
        at = axis * taps + t
        return tap_all[w, at : at + 1, :]

    def blur_rows(est, first, size):
        for p in range(size):
            terms = [est[first + p, t : t + rows_r, :] for t in range(taps)]
            for w in range(views):
                zb[w, p] = weighted(terms, [tap(w, 1, t) for t in range(taps)])
        for w in range(views):
            mixed = along_x(zb[w, 0:size].reshape(size * rows_r, 128), w, 0)
            xb[w, pl.ds(first, size)] = mixed.reshape(size, rows_r, 128)

    def ratios(r, at, w, lo, hi):
        base = CZ - 2 * margin
        column = [xb[w, base + p, at, :] for p in range(lo, hi + 2 * margin)]
        out = []
        for p in range(lo, hi):
            blurred = weighted(column[p - lo : p - lo + taps], [tap(w, 0, t) for t in range(taps)])
            blurred = jnp.maximum(blurred, TINY)
            inverse = pl.reciprocal(blurred, approx=True)
            inverse = inverse * (2.0 - blurred * inverse)
            out.append(jx[w, CZ - margin + p, pl.ds(r * 8 + HALO - margin, 8), :] * inverse)
        return out

    def correct(est, emit):
        for c in range(NOUT):
            low, high = CUTS[c], CUTS[c + 1]
            size = high - low
            done = low + 2 * margin if c > 0 else 0
            stop = high + 2 * margin

            @pl.loop(0, rows_r // 8, unroll=True)
            def _(r, low=low, high=high, done=done, stop=stop):
                at = pl.ds(pl.multiple_of(r * 8, 8), 8)
                for w in range(views):
                    ratio = [rt[w, p, at, :] for p in range(low, done)] + ratios(r, at, w, done, stop)
                    if high < CZ:
                        for p in range(max(high, done), stop):
                            rt[w, p, at, :] = ratio[p - low]
                    for p in range(high - low):
                        za[w, p, at, :] = weighted(ratio[p : p + taps], [tap(w, 0, taps - 1 - t) for t in range(taps)])

            factors = []
            for w in range(views):
                for p in range(size):
                    yb[w, p] = weighted([za[w, p, t : t + strip, :] for t in range(taps)],
                                        [tap(w, 1, taps - 1 - t) for t in range(taps)])
                factors.append(along_x(yb[w, 0:size].reshape(size * strip, 128), w, 1).reshape(size, strip, 128))
            emit(c, est[pl.ds(CZ + low, size), HALO : HALO + strip, :] * root(factors))

    def cut(c):
        return pl.ds(CUTS[c], CUTS[c + 1] - CUTS[c])

    join(0)
    for c in range(1, NCH):
        join(c)
        spread(c - 1)
    for c in range(0, NCH - 1):
        blur_rows(e0, CZ + c * CP, CP)
    spread(NCH - 1)
    blur_rows(e0, 2 * CZ - CP, CP)

    for c in range(NCH):
        for up, ok in ((True, below), (False, above)):
            @pl.when(ok)
            def _(up=up, c=c):
                copies = z_copies(c, up)
                for copy in copies:
                    copy.wait_recv()
                if len(copies) == views and views > 1:
                    for p in range(c * CP, (c + 1) * CP):
                        average((0 if up else 2 * CZ) + p)

            blur_rows(e0, (0 if up else 2 * CZ) + c * CP, CP)

    inner = pl.ds(HALO, strip)
    near = []
    for n, (dz, ds) in enumerate([(a, b) for b in (-1, 1) for a in (-1, 1)] + [(-1, 0), (1, 0), (0, -1), (0, 1)]):
        zok = {-1: below, 0: z >= 0, 1: above}[dz]
        sok = {-1: left, 0: z >= 0, 1: right}[ds]
        far_z = {-1: above, 0: z >= 0, 1: below}[dz]
        far_s = {-1: right, 0: z >= 0, 1: left}[ds]
        near.append((n, dz, ds, zok & sok, far_z & far_s))

    def near_copy(n, dz, ds, c):
        src_r = {-1: pl.ds(HALO, HALO), 0: inner, 1: pl.ds(strip, HALO)}[ds]
        dst_r = {-1: pl.ds(HALO + strip, HALO), 0: inner, 1: pl.ds(0, HALO)}[ds]
        dst = CZ - dz * CZ + CUTS[c]
        size = CUTS[c + 1] - CUTS[c]
        return pltpu.make_async_remote_copy(
            src_ref=e1.at[pl.ds(CZ + CUTS[c], size), src_r, :], dst_ref=e1.at[pl.ds(dst, size), dst_r, :],
            send_sem=es.at[n, c], recv_sem=er.at[n, c], device_id=dev(z + dz, *around[ds]), device_id_type=MESH)

    def emit_step(c, new):
        e1[pl.ds(CZ + CUTS[c], CUTS[c + 1] - CUTS[c]), HALO : HALO + strip, :] = new
        for n, dz, ds, ok, _ in near:
            @pl.when(ok)
            def _(n=n, dz=dz, ds=ds):
                near_copy(n, dz, ds, c).start()

    correct(e0, emit_step)

    @pl.loop(0, slabs)
    def _(t):
        for c in range(NCH):
            @pl.when(t > z)
            def _():
                up_copy(acc_ref, t, c).wait_send()

            @pl.when(t < z)
            def _():
                down_copy(acc_ref, t, c).wait_send()

    for c in range(NCH):
        for target, seat, ok, rows_of, send, recv in sends(c):
            @pl.when(ok & (target != me))
            def _(rows_of=rows_of, seat=seat, send=send, recv=recv, c=c):
                part_copy(c, v, rows_of, seat, send, recv).wait_send()

        for up, ok in ((True, above), (False, below)):
            @pl.when(ok)
            def _(up=up, c=c):
                for copy in z_copies(c, up):
                    copy.wait_send()

    def near_wait(c, way):
        for n, dz, ds, _, ok in near:
            if dz == way:
                @pl.when(ok)
                def _(n=n, dz=dz, ds=ds):
                    near_copy(n, dz, ds, c).wait_recv()

    for c in range(NOUT):
        near_wait(c, 0)
        blur_rows(e1, CZ + CUTS[c], CUTS[c + 1] - CUTS[c])
    for c in range(NOUT):
        for way in (1, -1):
            near_wait(c, way)
            blur_rows(e1, CZ - way * CZ + CUTS[c], CUTS[c + 1] - CUTS[c])

    def out_copy(c, w, target_g, i):
        at = pl.ds(pl.multiple_of(i * strip, 8), strip)
        part = cut(c)
        return pltpu.make_async_remote_copy(
            src_ref=lg.at[part], dst_ref=est_ref.at[part, at, :], send_sem=out_s.at[w, c],
            recv_sem=out_r.at[i, c], device_id=dev(z, w, target_g), device_id_type=MESH)

    def emit_last(c, new):
        lg[cut(c)] = new
        for w in range(views):
            away = (w != v) | (band != g)

            @pl.when(away)
            def _(w=w):
                out_copy(c, w, band, idx).start()

            @pl.when(jnp.logical_not(away))
            def _():
                est_ref[cut(c), pl.ds(pl.multiple_of(idx * strip, 8), strip), :] = new

    correct(e1, emit_last)

    for c in range(NOUT):
        for n, dz, ds, ok, _ in near:
            @pl.when(ok)
            def _(n=n, dz=dz, ds=ds, c=c):
                near_copy(n, dz, ds, c).wait_send()

    for c in range(NOUT):
        for i in range(views):
            @pl.when(g * views + i != me)
            def _(i=i, c=c):
                out_copy(c, 0, g, i).wait_recv()

    for c in range(NOUT):
        for w in range(views):
            @pl.when((w != v) | (band != g))
            def _(w=w, c=c):
                out_copy(c, w, band, idx).wait_send()


def store_kernel(est_in, joined_in, est_out, joined_out, sems):
    copies = [pltpu.make_async_copy(a, b, sems.at[n]) for n, (a, b) in enumerate(((est_in, est_out), (joined_in, joined_out)))]
    for copy in copies:
        copy.start()
    for copy in copies:
        copy.wait()


def on_device(dims, camera, background, destination, offsets, shift_frac, psf_taps):
    slabs, views, bands = dims
    blocks, planes, rows, cols = camera.shape[1:]
    taps = psf_taps.shape[-1]
    margin = taps // 2
    tall = CZ * rows + CZ
    strip = rows // views
    wide = strip + 2 * HALO
    tap_rows = -(-3 * taps // 8) * 8
    vmem = pl.BlockSpec(memory_space=pltpu.VMEM)
    hbm = functools.partial(pltpu.with_memory_space_constraint, memory_space=pltpu.HBM)
    cell = 4 * cols
    room = 2 * 1024 * 1024
    any_hbm = pl.BlockSpec(memory_space=pltpu.HBM)
    frac, psf = hbm(shift_frac[0]), hbm(jnp.transpose(psf_taps, (1, 0, 2)))
    acc = pl.pallas_call(
        functools.partial(deposit_kernel, rows),
        in_specs=[any_hbm] * 5,
        out_specs=vmem,
        out_shape=pltpu.VMEM((slabs, tall, cols), jnp.float32),
        scratch_shapes=[
            pltpu.SMEM((blocks,), jnp.int32),
            pltpu.SMEM((blocks,), jnp.int32),
            pltpu.SMEM((1, 1, 1), jnp.int32),
            pltpu.SMEM((3,), jnp.float32),
            pltpu.SMEM((slabs * CZ,), jnp.int32),
            pltpu.VMEM((blocks, planes, rows, cols), jnp.float32),
            pltpu.SemaphoreType.DMA((blocks // CHUNK,)),
            pltpu.SemaphoreType.DMA((4,)),
        ],
        compiler_params=pltpu.CompilerParams(
            vmem_limit_bytes=cell * (blocks * planes * rows + slabs * tall) + room),
        name="deposit",
    )(hbm(destination.reshape(-1)), hbm(offsets.reshape(-1)), background, frac, hbm(camera[0]))

    dma = pltpu.SemaphoreType.DMA
    f32 = jnp.float32
    shapes = [
        (slabs, tall, cols), (slabs, tall, cols), (views, tap_rows, cols),
        (views, 3 * CZ, wide, cols), (3 * CZ, wide, cols), (3 * CZ, wide, cols),
    ]
    late = [
        (views, 3 * CZ, strip + 2 * margin, cols), (views, CZ + 2 * margin, strip + 2 * margin, cols),
        (views, MOST, strip + 2 * margin, cols),
        (views, MOST, strip + 2 * margin, cols), (views, MOST, strip, cols), (CZ, strip, cols),
    ]
    total = sum([functools.reduce(lambda a, b: a * b, s) for s in shapes + late])
    total = total + cols * (slabs * tall + 2 * CZ * rows + views * 4 * cols)
    estimate, joined = pl.pallas_call(
        functools.partial(world_kernel, dims, rows, taps),
        in_specs=[vmem, any_hbm, any_hbm],
        out_specs=(vmem, vmem),
        out_shape=(
            pltpu.VMEM((CZ, rows, cols), f32),
            pltpu.VMEM((1, CZ, rows, cols), f32),
        ),
        scratch_shapes=[pltpu.SMEM((3,), f32), pltpu.VMEM((3, 1, taps), f32), pltpu.VMEM((tap_rows, cols), f32)]
        + [pltpu.VMEM(s, f32) for s in shapes]
        + [pltpu.VMEM((views, 2, 2 * cols, 2 * cols), jnp.bfloat16)]
        + [pltpu.VMEM(s, f32) for s in late]
        + [
            dma((2,)), dma((slabs, NCH)), dma((slabs, NCH)), dma((slabs, NCH)), dma((slabs, NCH)),
            dma((views,)), dma((views,)), dma,
            dma((views, NCH)), dma((views, NCH)), dma((NCH,)), dma((views, NCH)), dma((NCH,)), dma((views, NCH)),
            dma((2, views, NCH)), dma((2, views, NCH)), dma((8, NOUT)), dma((8, NOUT)),
            dma((views, NOUT)), dma((views, NOUT)),
        ],
        compiler_params=pltpu.CompilerParams(
            collective_id=0, has_side_effects=True, vmem_limit_bytes=4 * total + room),
        name="world",
    )(acc, frac, psf)
    return pl.pallas_call(
        store_kernel,
        in_specs=[vmem, vmem],
        out_specs=(pl.BlockSpec(memory_space=pltpu.HBM), pl.BlockSpec(memory_space=pltpu.HBM)),
        out_shape=(jax.ShapeDtypeStruct(estimate.shape, f32), jax.ShapeDtypeStruct(joined.shape, f32)),
        scratch_shapes=[dma((2,))],
        name="store",
    )(pltpu.with_memory_space_constraint(estimate, pltpu.VMEM), pltpu.with_memory_space_constraint(joined, pltpu.VMEM))


def solution(mesh):
    dims = (mesh.shape["gz"], mesh.shape["view"], mesh.shape["gy"])
    return jax.shard_map(
        functools.partial(on_device, dims),
        mesh=mesh,
        in_specs=(
            P("view", ("groups", "gz"), None, "gy", None),
            P("view", "gy", ("groups", "gz")),
            P("view", "gy", ("groups", "gz"), None),
            P("view", "gy", ("groups", "gz")),
            P("view", None),
            P("view", None, None),
        ),
        out_specs=(P(("groups", "gz"), "gy", None), P("view", ("groups", "gz"), "gy", None)),
        check_vma=False,
    )
```

```python
import functools

import jax
import jax.numpy as jnp
from jax import lax
from jax.experimental import pallas as pl
from jax.experimental.pallas import tpu as pltpu
from jax.sharding import PartitionSpec as P

CZ = 8
ITERS = 2
HALO = 8
CHUNK = 4
CP = 2
NCH = CZ // CP
CUTS = (0, 4, CZ)
NOUT = len(CUTS) - 1
MOST = max([b - a for a, b in zip(CUTS, CUTS[1:])])

DATA_FLOOR = 0.25
TINY = 1e-30
MESH = pl.DeviceIdType.MESH


def deposit_kernel(
    rows, dest_in, offs_in, level_in, frac_in, cam_ref, acc_ref,
    dest, offs, level, frac, hits, cam, sems, small,
):
    blocks, planes = cam_ref.shape[:2]
    slabs = acc_ref.shape[0]
    pairs = ((dest_in, dest), (offs_in, offs), (level_in, level), (frac_in, frac))
    copies = [pltpu.make_async_copy(a, b, small.at[n]) for n, (a, b) in enumerate(pairs)]
    for copy in copies:
        copy.start()

    def fetch(c):
        at = pl.ds(c * CHUNK, CHUNK)
        return pltpu.make_async_copy(cam_ref.at[at], cam.at[at], sems.at[c])

    for c in range(blocks // CHUNK):
        fetch(c).start()

    @pl.loop(0, slabs)
    def _(s):
        for p in range(CZ):
            hits[s * CZ + p] = 0
        acc_ref[s] = jnp.zeros(acc_ref.shape[1:], jnp.float32)

    for copy in copies:
        copy.wait()

    fz = frac[0]
    base = level[0, 0, 0].astype(jnp.float32)

    @pl.loop(0, blocks // CHUNK)
    def _(c):
        fetch(c).wait()
        for i in range(CHUNK):
            b = c * CHUNK + i
            s = dest[b]
            o = offs[b]
            mixed = (1.0 - fz) * cam[b, 0 : planes - 1] + (fz * cam[b, 1:planes] - base)
            at = pl.ds(pl.multiple_of(CZ + o * rows, 8), (planes - 1) * rows)
            acc_ref[s, at, :] = acc_ref[s, at, :] + mixed.reshape((planes - 1) * rows, 128)
            for k in range(planes - 1):
                hits[s * CZ + o + k] = hits[s * CZ + o + k] + 1

    @pl.loop(0, slabs, unroll=4)
    def _(s):
        for p in range(CZ):
            acc_ref[s, p : p + 1, :] = jnp.zeros((1, 128), jnp.float32) + hits[s * CZ + p].astype(jnp.float32)


def world_kernel(
    dims, rows, taps,
    acc_ref, frac_in, psf_in, est_ref, joined_ref,
    frac, psf, tap_in, ru, rd, tap_all, jx, e0, e1, kx, xb, rt, za, zb, yb, lg,
    small, us, ur, ds_, dr, tap_s, tap_r, loc_sem, ms, mr, los, lor, his, hir,
    zs, zr, es, er, out_s, out_r,
):
    loads = [pltpu.make_async_copy(a, b, small.at[n]) for n, (a, b) in enumerate(((frac_in, frac), (psf_in, psf)))]
    for load in loads:
        load.start()

    slabs, views, bands = dims
    strip = rows // views
    wide = strip + 2 * HALO
    margin = taps // 2
    z = lax.axis_index("gz")
    v = lax.axis_index("view")
    g = lax.axis_index("gy")
    strips = views * bands
    me = v * bands + g
    band, idx = lax.div(me, views), lax.rem(me, views)

    def dev(zz, vv, gg):
        return {"gz": zz, "view": vv, "gy": gg}

    def place(ss):
        return lax.div(ss, bands), lax.rem(ss, bands)

    around = {ds: place(jnp.clip(me + ds, 0, strips - 1)) for ds in (-1, 0, 1)}
    in_band = [g * views + i for i in range(views)]
    band_sides = (jnp.minimum((g + 1) * views, strips - 1), jnp.maximum(g * views - 1, 0))
    seats = [place(t) for t in in_band + list(band_sides)]

    below, above = z > 0, z < slabs - 1
    left, right = me > 0, me < strips - 1

    barrier = pltpu.get_barrier_semaphore()

    def greet(target):
        pl.semaphore_signal(barrier, inc=1, device_id=target, device_id_type=MESH)

    amount = strips - 1 + below.astype(jnp.int32) + above.astype(jnp.int32)
    for dz, ok in ((1, above), (-1, below)):
        @pl.when(ok)
        def _(dz=dz):
            greet(dev(z + dz, v, g))

    for t in range(strips):
        @pl.when(t != me)
        def _(t=t):
            greet(dev(z, t // bands, t % bands))

    def clear(ref, planes, lo, hi):
        @pl.loop(planes[0], planes[1])
        def _(p):
            ref[p, lo:hi, :] = jnp.zeros((hi - lo, 128), jnp.float32)

    pl.semaphore_wait(barrier, amount)

    def span(c):
        start = 0 if c == 0 else CZ + c * CP * rows
        return pl.ds(start, CZ + (c + 1) * CP * rows - start)

    def up_copy(src, t, c):
        return pltpu.make_async_remote_copy(
            src_ref=src.at[t, span(c)], dst_ref=ru.at[t, span(c)], send_sem=us.at[t, c],
            recv_sem=ur.at[t, c], device_id={"gz": z + 1}, device_id_type=MESH)

    def down_copy(src, t, c):
        return pltpu.make_async_remote_copy(
            src_ref=src.at[t, span(c)], dst_ref=rd.at[t, span(c)], send_sem=ds_.at[t, c],
            recv_sem=dr.at[t, c], device_id={"gz": z - 1}, device_id_type=MESH)

    @pl.when(z == 0)
    def _():
        @pl.loop(0, slabs - 1)
        def _(k):
            for c in range(NCH):
                up_copy(acc_ref, slabs - 1 - k, c).start()

    @pl.when(z == slabs - 1)
    def _():
        @pl.loop(0, slabs - 1)
        def _(k):
            for c in range(NCH):
                down_copy(acc_ref, k, c).start()

    for edge, flow, halo in ((z == 0, ru, (0, CZ)), (z == slabs - 1, rd, (2 * CZ, 3 * CZ))):
        @pl.when(edge)
        def _(flow=flow, halo=halo):
            flow[z] = jnp.zeros(flow.shape[1:], jnp.float32)
            for ref in [e0, e1] + [jx.at[w] for w in range(views)]:
                clear(ref, halo, 0, wide)

    for edge, lo, hi in ((me == 0, 0, HALO), (me == strips - 1, HALO + strip, wide)):
        @pl.when(edge)
        def _(lo=lo, hi=hi):
            clear(e1, (0, 3 * CZ), lo, hi)
            for w in range(views):
                clear(jx.at[w], (CZ, 2 * CZ), lo, hi)

    for load in loads:
        load.wait()

    for axis in range(3):
        scale = jnp.sum(psf[axis], axis=1, keepdims=True)
        share = psf[axis] / scale
        for t in range(taps):
            at = axis * taps + t
            tap_in[at : at + 1, :] = jnp.broadcast_to(share[:, t : t + 1], (1, 128))

    own_tap = pltpu.make_async_copy(tap_in, tap_all.at[v], loc_sem)
    own_tap.start()

    def tap_copy(d):
        return pltpu.make_async_remote_copy(
            src_ref=tap_in, dst_ref=tap_all.at[v], send_sem=tap_s.at[d - 1],
            recv_sem=tap_r.at[d - 1], device_id={"view": (v + d) % views}, device_id_type=MESH)

    for d in range(1, views):
        tap_copy(d).start()

    def pass_on(copy, ref, t, ok):
        @pl.when(ok)
        def _():
            for c in range(NCH):
                at = span(c)
                copy(ref, t, c).wait_recv()
                ref[t, at] = ref[t, at] + acc_ref[t, at]
                copy(ref, t, c).start()

    def pass_up(k):
        t = slabs - 1 - k
        pass_on(up_copy, ru, t, below & (t > z))

    def pass_down(k):
        pass_on(down_copy, rd, k, above & (k < z))

    @pl.loop(0, slabs - 1)
    def _(k):
        low = 2 * z < slabs

        @pl.when(low)
        def _():
            pass_up(k)
            pass_down(k)

        @pl.when(jnp.logical_not(low))
        def _():
            pass_down(k)
            pass_up(k)

    own_tap.wait()
    for d in range(1, views):
        tap_copy(d).wait()

    apart = lax.broadcasted_iota(jnp.int32, (128, 128), 0) - lax.broadcasted_iota(jnp.int32, (128, 128), 1)

    @pl.loop(0, views)
    def _(w):
        ahead = jnp.zeros((128, 128), jnp.float32)
        back = jnp.zeros((128, 128), jnp.float32)
        for t in range(taps):
            tap = tap_all[w, 2 * taps + t : 2 * taps + t + 1, :]
            ahead = jnp.where(apart == t - margin, tap, ahead)
            back = jnp.where(apart == margin - t, tap, back)
        for n, full in enumerate((ahead, back)):
            top = full.astype(jnp.bfloat16)
            kx[w, n, 0:128, 0:128] = top
            kx[w, n, 128:256, 0:128] = top
            kx[w, n, 0:128, 128:256] = (full - top.astype(jnp.float32)).astype(jnp.bfloat16)
            kx[w, n, 128:256, 128:256] = jnp.zeros((128, 128), jnp.bfloat16)

    fy, fx = frac[1], frac[2]
    last_row = lax.broadcasted_iota(jnp.int32, (rows, 128), 0) == rows - 1
    last_col = lax.broadcasted_iota(jnp.int32, (rows, 128), 1) == 127
    joined = joined_ref.at[0]
    mid = pl.ds(CZ, CZ)

    def planes_of(c):
        return pl.ds(c * CP, CP), pl.ds(CZ + c * CP, CP)

    def piece(i):
        lo, hi = max(i * strip - HALO, 0), min((i + 1) * strip + HALO, rows)
        return (lo, hi), (lo - i * strip + HALO, hi - i * strip + HALO)

    low_edge = ((rows - HALO, rows), (0, HALO))
    high_edge = ((0, HALO), (HALO + strip, wide))

    def part_copy(c, w, rows_of, seat, send, recv):
        src_p, dst_p = planes_of(c)
        (lo, hi), (dlo, dhi) = rows_of
        return pltpu.make_async_remote_copy(
            src_ref=joined.at[src_p, pl.ds(lo, hi - lo), :], dst_ref=jx.at[w, dst_p, pl.ds(dlo, dhi - dlo), :],
            send_sem=send, recv_sem=recv, device_id=dev(z, *seat), device_id_type=MESH)

    def sends(c):
        out = []
        for i in range(views):
            out.append((in_band[i], seats[i], z >= 0, piece(i), ms.at[i, c], mr.at[v, c]))
        out.append((band_sides[0], seats[views], g < bands - 1, low_edge, los.at[c], lor.at[v, c]))
        out.append((band_sides[1], seats[views + 1], g > 0, high_edge, his.at[c], hir.at[v, c]))
        return out

    def join(c):
        src_p, _ = planes_of(c)

        @pl.when(below)
        def _():
            up_copy(acc_ref, z, c).wait_recv()

        @pl.when(above)
        def _():
            down_copy(acc_ref, z, c).wait_recv()

        for p in range(c * CP, (c + 1) * CP):
            at = pl.ds(CZ + p * rows, rows)
            total = acc_ref[z, at, :] + ru[z, at, :] + rd[z, at, :]
            cnt = pl.ds(p, 1)
            covered = acc_ref[z, cnt, :] + ru[z, cnt, :] + rd[z, cnt, :]
            follow = jnp.where(last_row, total, pltpu.roll(total, rows - 1, 0))
            total = (1.0 - fy) * total + fy * follow
            follow = jnp.where(last_col, total, pltpu.roll(total, 127, 1))
            total = (1.0 - fx) * total + fx * follow
            joined_ref[0, p] = jnp.maximum(total / (covered + 1.0), DATA_FLOOR)
        for target, seat, ok, rows_of, send, recv in sends(c):
            (lo, hi), (dlo, dhi) = rows_of

            @pl.when(ok & (target != me))
            def _(rows_of=rows_of, seat=seat, send=send, recv=recv):
                part_copy(c, v, rows_of, seat, send, recv).start()

            @pl.when(ok & (target == me))
            def _(lo=lo, hi=hi, dlo=dlo, dhi=dhi):
                for p in range(c * CP, (c + 1) * CP):
                    jx[v, CZ + p, dlo:dhi, :] = joined_ref[0, p, lo:hi, :]

    def z_copy(ref, w, c, up, send, recv):
        dst = (0 if up else 2 * CZ) + c * CP
        src = CZ + c * CP
        a, b = ref.at[pl.ds(src, CP)], ref.at[pl.ds(dst, CP)]
        return pltpu.make_async_remote_copy(
            src_ref=a, dst_ref=b, send_sem=send, recv_sem=recv,
            device_id={"gz": z + 1 if up else z - 1}, device_id_type=MESH)

    def z_copies(c, up):
        side = 1 if up else 0
        near = c * CP >= CZ - margin if up else c * CP < margin
        if near:
            return [z_copy(jx.at[w], w, c, up, zs.at[side, w, c], zr.at[side, w, c]) for w in range(views)]
        return [z_copy(e0, 0, c, up, zs.at[side, 0, c], zr.at[side, 0, c])]

    def average(p):
        total = jx[0, p]
        for w in range(1, views):
            total = total + jx[w, p]
        e0[p] = total / views

    def spread(c):
        for w in range(views):
            for i in range(views):
                @pl.when((idx == i) & ((w != v) | (band != g)))
                def _(i=i, w=w):
                    part_copy(c, w, piece(i), (v, g), ms.at[i, c], mr.at[w, c]).wait_recv()

            @pl.when((idx == 0) & (band > 0) & ((w != v) | (band - 1 != g)))
            def _(w=w):
                part_copy(c, w, low_edge, (v, g), los.at[c], lor.at[w, c]).wait_recv()

            @pl.when((idx == views - 1) & (band < bands - 1) & ((w != v) | (band + 1 != g)))
            def _(w=w):
                part_copy(c, w, high_edge, (v, g), his.at[c], hir.at[w, c]).wait_recv()

        for p in range(c * CP, (c + 1) * CP):
            average(CZ + p)
        for up, ok in ((False, below), (True, above)):
            @pl.when(ok)
            def _(up=up):
                for copy in z_copies(c, up):
                    copy.start()

    planes_r = CZ + 2 * margin
    rows_r = strip + 2 * margin

    def along_x(u, w, n):
        top = u.astype(jnp.bfloat16)
        rest = (u - top.astype(jnp.float32)).astype(jnp.bfloat16)
        both = jnp.dot(jnp.concatenate([top, rest], axis=1), kx[w, n], preferred_element_type=jnp.float32)
        return both[:, 0:128] + both[:, 128:256]

    def weighted(terms, weights):
        total = weights[0] * terms[0]
        for term, weight in zip(terms[1:], weights[1:]):
            total = total + weight * term
        return total

    def root(terms):
        if len(terms) == 1:
            return terms[0]
        if len(terms) % 2:
            total = jnp.log(terms[0])
            for term in terms[1:]:
                total = total + jnp.log(term)
            return jnp.exp(total / len(terms))
        return root([jnp.sqrt(a * b) for a, b in zip(terms[0::2], terms[1::2])])

    def tap(w, axis, t):
        at = axis * taps + t
        return tap_all[w, at : at + 1, :]

    def blur_rows(est, first, size):
        for p in range(size):
            terms = [est[first + p, t : t + rows_r, :] for t in range(taps)]
            for w in range(views):
                zb[w, p] = weighted(terms, [tap(w, 1, t) for t in range(taps)])
        for w in range(views):
            mixed = along_x(zb[w, 0:size].reshape(size * rows_r, 128), w, 0)
            xb[w, pl.ds(first, size)] = mixed.reshape(size, rows_r, 128)

    def ratios(r, at, w, lo, hi):
        base = CZ - 2 * margin
        column = [xb[w, base + p, at, :] for p in range(lo, hi + 2 * margin)]
        out = []
        for p in range(lo, hi):
            blurred = weighted(column[p - lo : p - lo + taps], [tap(w, 0, t) for t in range(taps)])
            blurred = jnp.maximum(blurred, TINY)
            inverse = pl.reciprocal(blurred, approx=True)
            inverse = inverse * (2.0 - blurred * inverse)
            out.append(jx[w, CZ - margin + p, pl.ds(r * 8 + HALO - margin, 8), :] * inverse)
        return out

    def correct(est, emit):
        for c in range(NOUT):
            low, high = CUTS[c], CUTS[c + 1]
            size = high - low
            done = low + 2 * margin if c > 0 else 0
            stop = high + 2 * margin

            @pl.loop(0, rows_r // 8, unroll=True)
            def _(r, low=low, high=high, done=done, stop=stop):
                at = pl.ds(pl.multiple_of(r * 8, 8), 8)
                for w in range(views):
                    ratio = [rt[w, p, at, :] for p in range(low, done)] + ratios(r, at, w, done, stop)
                    if high < CZ:
                        for p in range(max(high, done), stop):
                            rt[w, p, at, :] = ratio[p - low]
                    for p in range(high - low):
                        za[w, p, at, :] = weighted(ratio[p : p + taps], [tap(w, 0, taps - 1 - t) for t in range(taps)])

            factors = []
            for w in range(views):
                for p in range(size):
                    yb[w, p] = weighted([za[w, p, t : t + strip, :] for t in range(taps)],
                                        [tap(w, 1, taps - 1 - t) for t in range(taps)])
                factors.append(along_x(yb[w, 0:size].reshape(size * strip, 128), w, 1).reshape(size, strip, 128))
            emit(c, est[pl.ds(CZ + low, size), HALO : HALO + strip, :] * root(factors))

    def cut(c):
        return pl.ds(CUTS[c], CUTS[c + 1] - CUTS[c])

    join(0)
    for c in range(1, NCH):
        join(c)
        spread(c - 1)
    for c in range(0, NCH - 1):
        blur_rows(e0, CZ + c * CP, CP)
    spread(NCH - 1)
    blur_rows(e0, 2 * CZ - CP, CP)

    for c in range(NCH):
        for up, ok in ((True, below), (False, above)):
            @pl.when(ok)
            def _(up=up, c=c):
                copies = z_copies(c, up)
                for copy in copies:
                    copy.wait_recv()
                if len(copies) == views and views > 1:
                    for p in range(c * CP, (c + 1) * CP):
                        average((0 if up else 2 * CZ) + p)

            blur_rows(e0, (0 if up else 2 * CZ) + c * CP, CP)

    inner = pl.ds(HALO, strip)
    near = []
    for n, (dz, ds) in enumerate([(a, b) for b in (-1, 1) for a in (-1, 1)] + [(-1, 0), (1, 0), (0, -1), (0, 1)]):
        zok = {-1: below, 0: z >= 0, 1: above}[dz]
        sok = {-1: left, 0: z >= 0, 1: right}[ds]
        far_z = {-1: above, 0: z >= 0, 1: below}[dz]
        far_s = {-1: right, 0: z >= 0, 1: left}[ds]
        near.append((n, dz, ds, zok & sok, far_z & far_s))

    def near_copy(n, dz, ds, c):
        src_r = {-1: pl.ds(HALO, HALO), 0: inner, 1: pl.ds(strip, HALO)}[ds]
        dst_r = {-1: pl.ds(HALO + strip, HALO), 0: inner, 1: pl.ds(0, HALO)}[ds]
        dst = CZ - dz * CZ + CUTS[c]
        size = CUTS[c + 1] - CUTS[c]
        return pltpu.make_async_remote_copy(
            src_ref=e1.at[pl.ds(CZ + CUTS[c], size), src_r, :], dst_ref=e1.at[pl.ds(dst, size), dst_r, :],
            send_sem=es.at[n, c], recv_sem=er.at[n, c], device_id=dev(z + dz, *around[ds]), device_id_type=MESH)

    def emit_step(c, new):
        e1[pl.ds(CZ + CUTS[c], CUTS[c + 1] - CUTS[c]), HALO : HALO + strip, :] = new
        for n, dz, ds, ok, _ in near:
            @pl.when(ok)
            def _(n=n, dz=dz, ds=ds):
                near_copy(n, dz, ds, c).start()

    correct(e0, emit_step)

    @pl.loop(0, slabs)
    def _(t):
        for c in range(NCH):
            @pl.when(t > z)
            def _():
                up_copy(acc_ref, t, c).wait_send()

            @pl.when(t < z)
            def _():
                down_copy(acc_ref, t, c).wait_send()

    for c in range(NCH):
        for target, seat, ok, rows_of, send, recv in sends(c):
            @pl.when(ok & (target != me))
            def _(rows_of=rows_of, seat=seat, send=send, recv=recv, c=c):
                part_copy(c, v, rows_of, seat, send, recv).wait_send()

        for up, ok in ((True, above), (False, below)):
            @pl.when(ok)
            def _(up=up, c=c):
                for copy in z_copies(c, up):
                    copy.wait_send()

    def near_wait(c, way):
        for n, dz, ds, _, ok in near:
            if dz == way:
                @pl.when(ok)
                def _(n=n, dz=dz, ds=ds):
                    near_copy(n, dz, ds, c).wait_recv()

    for c in range(NOUT):
        near_wait(c, 0)
        blur_rows(e1, CZ + CUTS[c], CUTS[c + 1] - CUTS[c])
    for c in range(NOUT):
        for way in (1, -1):
            near_wait(c, way)
            blur_rows(e1, CZ - way * CZ + CUTS[c], CUTS[c + 1] - CUTS[c])

    def out_copy(c, w, target_g, i):
        at = pl.ds(pl.multiple_of(i * strip, 8), strip)
        part = cut(c)
        return pltpu.make_async_remote_copy(
            src_ref=lg.at[part], dst_ref=est_ref.at[part, at, :], send_sem=out_s.at[w, c],
            recv_sem=out_r.at[i, c], device_id=dev(z, w, target_g), device_id_type=MESH)

    def emit_last(c, new):
        lg[cut(c)] = new
        for w in range(views):
            away = (w != v) | (band != g)

            @pl.when(away)
            def _(w=w):
                out_copy(c, w, band, idx).start()

            @pl.when(jnp.logical_not(away))
            def _():
                est_ref[cut(c), pl.ds(pl.multiple_of(idx * strip, 8), strip), :] = new

    correct(e1, emit_last)

    for c in range(NOUT):
        for n, dz, ds, ok, _ in near:
            @pl.when(ok)
            def _(n=n, dz=dz, ds=ds, c=c):
                near_copy(n, dz, ds, c).wait_send()

    for c in range(NOUT):
        for i in range(views):
            @pl.when(g * views + i != me)
            def _(i=i, c=c):
                out_copy(c, 0, g, i).wait_recv()

    for c in range(NOUT):
        for w in range(views):
            @pl.when((w != v) | (band != g))
            def _(w=w, c=c):
                out_copy(c, w, band, idx).wait_send()


def store_kernel(est_in, joined_in, est_out, joined_out, sems):
    copies = [pltpu.make_async_copy(a, b, sems.at[n]) for n, (a, b) in enumerate(((est_in, est_out), (joined_in, joined_out)))]
    for copy in copies:
        copy.start()
    for copy in copies:
        copy.wait()


def on_device(dims, camera, background, destination, offsets, shift_frac, psf_taps):
    slabs, views, bands = dims
    blocks, planes, rows, cols = camera.shape[1:]
    taps = psf_taps.shape[-1]
    margin = taps // 2
    tall = CZ * rows + CZ
    strip = rows // views
    wide = strip + 2 * HALO
    tap_rows = -(-3 * taps // 8) * 8
    vmem = pl.BlockSpec(memory_space=pltpu.VMEM)
    hbm = functools.partial(pltpu.with_memory_space_constraint, memory_space=pltpu.HBM)
    cell = 4 * cols
    room = 2 * 1024 * 1024
    any_hbm = pl.BlockSpec(memory_space=pltpu.HBM)
    frac, psf = hbm(shift_frac[0]), hbm(jnp.transpose(psf_taps, (1, 0, 2)))
    acc = pl.pallas_call(
        functools.partial(deposit_kernel, rows),
        in_specs=[any_hbm] * 5,
        out_specs=vmem,
        out_shape=pltpu.VMEM((slabs, tall, cols), jnp.float32),
        scratch_shapes=[
            pltpu.SMEM((blocks,), jnp.int32),
            pltpu.SMEM((blocks,), jnp.int32),
            pltpu.SMEM((1, 1, 1), jnp.int32),
            pltpu.SMEM((3,), jnp.float32),
            pltpu.SMEM((slabs * CZ,), jnp.int32),
            pltpu.VMEM((blocks, planes, rows, cols), jnp.float32),
            pltpu.SemaphoreType.DMA((blocks // CHUNK,)),
            pltpu.SemaphoreType.DMA((4,)),
        ],
        compiler_params=pltpu.CompilerParams(
            vmem_limit_bytes=cell * (blocks * planes * rows + slabs * tall) + room),
        name="deposit",
    )(hbm(destination.reshape(-1)), hbm(offsets.reshape(-1)), background, frac, hbm(camera[0]))

    dma = pltpu.SemaphoreType.DMA
    f32 = jnp.float32
    shapes = [
        (slabs, tall, cols), (slabs, tall, cols), (views, tap_rows, cols),
        (views, 3 * CZ, wide, cols), (3 * CZ, wide, cols), (3 * CZ, wide, cols),
    ]
    late = [
        (views, 3 * CZ, strip + 2 * margin, cols), (views, CZ + 2 * margin, strip + 2 * margin, cols),
        (views, MOST, strip + 2 * margin, cols),
        (views, MOST, strip + 2 * margin, cols), (views, MOST, strip, cols), (CZ, strip, cols),
    ]
    total = sum([functools.reduce(lambda a, b: a * b, s) for s in shapes + late])
    total = total + cols * (slabs * tall + 2 * CZ * rows + views * 4 * cols)
    estimate, joined = pl.pallas_call(
        functools.partial(world_kernel, dims, rows, taps),
        in_specs=[vmem, any_hbm, any_hbm],
        out_specs=(vmem, vmem),
        out_shape=(
            pltpu.VMEM((CZ, rows, cols), f32),
            pltpu.VMEM((1, CZ, rows, cols), f32),
        ),
        scratch_shapes=[pltpu.SMEM((3,), f32), pltpu.VMEM((3, 1, taps), f32), pltpu.VMEM((tap_rows, cols), f32)]
        + [pltpu.VMEM(s, f32) for s in shapes]
        + [pltpu.VMEM((views, 2, 2 * cols, 2 * cols), jnp.bfloat16)]
        + [pltpu.VMEM(s, f32) for s in late]
        + [
            dma((2,)), dma((slabs, NCH)), dma((slabs, NCH)), dma((slabs, NCH)), dma((slabs, NCH)),
            dma((views,)), dma((views,)), dma,
            dma((views, NCH)), dma((views, NCH)), dma((NCH,)), dma((views, NCH)), dma((NCH,)), dma((views, NCH)),
            dma((2, views, NCH)), dma((2, views, NCH)), dma((8, NOUT)), dma((8, NOUT)),
            dma((views, NOUT)), dma((views, NOUT)),
        ],
        compiler_params=pltpu.CompilerParams(
            collective_id=0, has_side_effects=True, vmem_limit_bytes=4 * total + room),
        name="world",
    )(acc, frac, psf)
    return pl.pallas_call(
        store_kernel,
        in_specs=[vmem, vmem],
        out_specs=(pl.BlockSpec(memory_space=pltpu.HBM), pl.BlockSpec(memory_space=pltpu.HBM)),
        out_shape=(jax.ShapeDtypeStruct(estimate.shape, f32), jax.ShapeDtypeStruct(joined.shape, f32)),
        scratch_shapes=[dma((2,))],
        name="store",
    )(pltpu.with_memory_space_constraint(estimate, pltpu.VMEM), pltpu.with_memory_space_constraint(joined, pltpu.VMEM))


def solution(mesh):
    dims = (mesh.shape["gz"], mesh.shape["view"], mesh.shape["gy"])
    return jax.shard_map(
        functools.partial(on_device, dims),
        mesh=mesh,
        in_specs=(
            P("view", ("groups", "gz"), None, "gy", None),
            P("view", "gy", ("groups", "gz")),
            P("view", "gy", ("groups", "gz"), None),
            P("view", "gy", ("groups", "gz")),
            P("view", None),
            P("view", None, None),
        ),
        out_specs=(P(("groups", "gz"), "gy", None), P("view", ("groups", "gz"), "gy", None)),
        check_vma=False,
    )
```
